128 devices in a mesh: tm: 64 (over x_hi, z, y, core), row: 2 (over x_lo).
Axes of the slice: x: 4 (x_hi: 2, x_lo: 2; x = x_hi * 2 + x_lo), y: 4, z: 4, core: 2. Of those that a mesh axis runs over, the one named last changes fastest.
Arguments:
- wavefront: float32 [512, 2, 256, 256], P('tm', None, 'row'), may hold values from -6 to 6
- particle_phase: float32 [512, 4096], P('tm', 'row'), may hold values from -3.140625 to 3.140625
- particle_energy: float32 [512, 4096], P('tm', 'row'), may hold values from -6 to 6
- row_offset: float32 [512, 4096], P('tm', 'row'), may hold values from -0.5 to 0.5
- row_cell: int32 [512, 4096], P('tm', 'row'), may hold values from 0 to 255, as said below
- col_cell: int32 [512, 4096], P('tm', 'row'), may hold values from 0 to 255
Outputs:
- wavefront_out: float32 [512, 2, 256, 256], P('tm', None, 'row')
- phase_out: float32 [512, 4096], P('tm', 'row')
- energy_out: float32 [512, 4096], P('tm', 'row')
The draws below stay inside these ranges and needn't reach their ends.
Inputs may be any that keep to these rules, and one draw needn't show every extreme that they name: `row_cell`: the particle at position p of a slice lies in rows 128 * (p // 2048) to 128 * (p // 2048) + 127.
All inputs are finite; a program needn't handle non-finite values.
Results may differ from the reference program's by a relative error of at most 0.0003.
Values sent between devices are 32-bit elements; how exact they have to be, the bound alone decides.
No kernel may reach another device: no remote copies, remote signals or barrier semaphores. Data moves between devices by JAX's collectives and lax.ppermute only.
A program may use at most 64 MiB of HBM per device.

```python
import math
import jax
import jax.numpy as jnp
from jax import lax

NR = 256
NC = 256
P_SIZE = 4096
STEPS = 2
SLICES = 512
ROWS_DEV = 128
PART_DEV = 2048


def draw_row_cell(key, part):
    position = jnp.arange(P_SIZE, dtype=jnp.int32)[None, :]
    inside = jax.random.randint(key, (SLICES, P_SIZE), 0, ROWS_DEV, dtype=jnp.int32)
    within = position % PART_DEV
    inside = jnp.where(within == 0, 0, jnp.where(within == 1, ROWS_DEV - 1, inside))
    return position // PART_DEV * ROWS_DEV + inside


def plant(array, stream_key, low, top_value):
    shape = array.shape
    place = [jax.random.randint(jax.random.fold_in(stream_key, axis), (), 0, shape[axis]) for axis in range(len(shape))]
    array = array.at[tuple(place)].set(low)
    longest = shape.index(max(shape))
    place[longest] = (place[longest] + 1) % shape[longest]
    return array.at[tuple(place)].set(top_value)


def block_scale(stream_key, shape, pieces, least, top_value):
    def one(dim, blocks):
        draws = jax.random.uniform(jax.random.fold_in(jax.random.fold_in(stream_key, 6), dim), (blocks,), jnp.float32, least / len(pieces), top_value / len(pieces))
        return jnp.repeat(jnp.exp(draws), shape[dim] // blocks).reshape((-1,) + (1,) * (len(shape) - dim - 1))

    gain = one(*pieces[0])
    for cut in pieces[1:]:
        gain = gain * one(*cut)
    return gain


def scatter_about(own_key, shape, deviation, limit, cuts=(), held_as=jnp.bfloat16):
    array = jax.random.normal(own_key, shape, jnp.float32) * deviation
    if len(cuts) > 0:
        array = block_scale(own_key, shape, cuts, -0.22, 0.18) * array
    return jnp.clip(array, min=-limit, max=limit).astype(held_as)


def setup_inputs(seed: int = 0) -> dict:
    splits = jax.random.split(jax.random.key(seed), 7)
    return {
        "wavefront": scatter_about(splits[0], (SLICES, 2, NR, NC), 1.0, 6.0, ((0, 64), (2, 2)), jnp.float32),
        "particle_phase": jnp.clip(jax.random.uniform(splits[1], (SLICES, P_SIZE), jnp.float32, -3.140625, 3.140625), -3.140625, 3.140625),
        "particle_energy": scatter_about(splits[2], (SLICES, P_SIZE), 1.0, 6.0, ((0, 64), (1, 2)), jnp.float32),
        "row_offset": jnp.clip(jax.random.uniform(splits[3], (SLICES, P_SIZE), jnp.float32, -0.5, 0.5) * block_scale(splits[3], (SLICES, P_SIZE), ((0, 64), (1, 2)), -0.4, 0.0), -0.5, 0.5),
        "row_cell": draw_row_cell(jax.random.fold_in(splits[6], 71), 0),
        "col_cell": plant(jax.random.randint(splits[5], (SLICES, P_SIZE), 0, NC), jax.random.fold_in(splits[5], 1), 0, NC - 1).astype(jnp.int32),
    }


PUSH_GAIN = 0.5
PHASE_ADVANCE = 1.0
SOURCE_GAIN = 1.0


def phase_ramp(length):
    number = jnp.arange(length, dtype=jnp.int32)
    signed = jnp.where(number < length // 2, number, number - length).astype(jnp.float32)
    return (math.pi / length) * signed * signed


def interact(wavefront, padded, halo_rows, own_rows, col_cell, particle_phase, particle_energy, row_offset):
    slice_count = padded.shape[0]
    col_total = padded.shape[3]
    flattened = padded.reshape(slice_count, 2, padded.shape[2] * col_total)

    def sample_at(row_shift):
        target = (halo_rows + row_shift) * col_total + col_cell
        return (jnp.take_along_axis(flattened[:, 0], target, axis=1),
                jnp.take_along_axis(flattened[:, 1], target, axis=1))

    low_real, low_imag = sample_at(-1)
    mid_real, mid_imag = sample_at(0)
    high_real, high_imag = sample_at(1)
    lower_gap = 0.5 - row_offset
    upper_gap = 0.5 + row_offset
    weight_low = 0.5 * lower_gap * lower_gap
    weight_mid = 0.75 - row_offset * row_offset
    weight_high = 0.5 * upper_gap * upper_gap
    sampled_real = weight_low * low_real + weight_mid * mid_real + weight_high * high_real
    sampled_imag = weight_low * low_imag + weight_mid * mid_imag + weight_high * high_imag
    driving = sampled_real * jnp.cos(particle_phase) - sampled_imag * jnp.sin(particle_phase)
    particle_energy = particle_energy - PUSH_GAIN * driving
    particle_phase = particle_phase + PHASE_ADVANCE * particle_energy
    rows_own = wavefront.shape[2]
    target = own_rows * col_total + col_cell
    slice_index = jnp.arange(slice_count, dtype=jnp.int32)[:, None]
    deposit = jnp.zeros((slice_count, 2, rows_own * col_total), jnp.float32)
    deposit = deposit.at[slice_index, 0, target].add(SOURCE_GAIN * jnp.cos(particle_phase))
    deposit = deposit.at[slice_index, 1, target].add(-SOURCE_GAIN * jnp.sin(particle_phase))
    return wavefront + deposit.reshape(wavefront.shape), particle_phase, particle_energy


def reference(wavefront, particle_phase, particle_energy, row_offset, row_cell, col_cell):
    total_phase = phase_ramp(NR)[:, None] + phase_ramp(NC)[None, :]
    factor = lax.complex(jnp.cos(total_phase), -jnp.sin(total_phase))
    for period in range(STEPS):
        wavefront = jnp.concatenate([jnp.zeros_like(wavefront[:1]), wavefront[:-1]], 0)
        padded = jnp.pad(wavefront, ((0, 0), (0, 0), (1, 1), (0, 0)))
        wavefront, particle_phase, particle_energy = interact(
            wavefront, padded, row_cell + 1, row_cell, col_cell,
            particle_phase, particle_energy, row_offset)
        complex_wave = lax.complex(wavefront[:, 0], wavefront[:, 1])
        complex_wave = jnp.fft.ifft2(jnp.fft.fft2(complex_wave) * factor)
        wavefront = jnp.stack([jnp.real(complex_wave), jnp.imag(complex_wave)], 1)
    return wavefront, particle_phase, particle_energy
```

```python
import math
import numpy as np
import ml_dtypes
import jax, jax.numpy as jnp
from jax import lax
from jax.experimental import pallas as pl
from jax.experimental.pallas import tpu as pltpu

BF = jnp.bfloat16
F32 = jnp.float32
N = 256
WIN = 144

def split_np(m):
    hi = m.astype(ml_dtypes.bfloat16)
    lo = (m - hi.astype(np.float64)).astype(ml_dtypes.bfloat16)
    return hi, lo

def tables():
    k = np.arange(N)
    m = np.where(k < N // 2, k, k - N).astype(np.float64)
    h = np.exp(-1j * np.pi / N * m * m)
    dft = np.exp(-2j * np.pi / N * (k[:, None] * k[None, :] % N))
    a = (np.conj(dft) / N) @ (h[:, None] * dft)
    ar, ai = a.real, a.imag
    right = np.block([[ar, ai], [-ai, ar]])
    left = np.block([[ar, -ai], [ai, ar]])
    rh, rl = split_np(right)
    lh, ll = split_np(left)
    return np.concatenate([rh, rh, rl], 0), np.concatenate([lh, lh, ll], 1)

def sincos(x):
    n = jnp.round(x * (1.0 / math.pi))
    r = x - n * 3.140625
    r = r - n * 9.670257568359375e-4
    r = r - n * 6.277114152908325e-07
    half = n * 0.5
    odd = half - jnp.floor(half)
    sign = 1.0 - 4.0 * odd
    y = r * r
    s = -2.3889859e-08
    s = s * y + 2.7525562e-06
    s = s * y - 1.98408740e-04
    s = s * y + 8.33333310e-03
    s = s * y - 1.66666667e-01
    s = r + r * y * s
    c = 2.08767570e-09 - 1.1470746e-11 * y
    c = c * y - 2.75573192e-07
    c = c * y + 2.48015873e-05
    c = c * y - 1.38888889e-03
    c = c * y + 4.16666667e-02
    c = c * y - 0.5
    c = c * y + 1.0
    return s * sign, c * sign

def hilo(x):
    hi = x.astype(BF)
    lo = (x - hi.astype(F32)).astype(BF)
    return hi, lo

def body(f_ref, ph_ref, en_ref, off_ref, row_ref, col_ref, r_ref, l_ref,
         fo_ref, pho_ref, eno_ref,
         c_ref, samp_ref, w_ref, s_ref, sr_ref, x_ref):
    off = off_ref[0]
    lg = 0.5 - off
    ug = 0.5 + off
    w_ref[0] = 0.5 * lg * lg
    w_ref[1] = 0.75 - off * off
    w_ref[2] = 0.5 * ug * ug
    iota_c = lax.broadcasted_iota(jnp.int32, (16, 16, 128), 0) * 16 + lax.broadcasted_iota(jnp.int32, (16, 16, 128), 1)
    iota_c = iota_c.astype(F32).astype(BF)
    one = jnp.ones((16, 128), BF)
    zero = jnp.zeros((16, 128), BF)
    iota_r = lax.broadcasted_iota(jnp.int32, (WIN, 128), 0).astype(F32)
    for h in range(2):
        win0 = 0 if h == 0 else N - WIN
        fw = f_ref[0, :, win0:win0 + WIN, :].reshape(2 * WIN, N)
        hi, lo = hilo(fw)
        for k in range(16):
            j = 16 * h + k
            c = jnp.broadcast_to(col_ref[0, j:j + 1, :], (16, 128)).astype(BF)
            c_ref[h, :, 128 * k:128 * k + 128] = jnp.where(iota_c == c[None], one[None], zero[None]).reshape(N, 128)
        for k2 in range(8):
            cc = c_ref[h, :, 256 * k2:256 * k2 + 256]
            g2 = jnp.dot(hi, cc, preferred_element_type=F32) + jnp.dot(lo, cc, preferred_element_type=F32)
            for kk in range(2):
                j = 16 * h + 2 * k2 + kk
                g = g2[:, 128 * kk:128 * kk + 128]
                rr = row_ref[0, j:j + 1, :] - float(win0)
                w = jnp.where(iota_r == rr, w_ref[1, j:j + 1, :],
                    jnp.where(iota_r == rr - 1.0, w_ref[0, j:j + 1, :],
                    jnp.where(iota_r == rr + 1.0, w_ref[2, j:j + 1, :], 0.0)))
                samp_ref[0, j:j + 1, :] = jnp.sum(w * g[:WIN], 0, keepdims=True)
                samp_ref[1, j:j + 1, :] = jnp.sum(w * g[WIN:], 0, keepdims=True)
    ph = ph_ref[0]
    s0, c0 = sincos(ph)
    en = en_ref[0] - 0.5 * (samp_ref[0] * c0 - samp_ref[1] * s0)
    ph = ph + en
    pho_ref[0] = ph
    eno_ref[0] = en
    s1, c1 = sincos(ph)
    s1 = -s1
    for z, v in ((0, c1), (1, s1)):
        vh = v.astype(BF).astype(F32)
        s_ref[2 * z] = vh
        s_ref[2 * z + 1] = v - vh
    iota_d = iota_c[:8]
    for h in range(2):
        for k in range(16):
            j = 16 * h + k
            rr = jnp.broadcast_to(row_ref[0, j:j + 1, :] - float(128 * h), (16, 128)).astype(BF)
            m = iota_d == rr[None]
            for q in range(4):
                sv = jnp.broadcast_to(s_ref[q, j:j + 1, :], (16, 128)).astype(BF)
                sr_ref[128 * q:128 * q + 128, 128 * k:128 * k + 128] = jnp.where(m, sv[None], zero[None]).reshape(128, 128)
        d = lax.dot_general(sr_ref[...], c_ref[h], (((1,), (1,)), ((), ())), preferred_element_type=F32)
        for z in range(2):
            x_ref[128 * h:128 * h + 128, N * z:N * z + N] = (
                f_ref[0, z, 128 * h:128 * h + 128, :] + d[256 * z:256 * z + 128] + d[256 * z + 128:256 * z + 256])
    xh, xl = hilo(x_ref[...])
    y = jnp.dot(jnp.concatenate([xh, xl, xh], 1), r_ref[...], preferred_element_type=F32)
    y2 = jnp.concatenate([y[:, :N], y[:, N:]], 0)
    yh, yl = hilo(y2)
    z = jnp.dot(l_ref[...], jnp.concatenate([yh, yl, yh], 0), preferred_element_type=F32)
    fo_ref[0] = z.reshape(2, N, N)

def slots(field, ph, en, off, row, col, right, left):
    n = field.shape[0]
    fs = pl.BlockSpec((1, 2, N, N), lambda i: (i, 0, 0, 0))
    ps = pl.BlockSpec((1, 32, 128), lambda i: (i, 0, 0))
    full = lambda a: pl.BlockSpec(a.shape, lambda i: (0,) * a.ndim)
    return pl.pallas_call(
        body, grid=(n,),
        in_specs=[fs, ps, ps, ps, ps, ps, full(right), full(left)],
        out_specs=[fs, ps, ps],
        out_shape=[jax.ShapeDtypeStruct(field.shape, F32), jax.ShapeDtypeStruct(ph.shape, F32), jax.ShapeDtypeStruct(ph.shape, F32)],
        scratch_shapes=[pltpu.VMEM((2, N, 2048), BF), pltpu.VMEM((2, 32, 128), F32), pltpu.VMEM((3, 32, 128), F32),
                        pltpu.VMEM((4, 32, 128), F32), pltpu.VMEM((512, 2048), BF), pltpu.VMEM((N, 512), F32)],
        compiler_params=pltpu.CompilerParams(vmem_limit_bytes=48 << 20),
    )(field, ph, en, off, row, col, right, left)


def other_half(value, start, count):
    return lax.dynamic_slice_in_dim(value, start, count, 0)


def run(field, zero_slot, particles, right, left):
    phase, energy, offset, row, col = particles
    device = lax.axis_index(("tm", "row"))
    scale = jnp.where((jnp.arange(4) == zero_slot) & (device == 0), 0.0, 1.0).astype(F32)
    field = field * scale[:, None, None, None]
    return slots(field, phase, energy, offset, row, col, right, left)


def body_all(wavefront, particle_phase, particle_energy, row_offset, row_cell, col_cell):
    right, left = (jnp.asarray(a) for a in tables())
    r = lax.axis_index("row")
    first = r == 0
    nt = lax.axis_size("tm")
    both = ("tm", "row")
    swap = [(2 * t + s, 2 * t + 1 - s) for t in range(nt) for s in range(2)]
    chain = [(i, (i + 1) % (2 * nt)) for i in range(2 * nt)]
    ahead = [(2 * t, (2 * t + 2) % (2 * nt)) for t in range(nt)]
    back = [(j, i) for i, j in chain]

    parts = jnp.stack([particle_phase, particle_energy, row_offset,
                       row_cell.astype(F32), col_cell.astype(F32)], 1).reshape(8, 5, 16, 128)
    p_swap = lax.ppermute(other_half(parts, 4 - 4 * r, 4), both, swap)
    p_chain = lax.ppermute(other_half(parts, 3 + 4 * r, 1), both, chain)
    p_ahead = lax.ppermute(parts[7:8], both, ahead)
    f_chain = lax.ppermute(other_half(wavefront, 2 + 4 * r, 2), both, chain)
    f_ahead = lax.ppermute(wavefront[6:8], both, ahead)
    f_swap = lax.ppermute(other_half(wavefront, 4 - 4 * r, 2), both, swap)

    def joined(own, other, axis):
        return jnp.concatenate([jnp.where(first, own, other), jnp.where(first, other, own)], axis)

    p_own = jnp.where(first, jnp.concatenate([p_ahead, parts[:4]], 0), parts[3:])
    p_all = joined(p_own, jnp.concatenate([p_chain, p_swap], 0), 2)
    f_own = jnp.where(first, jnp.concatenate([f_ahead, wavefront[:2]], 0), wavefront[2:6])
    field = joined(f_own, jnp.concatenate([f_chain, f_swap], 0), 2)
    p_first = [p_all[:4, i] for i in range(5)]
    field, phase, energy = run(field, 1, p_first, right, left)
    pushed = jnp.stack([phase, energy], 1)
    p_last = lax.ppermute(pushed[:1], both, back)
    pushed = jnp.concatenate([pushed[1:], p_last], 0)
    field, phase, energy = run(field, 0, [pushed[:, 0], pushed[:, 1]] + [p_all[1:, i] for i in range(2, 5)], right, left)

    def home(value, axis):
        count = value.shape[axis] // 2
        own = lax.dynamic_slice_in_dim(value, r * count, count, axis)
        away = lax.dynamic_slice_in_dim(value, (1 - r) * count, count, axis)
        return joined(own, lax.ppermute(away, both, swap), 0)

    field = home(field, 2)
    pushed = home(jnp.stack([phase, energy], 1), 2)
    return field, pushed[:, 0].reshape(8, 2048), pushed[:, 1].reshape(8, 2048)


def solution(mesh):
    P = jax.sharding.PartitionSpec
    wide, flat = P("tm", None, "row", None), P("tm", "row")
    return jax.shard_map(body_all, mesh=mesh, in_specs=(wide,) + (flat,) * 5,
                         out_specs=(wide, flat, flat), check_vma=False)
```

```python
import math

import jax
import jax.numpy as jnp
import ml_dtypes
import numpy as np
from jax import lax
from jax.experimental import pallas as pl
from jax.experimental.pallas import tpu as pltpu

BF = jnp.bfloat16
F32 = jnp.float32
N = 256
HALF = 128
PART = 2048
ROWS = PART // N
WIN = 144
FIELDS = 5 * ROWS
PUSHED = 2 * ROWS
PIECE = 2 * HALF + PUSHED


def split_np(m):
    hi = m.astype(ml_dtypes.bfloat16)
    return hi, (m - hi.astype(np.float64)).astype(ml_dtypes.bfloat16)


def tables():
    k = np.arange(N)
    m = np.where(k < N // 2, k, k - N).astype(np.float64)
    h = np.exp(-1j * np.pi / N * m * m)
    dft = np.exp(-2j * np.pi / N * (k[:, None] * k[None, :] % N))
    a = (np.conj(dft) / N) @ (h[:, None] * dft)
    right = np.block([[a.real, a.imag], [-a.imag, a.real]])
    left = np.block([[a.real, -a.imag], [a.imag, a.real]])
    return np.stack(split_np(right)), np.stack(split_np(left))


def sincos(x):
    n = jnp.round(x * (1.0 / math.pi))
    r = x - n * 3.140625
    r = r - n * 9.670257568359375e-4
    r = r - n * 6.277114152908325e-07
    half = n * 0.5
    sign = 1.0 - 4.0 * (half - jnp.floor(half))
    y = r * r
    s = -2.3889859e-08
    for c in (2.7525562e-06, -1.98408740e-04, 8.33333310e-03, -1.66666667e-01):
        s = s * y + c
    s = r + r * y * s
    c = 2.08767570e-09 - 1.1470746e-11 * y
    for d in (-2.75573192e-07, 2.48015873e-05, -1.38888889e-03, 4.16666667e-02, -0.5, 1.0):
        c = c * y + d
    return s * sign, c * sign


def hilo(x):
    hi = x.astype(BF)
    return hi, (x - hi.astype(F32)).astype(BF)


def mm(a, b):
    return jnp.dot(a, b, preferred_element_type=F32)


def step(f_ref, p_ref, tab_r, tab_l, out_ref, c_ref, w_ref, s_ref, sr_ref, x_ref, samp_ref):
    iota_c = (lax.broadcasted_iota(jnp.int32, (16, 16, N), 0) * 16
              + lax.broadcasted_iota(jnp.int32, (16, 16, N), 1)).astype(F32).astype(BF)
    one = jnp.ones((16, N), BF)
    zero = jnp.zeros((16, N), BF)
    iota_r = lax.broadcasted_iota(jnp.int32, (WIN, N), 0).astype(F32)
    for h in range(2):
        off = p_ref[h, 2 * ROWS:3 * ROWS]
        lower = 0.5 - off
        upper = 0.5 + off
        w_ref[0] = 0.5 * lower * lower
        w_ref[1] = 0.75 - off * off
        w_ref[2] = 0.5 * upper * upper
        win0 = 0 if h == 0 else N - WIN
        hi, lo = hilo(f_ref[:, win0:win0 + WIN, :].reshape(2 * WIN, N))
        for k in range(ROWS):
            col = jnp.broadcast_to(p_ref[h, 4 * ROWS + k:4 * ROWS + k + 1, :], (16, N)).astype(BF)
            hot = jnp.where(iota_c == col[None], one[None], zero[None]).reshape(N, N)
            c_ref[h, :, N * k:N * k + N] = hot
            g = mm(hi, hot) + mm(lo, hot)
            at = p_ref[h, 3 * ROWS + k:3 * ROWS + k + 1, :] - float(win0)
            w = jnp.where(iota_r == at, w_ref[1, k:k + 1, :],
                          jnp.where(iota_r == at - 1.0, w_ref[0, k:k + 1, :],
                                    jnp.where(iota_r == at + 1.0, w_ref[2, k:k + 1, :], 0.0)))
            samp_ref[0, k:k + 1, :] = jnp.sum(w * g[:WIN], 0, keepdims=True)
            samp_ref[1, k:k + 1, :] = jnp.sum(w * g[WIN:], 0, keepdims=True)
        phase = p_ref[h, :ROWS]
        sine, cosine = sincos(phase)
        energy = p_ref[h, ROWS:2 * ROWS] - 0.5 * (samp_ref[0] * cosine - samp_ref[1] * sine)
        phase = phase + energy
        p_ref[h, :ROWS] = phase
        p_ref[h, ROWS:2 * ROWS] = energy
        sine, cosine = sincos(phase)
        for z, v in ((0, cosine), (1, -sine)):
            vh = v.astype(BF).astype(F32)
            s_ref[2 * z] = vh
            s_ref[2 * z + 1] = v - vh
        for k in range(ROWS):
            at = jnp.broadcast_to(p_ref[h, 3 * ROWS + k:3 * ROWS + k + 1, :] - float(HALF * h), (16, N)).astype(BF)
            here = iota_c[:8] == at[None]
            for q in range(4):
                value = jnp.broadcast_to(s_ref[q, k:k + 1, :], (16, N)).astype(BF)
                sr_ref[HALF * q:HALF * q + HALF, N * k:N * k + N] = jnp.where(here, value[None], zero[None]).reshape(HALF, N)
        d = lax.dot_general(sr_ref[...], c_ref[h], (((1,), (1,)), ((), ())), preferred_element_type=F32)
        for z in range(2):
            x_ref[HALF * h:HALF * h + HALF, N * z:N * z + N] = (
                f_ref[z, HALF * h:HALF * h + HALF, :]
                + d[2 * HALF * z:2 * HALF * z + HALF] + d[2 * HALF * z + HALF:2 * HALF * z + 2 * HALF])
    xh, xl = hilo(x_ref[...])
    y = mm(xh, tab_r[0]) + mm(xl, tab_r[0]) + mm(xh, tab_r[1])
    yh, yl = hilo(jnp.concatenate([y[:, :N], y[:, N:]], 0))
    out = mm(tab_l[0], yh) + mm(tab_l[0], yl) + mm(tab_l[1], yh)
    out_ref[...] = out.reshape(2, N, N)


WORK = [pltpu.VMEM((2, N, PART), BF), pltpu.VMEM((3, ROWS, N), F32), pltpu.VMEM((4, ROWS, N), F32),
        pltpu.VMEM((4 * HALF, PART), BF), pltpu.VMEM((N, 2 * N), F32), pltpu.VMEM((2, ROWS, N), F32)]
FIELD = pltpu.VMEM((2, N, N), F32)
PARTS = pltpu.VMEM((2, FIELDS, N), F32)
ANY = pl.BlockSpec(memory_space=pl.ANY)
VM = pl.BlockSpec(memory_space=pltpu.VMEM)
SM = pl.BlockSpec(memory_space=pltpu.SMEM)


class Copies:
    def __init__(self, sems):
        self.sems = sems
        self.used = 0
        self.open = []

    def start(self, src, dst):
        copy = pltpu.make_async_copy(src, dst, self.sems.at[self.used])
        self.used += 1
        copy.start()
        self.open.append(copy)

    def wait(self):
        for copy in self.open:
            copy.wait()
        self.open = []


def call(kernel, outs, out_specs, scratch, copies, in_specs, flops):
    return pl.pallas_call(
        kernel, out_shape=[jax.ShapeDtypeStruct(s, F32) for s in outs], in_specs=in_specs, out_specs=out_specs,
        scratch_shapes=scratch + [pltpu.SemaphoreType.DMA((copies,))],
        cost_estimate=pl.CostEstimate(flops=flops, bytes_accessed=4 << 20, transcendentals=0),
        compiler_params=pltpu.CompilerParams(vmem_limit_bytes=40 << 20))


def pack_kernel(meta, wave, *refs):
    sources, (all_ref, swap_ref, chain_ref, ahead_ref), (packed, sems) = refs[:5], refs[5:9], refs[9:]
    r = meta[0]
    rows = 2 * N
    copies = Copies(sems)
    copies.start(wave.at[pl.ds(N * (4 - 4 * r), rows)], swap_ref.at[pl.ds(0, rows)])
    copies.start(wave.at[pl.ds(N * (2 + 4 * r), rows)], chain_ref.at[pl.ds(0, rows)])
    copies.start(wave.at[pl.ds(N * (6 - 4 * r), rows)], ahead_ref.at[pl.ds(0, rows)])
    for a, src in enumerate(sources):
        for s in range(8):
            for k in range(ROWS):
                packed[s, a * ROWS + k:a * ROWS + k + 1, :] = src[s:s + 1, N * k:N * k + N].astype(F32)
    copies.start(packed, all_ref)
    for i in range(4):
        copies.start(packed.at[4 - 4 * r + i], swap_ref.at[pl.ds(rows + FIELDS * i, FIELDS)])
    copies.start(packed.at[3 + 4 * r], chain_ref.at[pl.ds(rows, FIELDS)])
    copies.start(packed.at[7 - 4 * r], ahead_ref.at[pl.ds(rows, FIELDS)])
    copies.wait()


def field_in(copies, r, f_ref, own, own_row, other, other_row):
    for z in range(2):
        copies.start(own.at[pl.ds(own_row + HALF * z, HALF)], f_ref.at[z, pl.ds(pl.multiple_of(HALF * r, HALF), HALF)])
        copies.start(other.at[pl.ds(other_row + HALF * z, HALF)],
                     f_ref.at[z, pl.ds(pl.multiple_of(HALF - HALF * r, HALF), HALF)])


def piece_out(copies, r, z_ref, p_ref, own, away, i):
    for half, dst in ((r, own), (1 - r, away)):
        for z in range(2):
            copies.start(z_ref.at[z, pl.ds(pl.multiple_of(HALF * half, HALF), HALF)], dst.at[i, pl.ds(HALF * z, HALF)])
        copies.start(p_ref.at[half, pl.ds(0, PUSHED)], dst.at[i, pl.ds(2 * HALF, PUSHED)])


def first_kernel(meta, wave, parts, swap, tab_r, tab_l, d_ref, q_ref, own, away, f2, f3, p1, p2, z, *rest):
    work, sems = rest[:-1], rest[-1]
    r = meta[0]
    copies = Copies(sems)
    field_in(copies, r, f2, wave, N * 4 * r, swap, 0)
    field_in(copies, r, f3, wave, N * (4 * r + 1), swap, N)
    for p, i in ((p1, 1), (p2, 2)):
        copies.start(parts.at[4 * r + i], p.at[r])
        copies.start(swap.at[pl.ds(2 * N + FIELDS * i, FIELDS)], p.at[1 - r])
    copies.wait()
    step(f3, p2, tab_r, tab_l, d_ref, *work)
    step(f2, p1, tab_r, tab_l, f3, *work)
    copies.start(p1, q_ref)
    step(f3, p2, tab_r, tab_l, z, *work)
    piece_out(copies, r, z, p2, own, away, 0)
    copies.wait()


def second_kernel(meta, parts, swap, chain, ahead, tab_r, tab_l, d_ref, q_ref, pushed, f0, f1, p0, pm, *rest):
    work, sems = rest[:-1], rest[-1]
    r = meta[0]
    copies = Copies(sems)
    field_in(copies, r, f0, ahead, 0, chain, 0)
    field_in(copies, r, f1, ahead, N, chain, N)
    copies.start(ahead.at[pl.ds(2 * N, FIELDS)], pm.at[r])
    copies.start(chain.at[pl.ds(2 * N, FIELDS)], pm.at[1 - r])
    copies.start(parts.at[4 * r], p0.at[r])
    copies.start(swap.at[pl.ds(2 * N, FIELDS)], p0.at[1 - r])
    copies.wait()

    @pl.when(meta[1] == 1)
    def _():
        f1[...] = jnp.zeros_like(f1)

    step(f0, pm, tab_r, tab_l, d_ref.at[0], *work)
    copies.start(pm.at[:, pl.ds(0, PUSHED)], pushed)
    step(f1, p0, tab_r, tab_l, d_ref.at[1], *work)
    copies.start(p0, q_ref)
    copies.wait()


def third_kernel(meta, d_ref, q0, q1, tab_r, tab_l, own, away, f0, p0, p1, z0, z1, *rest):
    work, sems = rest[:-1], rest[-1]
    r = meta[0]
    copies = Copies(sems)
    copies.start(d_ref.at[0], f0)
    copies.start(q0, p0)
    copies.start(q1, p1)
    copies.wait()

    @pl.when(meta[1] == 1)
    def _():
        f0[...] = jnp.zeros_like(f0)

    step(f0, p0, tab_r, tab_l, z0, *work)
    piece_out(copies, r, z0, p0, own, away, 0)
    step(d_ref.at[1], p1, tab_r, tab_l, z1, *work)
    piece_out(copies, r, z1, p1, own, away, 1)
    copies.wait()


def fourth_kernel(meta, d_ref, parts, swap, pushed, tab_r, tab_l, own, away, p3, z, *rest):
    work, sems = rest[:-1], rest[-1]
    r = meta[0]
    copies = Copies(sems)
    copies.start(parts.at[4 * r + 3], p3.at[r])
    copies.start(swap.at[pl.ds(2 * N + FIELDS * 3, FIELDS)], p3.at[1 - r])
    copies.wait()
    copies.start(pushed, p3.at[:, pl.ds(0, PUSHED)])
    copies.wait()
    step(d_ref, p3, tab_r, tab_l, z, *work)
    piece_out(copies, r, z, p3, own, away, 0)
    copies.wait()


def final_kernel(meta, *refs):
    pieces, (wave, phase, energy), (packed, sems) = refs[:6], refs[6:9], refs[9:]
    r = meta[0]
    copies = Copies(sems)
    for half in range(2):
        base = 4 * r if half == 0 else 4 - 4 * r
        for ref, slots in zip(pieces[3 * half:3 * half + 3], ((2,), (0, 1), (3,))):
            for i, slot in enumerate(slots):
                copies.start(ref.at[i, pl.ds(0, N)], wave.at[pl.ds((base + slot) * N, N)])
                copies.start(ref.at[i, pl.ds(N, PUSHED)], packed.at[base + slot])
    copies.wait()
    for s in range(8):
        for k in range(ROWS):
            phase[s:s + 1, N * k:N * k + N] = packed[s, k:k + 1, :]
            energy[s:s + 1, N * k:N * k + N] = packed[s, ROWS + k:ROWS + k + 1, :]


def body(wavefront, particle_phase, particle_energy, row_offset, row_cell, col_cell):
    tab_r, tab_l = (jnp.asarray(a) for a in tables())
    r = lax.axis_index("row")
    nt = lax.axis_size("tm")
    both = ("tm", "row")
    swap = [(i, i ^ 1) for i in range(2 * nt)]
    chain = [(i, (i + 1) % (2 * nt)) for i in range(2 * nt)]
    ahead = [(i, (i + 2) % (2 * nt) if i % 2 == 0 else i) for i in range(2 * nt)]
    back = [(j, i) for i, j in chain]
    meta = jnp.stack([r, (lax.axis_index(both) == 0).astype(jnp.int32)]).astype(jnp.int32)
    wave = wavefront.reshape(8 * N, N)
    unit = 1 << 31

    parts, to_swap, to_chain, to_ahead = call(
        pack_kernel, [(8, FIELDS, N), (2 * N + 4 * FIELDS, N), (2 * N + FIELDS, N), (2 * N + FIELDS, N)],
        [ANY] * 4, [pltpu.VMEM((8, FIELDS, N), F32)], 10, [SM, ANY] + [VM] * 5, 1 << 20,
    )(meta, wave, particle_phase, particle_energy, row_offset, row_cell, col_cell)
    f_swap = lax.ppermute(to_swap, both, swap)
    f_chain = lax.ppermute(to_chain, both, chain)
    f_ahead = lax.ppermute(to_ahead, both, ahead)

    d3, q1, own_a, away_a = call(
        first_kernel, [(2, N, N), (2, FIELDS, N), (1, PIECE, N), (1, PIECE, N)], [VM, ANY, ANY, ANY],
        [FIELD, FIELD, PARTS, PARTS, FIELD] + WORK, 24, [SM, ANY, ANY, ANY, VM, VM], 3 * unit,
    )(meta, wave, parts, f_swap, tab_r, tab_l)
    back_a = lax.ppermute(away_a, both, swap)
    d01, q0, pushed = call(
        second_kernel, [(2, 2, N, N), (2, FIELDS, N), (2, PUSHED, N)], [VM, ANY, ANY],
        [FIELD, FIELD, PARTS, PARTS] + WORK, 24, [SM, ANY, ANY, ANY, ANY, VM, VM], 2 * unit,
    )(meta, parts, f_swap, f_chain, f_ahead, tab_r, tab_l)
    pushed = lax.ppermute(pushed, both, back)
    own_b, away_b = call(
        third_kernel, [(2, PIECE, N), (2, PIECE, N)], [ANY, ANY],
        [FIELD, PARTS, PARTS, FIELD, FIELD] + WORK, 24, [SM, VM, ANY, ANY, VM, VM], 2 * unit,
    )(meta, d01, q0, q1, tab_r, tab_l)
    back_b = lax.ppermute(away_b, both, swap)
    own_c, away_c = call(
        fourth_kernel, [(1, PIECE, N), (1, PIECE, N)], [ANY, ANY],
        [PARTS, FIELD] + WORK, 24, [SM, VM, ANY, ANY, ANY, VM, VM], unit,
    )(meta, d3, parts, f_swap, pushed, tab_r, tab_l)
    back_c = lax.ppermute(away_c, both, swap)
    wave, phase, energy = call(
        final_kernel, [(8 * N, N), (8, PART), (8, PART)], [ANY, VM, VM],
        [pltpu.VMEM((8, PUSHED, N), F32)], 16, [SM] + [ANY] * 6, 1 << 20,
    )(meta, own_a, own_b, own_c, back_a, back_b, back_c)
    return wave.reshape(8, 2, HALF, N), phase, energy


def solution(mesh):
    P = jax.sharding.PartitionSpec
    wide, flat = P("tm", None, "row", None), P("tm", "row")
    return jax.shard_map(body, mesh=mesh, in_specs=(wide,) + (flat,) * 5,
                         out_specs=(wide, flat, flat), check_vma=False)
```

```python
import math

import jax
import jax.numpy as jnp
import ml_dtypes
import numpy as np
from jax import lax
from jax.experimental import pallas as pl
from jax.experimental.pallas import tpu as pltpu

BF = jnp.bfloat16
F32 = jnp.float32
F8 = jnp.float8_e5m2
UP = 1024.0
DOWN = 1.0 / UP
N = 256
HALF = 128
PART = 2048
ROWS = PART // N
WIN = 144
FIELDS = 5 * ROWS
PUSHED = 2 * ROWS
PIECE = 2 * HALF + PUSHED


def split_np(m):
    hi = m.astype(ml_dtypes.bfloat16)
    return hi, (m - hi.astype(np.float64)).astype(ml_dtypes.bfloat16)


def tables():
    k = np.arange(N)
    m = np.where(k < N // 2, k, k - N).astype(np.float64)
    h = np.exp(-1j * np.pi / N * m * m)
    dft = np.exp(-2j * np.pi / N * (k[:, None] * k[None, :] % N))
    a = (np.conj(dft) / N) @ (h[:, None] * dft)
    c0, c1 = a[:HALF, :HALF], a[:HALF, HALF:]
    both = [0.5 * (c0 + c1), 0.5 * (c0 - c1)]
    right = np.stack([np.block([[b.real, b.imag], [-b.imag, b.real]]) for b in both])
    left = np.stack([np.block([[b.real, -b.imag], [b.imag, b.real]]) for b in both])
    return np.stack(split_np(right)), np.stack(split_np(left))


def sincos(x):
    n = jnp.round(x * (1.0 / math.pi))
    r = x - n * 3.140625
    r = r - n * 9.670257568359375e-4
    r = r - n * 6.277114152908325e-07
    half = n * 0.5
    sign = 1.0 - 4.0 * (half - jnp.floor(half))
    y = r * r
    s = -2.3889859e-08
    for c in (2.7525562e-06, -1.98408740e-04, 8.33333310e-03, -1.66666667e-01):
        s = s * y + c
    s = r + r * y * s
    c = 2.08767570e-09 - 1.1470746e-11 * y
    for d in (-2.75573192e-07, 2.48015873e-05, -1.38888889e-03, 4.16666667e-02, -0.5, 1.0):
        c = c * y + d
    return s * sign, c * sign


def hilo(x):
    hi = x.astype(BF)
    return hi, (x - hi.astype(F32)).astype(BF)


def mm(a, b):
    return jnp.dot(a, b, preferred_element_type=F32)


def step(f_ref, p_ref, tab_r, tab_l, out_ref, c_ref, w_ref, s_ref, sr_ref, x_ref, samp_ref, c8_ref, sr8_ref):
    iota_c = (lax.broadcasted_iota(jnp.int32, (16, 16, N), 0) * 16
              + lax.broadcasted_iota(jnp.int32, (16, 16, N), 1)).astype(F32).astype(BF)
    one = jnp.ones((16, N), BF)
    zero = jnp.zeros((16, N), BF)
    down = jnp.full((16, N), DOWN, BF)
    iota_r = lax.broadcasted_iota(jnp.int32, (WIN, N), 0).astype(F32)
    for h in range(2):
        off = p_ref[h, 2 * ROWS:3 * ROWS]
        lower = 0.5 - off
        upper = 0.5 + off
        w_ref[0] = 0.5 * lower * lower
        w_ref[1] = 0.75 - off * off
        w_ref[2] = 0.5 * upper * upper
        win0 = 0 if h == 0 else N - WIN
        field = f_ref[:, win0:win0 + WIN, :].reshape(2 * WIN, N)
        hi = field.astype(BF)
        lo = ((field - hi.astype(F32)) * UP).astype(F8)
        for k in range(ROWS):
            col = jnp.broadcast_to(p_ref[h, 4 * ROWS + k:4 * ROWS + k + 1, :], (16, N)).astype(BF)
            hot = jnp.where(iota_c == col[None], one[None], zero[None]).reshape(N, N)
            c_ref[h, :, N * k:N * k + N] = hot
            hot8 = jnp.where(iota_c == col[None], down[None], zero[None]).reshape(N, N).astype(F8)
            c8_ref[h, :, N * k:N * k + N] = hot8
            g = mm(hi, hot) + mm(lo, hot8)
            at = p_ref[h, 3 * ROWS + k:3 * ROWS + k + 1, :] - float(win0)
            w = jnp.where(iota_r == at, w_ref[1, k:k + 1, :],
                          jnp.where(iota_r == at - 1.0, w_ref[0, k:k + 1, :],
                                    jnp.where(iota_r == at + 1.0, w_ref[2, k:k + 1, :], 0.0)))
            samp_ref[0, k:k + 1, :] = jnp.sum(w * g[:WIN], 0, keepdims=True)
            samp_ref[1, k:k + 1, :] = jnp.sum(w * g[WIN:], 0, keepdims=True)
        phase = p_ref[h, :ROWS]
        sine, cosine = sincos(phase)
        energy = p_ref[h, ROWS:2 * ROWS] - 0.5 * (samp_ref[0] * cosine - samp_ref[1] * sine)
        phase = phase + energy
        p_ref[h, :ROWS] = phase
        p_ref[h, ROWS:2 * ROWS] = energy
        sine, cosine = sincos(phase)
        for z, v in ((0, cosine), (1, -sine)):
            vh = v.astype(BF).astype(F32)
            s_ref[2 * z] = vh
            s_ref[2 * z + 1] = v - vh
        for k in range(ROWS):
            at = jnp.broadcast_to(p_ref[h, 3 * ROWS + k:3 * ROWS + k + 1, :] - float(HALF * h), (16, N)).astype(BF)
            here = iota_c[:8] == at[None]
            for z in range(2):
                value = jnp.broadcast_to(s_ref[2 * z, k:k + 1, :], (16, N)).astype(BF)
                sr_ref[HALF * z:HALF * z + HALF, N * k:N * k + N] = jnp.where(here, value[None], zero[None]).reshape(HALF, N)
                value = jnp.broadcast_to(s_ref[2 * z + 1, k:k + 1, :] * UP, (16, N)).astype(BF)
                sr8_ref[HALF * z:HALF * z + HALF, N * k:N * k + N] = jnp.where(here, value[None], zero[None]).reshape(HALF, N).astype(F8)
        d = lax.dot_general(sr_ref[...], c_ref[h], (((1,), (1,)), ((), ())), preferred_element_type=F32)
        d = d + lax.dot_general(sr8_ref[...], c8_ref[h], (((1,), (1,)), ((), ())), preferred_element_type=F32)
        for z in range(2):
            x_ref[HALF * h:HALF * h + HALF, N * z:N * z + N] = (
                f_ref[z, HALF * h:HALF * h + HALF, :]
                + d[HALF * z:HALF * z + HALF])
    quads = [[], []]
    for z in range(2):
        top = x_ref[:HALF, N * z:N * z + N]
        low = x_ref[HALF:, N * z:N * z + N]
        rows = jnp.concatenate([top + low, top - low], 0)
        quads[0].append(rows[:, :HALF] + rows[:, HALF:])
        quads[1].append(rows[:, :HALF] - rows[:, HALF:])
    turned = []
    for e in range(2):
        xh, xl = hilo(jnp.concatenate(quads[e], 1))
        turned.append(mm(xh, tab_r[0, e]) + mm(xl, tab_r[0, e]) + mm(xh, tab_r[1, e]))
    halves = []
    for e in range(2):
        rows = slice(HALF * e, HALF * e + HALF)
        y = jnp.concatenate([jnp.concatenate([turned[0][rows, :HALF], turned[1][rows, :HALF]], 1),
                             jnp.concatenate([turned[0][rows, HALF:], turned[1][rows, HALF:]], 1)], 0)
        yh, yl = hilo(y)
        halves.append(mm(tab_l[0, e], yh) + mm(tab_l[0, e], yl) + mm(tab_l[1, e], yh))
    for e, rows in enumerate((halves[0] + halves[1], halves[0] - halves[1])):
        left, right = rows[:, :HALF], rows[:, HALF:]
        out = jnp.concatenate([left + right, left - right], 1)
        out_ref[0, HALF * e:HALF * e + HALF] = out[:HALF]
        out_ref[1, HALF * e:HALF * e + HALF] = out[HALF:]


WORK = [pltpu.VMEM((2, N, PART), BF), pltpu.VMEM((3, ROWS, N), F32), pltpu.VMEM((4, ROWS, N), F32),
        pltpu.VMEM((N, PART), BF), pltpu.VMEM((N, 2 * N), F32), pltpu.VMEM((2, ROWS, N), F32),
        pltpu.VMEM((2, N, PART), F8), pltpu.VMEM((N, PART), F8)]
FIELD = pltpu.VMEM((2, N, N), F32)
PARTS = pltpu.VMEM((2, FIELDS, N), F32)
TABLE = pltpu.VMEM((2, 2, N, N), BF)
ANY = pl.BlockSpec(memory_space=pl.ANY)
VM = pl.BlockSpec(memory_space=pltpu.VMEM)
SM = pl.BlockSpec(memory_space=pltpu.SMEM)
HB = pl.BlockSpec(memory_space=pltpu.HBM)


class Copies:
    def __init__(self, sems):
        self.sems = sems
        self.used = 0
        self.open = []

    def start(self, src, dst):
        copy = pltpu.make_async_copy(src, dst, self.sems.at[self.used])
        self.used += 1
        copy.start()
        self.open.append(copy)

    def wait(self):
        for copy in self.open:
            copy.wait()
        self.open = []


def call(kernel, outs, out_specs, scratch, copies, in_specs, flops, aliases={}, vmem=40960):
    return pl.pallas_call(
        kernel, out_shape=[jax.ShapeDtypeStruct(s, F32) for s in outs], in_specs=in_specs, out_specs=out_specs,
        scratch_shapes=scratch + [pltpu.SemaphoreType.DMA((copies,))],
        input_output_aliases=aliases, cost_estimate=pl.CostEstimate(flops=flops, bytes_accessed=4 << 20, transcendentals=0),
        compiler_params=pltpu.CompilerParams(vmem_limit_bytes=vmem << 10))


def pack_kernel(meta, wave, *refs):
    sources, (all_ref, swap_ref, chain_ref, ahead_ref), rest = refs[:5], refs[5:9], refs[9:]
    floats, ints, packed, sems = rest
    r = meta[0]
    rows = 2 * N
    loads, copies = Copies(sems), Copies(sems)
    copies.used = 5
    for a, src in enumerate(sources):
        loads.start(src, floats.at[a] if a < 3 else ints.at[a - 3])
    copies.start(wave.at[pl.ds(N * (4 - 4 * r), rows)], swap_ref.at[pl.ds(0, rows)])
    copies.start(wave.at[pl.ds(N * (2 + 4 * r), rows)], chain_ref.at[pl.ds(0, rows)])
    copies.start(wave.at[pl.ds(N * (6 - 4 * r), rows)], ahead_ref.at[pl.ds(0, rows)])
    loads.wait()
    for a in range(5):
        src = floats.at[a] if a < 3 else ints.at[a - 3]
        for s in range(8):
            for k in range(ROWS):
                packed[s, a * ROWS + k:a * ROWS + k + 1, :] = src[s:s + 1, N * k:N * k + N].astype(F32)
    copies.start(packed, all_ref)
    for i in range(4):
        copies.start(packed.at[4 - 4 * r + i], swap_ref.at[pl.ds(rows + FIELDS * i, FIELDS)])
    copies.start(packed.at[3 + 4 * r], chain_ref.at[pl.ds(rows, FIELDS)])
    copies.start(packed.at[7 - 4 * r], ahead_ref.at[pl.ds(rows, FIELDS)])
    copies.wait()


def field_in(copies, r, f_ref, own, own_row, other, other_row):
    for z in range(2):
        copies.start(own.at[pl.ds(own_row + HALF * z, HALF)], f_ref.at[z, pl.ds(pl.multiple_of(HALF * r, HALF), HALF)])
        copies.start(other.at[pl.ds(other_row + HALF * z, HALF)],
                     f_ref.at[z, pl.ds(pl.multiple_of(HALF - HALF * r, HALF), HALF)])


def piece_out(copies, r, z_ref, p_ref, own, away, i):
    for half, dst in ((r, own), (1 - r, away)):
        for z in range(2):
            copies.start(z_ref.at[z, pl.ds(pl.multiple_of(HALF * half, HALF), HALF)], dst.at[i, pl.ds(HALF * z, HALF)])
        copies.start(p_ref.at[half, pl.ds(0, PUSHED)], dst.at[i, pl.ds(2 * HALF, PUSHED)])


def first_kernel(meta, wave, parts, swap, tab_r, tab_l, d_ref, q_ref, own, away, f2, f3, p1, p2, z, z3, tr, tl, *rest):
    work, sems = rest[:-1], rest[-1]
    r = meta[0]
    copies = Copies(sems)
    field_in(copies, r, f3, wave, N * (4 * r + 1), swap, N)
    for p, i in ((p2, 2), (p1, 1)):
        copies.start(parts.at[4 * r + i], p.at[r])
        copies.start(swap.at[pl.ds(2 * N + FIELDS * i, FIELDS)], p.at[1 - r])
    copies.start(tab_r, tr)
    copies.start(tab_l, tl)
    field_in(copies, r, f2, wave, N * 4 * r, swap, 0)
    copies.wait()
    step(f3, p2, tr, tl, z3, *work)
    copies.start(z3, d_ref)
    step(f2, p1, tr, tl, f3, *work)
    copies.start(p1, q_ref)
    step(f3, p2, tr, tl, z, *work)
    piece_out(copies, r, z, p2, own, away, 0)
    copies.wait()


def second_kernel(meta, after, parts, swap, chain, ahead, tab_r, tab_l, d_ref, q_ref, pushed,
                  f0, f1, p0, pm, z0, z1, tr, tl, *rest):
    work, sems = rest[:-1], rest[-1]
    r = meta[0]
    copies = Copies(sems)
    field_in(copies, r, f0, ahead, 0, chain, 0)
    copies.start(ahead.at[pl.ds(2 * N, FIELDS)], pm.at[r])
    copies.start(chain.at[pl.ds(2 * N, FIELDS)], pm.at[1 - r])
    copies.start(tab_r, tr)
    copies.start(tab_l, tl)
    field_in(copies, r, f1, ahead, N, chain, N)
    copies.start(parts.at[4 * r], p0.at[r])
    copies.start(swap.at[pl.ds(2 * N, FIELDS)], p0.at[1 - r])
    copies.wait()

    @pl.when(meta[1] == 1)
    def _():
        f1[...] = jnp.zeros_like(f1)

    step(f0, pm, tr, tl, z0, *work)
    copies.start(pm.at[:, pl.ds(0, PUSHED)], pushed)
    copies.start(z0, d_ref.at[0])
    step(f1, p0, tr, tl, z1, *work)
    copies.start(p0, q_ref)
    copies.start(z1, d_ref.at[1])
    copies.wait()


def own_out(copies, r, z_ref, wave, slot):
    for z in range(2):
        copies.start(z_ref.at[z, pl.ds(pl.multiple_of(HALF * r, HALF), HALF)],
                     wave.at[pl.ds((4 * r + slot) * N + HALF * z, HALF)])


def third_kernel(meta, d_ref, q0, q1, own_a, back_a, tab_r, tab_l, own, away, wave,
                 f0, f1, p0, p1, z0, z1, tr, tl, *rest):
    work, sems = rest[:-1], rest[-1]
    r = meta[0]
    copies, moves = Copies(sems), Copies(sems)
    moves.used = 24
    copies.start(d_ref.at[0], f0)
    copies.start(q0, p0)
    copies.start(tab_r, tr)
    copies.start(tab_l, tl)
    copies.start(d_ref.at[1], f1)
    copies.start(q1, p1)
    copies.wait()
    for ref, slot in ((own_a, 4 * r + 2), (back_a, 6 - 4 * r)):
        moves.start(ref.at[0, pl.ds(0, N)], wave.at[pl.ds(slot * N, N)])

    @pl.when(meta[1] == 1)
    def _():
        f0[...] = jnp.zeros_like(f0)

    step(f0, p0, tr, tl, z0, *work)
    piece_out(copies, r, z0, p0, own, away, 0)
    own_out(moves, r, z0, wave, 0)
    step(f1, p1, tr, tl, z1, *work)
    piece_out(copies, r, z1, p1, own, away, 1)
    own_out(moves, r, z1, wave, 1)
    copies.wait()
    moves.wait()


def fourth_kernel(meta, d_ref, parts, swap, pushed, tab_r, tab_l, wave_in, own, away, wave, f3, p3, z, tr, tl, *rest):
    work, sems = rest[:-1], rest[-1]
    r = meta[0]
    copies = Copies(sems)
    copies.start(parts.at[4 * r + 3], p3.at[r])
    copies.start(swap.at[pl.ds(2 * N + FIELDS * 3, FIELDS)], p3.at[1 - r])
    copies.start(d_ref, f3)
    copies.start(tab_r, tr)
    copies.start(tab_l, tl)
    copies.wait()
    copies.start(pushed, p3.at[:, pl.ds(0, PUSHED)])
    copies.wait()
    step(f3, p3, tr, tl, z, *work)
    piece_out(copies, r, z, p3, own, away, 0)
    own_out(copies, r, z, wave, 3)
    copies.wait()


def final_kernel(meta, *refs):
    pieces, (wave, phase, energy), (packed, sems) = refs[:6], refs[7:10], refs[10:]
    r = meta[0]
    moves, copies = Copies(sems), Copies(sems)
    copies.used = 4
    for half in range(2):
        base = 4 * r if half == 0 else 4 - 4 * r
        for n, (ref, slots) in enumerate(zip(pieces[3 * half:3 * half + 3], ((2,), (0, 1), (3,)))):
            for i, slot in enumerate(slots):
                if half == 1 and n > 0:
                    moves.start(ref.at[i, pl.ds(0, N)], wave.at[pl.ds((base + slot) * N, N)])
                copies.start(ref.at[i, pl.ds(N, PUSHED)], packed.at[base + slot])
    copies.wait()
    for s in range(8):
        for k in range(ROWS):
            phase[s:s + 1, N * k:N * k + N] = packed[s, k:k + 1, :]
            energy[s:s + 1, N * k:N * k + N] = packed[s, ROWS + k:ROWS + k + 1, :]
    moves.wait()


def body(wavefront, particle_phase, particle_energy, row_offset, row_cell, col_cell):
    tab_r, tab_l = (jnp.asarray(a) for a in tables())
    r = lax.axis_index("row")
    nt = lax.axis_size("tm")
    both = ("tm", "row")
    swap = [(i, i ^ 1) for i in range(2 * nt)]
    chain = [(i, (i + 1) % (2 * nt)) for i in range(2 * nt)]
    ahead = [(i, (i + 2) % (2 * nt) if i % 2 == 0 else i) for i in range(2 * nt)]
    back = [(j, i) for i, j in chain]
    meta = jnp.stack([r, (lax.axis_index(both) == 0).astype(jnp.int32)]).astype(jnp.int32)
    wave = wavefront.reshape(8 * N, N)
    unit = 1 << 33

    parts, to_swap, to_chain, to_ahead = call(
        pack_kernel, [(8, FIELDS, N), (2 * N + 4 * FIELDS, N), (2 * N + FIELDS, N), (2 * N + FIELDS, N)],
        [ANY] * 4, [pltpu.VMEM((3, 8, PART), F32), pltpu.VMEM((2, 8, PART), jnp.int32), pltpu.VMEM((8, FIELDS, N), F32)],
        16, [SM] + [HB] * 6, 1 << 20, vmem=60 << 10,
    )(meta, wave, particle_phase, particle_energy, row_offset, row_cell, col_cell)
    f_swap = lax.ppermute(to_swap, both, swap)
    f_chain = lax.ppermute(to_chain, both, chain)
    f_ahead = lax.ppermute(to_ahead, both, ahead)

    d3, q1, own_a, away_a = call(
        first_kernel, [(2, N, N), (2, FIELDS, N), (1, PIECE, N), (1, PIECE, N)], [ANY] * 4,
        [FIELD, FIELD, PARTS, PARTS, FIELD, FIELD, TABLE, TABLE] + WORK, 32, [SM] + [ANY] * 5, 3 * unit,
    )(meta, wave, parts, f_swap, tab_r, tab_l)
    back_a = lax.ppermute(away_a, both, swap)
    d01, q0, pushed = call(
        second_kernel, [(2, 2, N, N), (2, FIELDS, N), (2, PUSHED, N)], [ANY] * 3,
        [FIELD, FIELD, PARTS, PARTS, FIELD, FIELD, TABLE, TABLE] + WORK, 32, [SM] + [ANY] * 7, 2 * unit,
    )(meta, q1, parts, f_swap, f_chain, f_ahead, tab_r, tab_l)
    pushed = lax.ppermute(pushed, both, back)
    own_b, away_b, wave = call(
        third_kernel, [(2, PIECE, N), (2, PIECE, N), (8 * N, N)], [ANY] * 3,
        [FIELD, FIELD, PARTS, PARTS, FIELD, FIELD, TABLE, TABLE] + WORK, 32, [SM] + [ANY] * 7, 2 * unit,
    )(meta, d01, q0, q1, own_a, back_a, tab_r, tab_l)
    back_b = lax.ppermute(away_b, both, swap)
    own_c, away_c, wave = call(
        fourth_kernel, [(1, PIECE, N), (1, PIECE, N), (8 * N, N)], [ANY] * 3,
        [FIELD, PARTS, FIELD, TABLE, TABLE] + WORK, 32, [SM] + [ANY] * 7, 2 * unit, {7: 2},
    )(meta, d3, parts, f_swap, pushed, tab_r, tab_l, wave)
    back_c = lax.ppermute(away_c, both, swap)
    wave, phase, energy = call(
        final_kernel, [(8 * N, N), (8, PART), (8, PART)], [HB, VM, VM],
        [pltpu.VMEM((8, PUSHED, N), F32)], 16, [SM] + [ANY] * 6 + [HB], 1 << 20, {7: 0},
    )(meta, own_a, own_b, own_c, back_a, back_b, back_c, wave)
    return wave.reshape(8, 2, HALF, N), phase, energy


def solution(mesh):
    P = jax.sharding.PartitionSpec
    wide, flat = P("tm", None, "row", None), P("tm", "row")
    return jax.shard_map(body, mesh=mesh, in_specs=(wide,) + (flat,) * 5,
                         out_specs=(wide, flat, flat), check_vma=False)
```

```python
import math

import jax
import jax.numpy as jnp
import ml_dtypes
import numpy as np
from jax import lax
from jax.experimental import pallas as pl
from jax.experimental.pallas import tpu as pltpu

BF = jnp.bfloat16
F32 = jnp.float32
F8 = jnp.float8_e5m2
UP = 1024.0
DOWN = 1.0 / UP
N = 256
HALF = 128
PART = 2048
ROWS = PART // N
WIN = 144
FIELDS = 5 * ROWS
PUSHED = 2 * ROWS
PIECE = 2 * HALF + PUSHED


def split_np(m):
    hi = m.astype(ml_dtypes.bfloat16)
    return hi, (m - hi.astype(np.float64)).astype(ml_dtypes.bfloat16)


def tables():
    k = np.arange(N)
    m = np.where(k < N // 2, k, k - N).astype(np.float64)
    h = np.exp(-1j * np.pi / N * m * m)
    dft = np.exp(-2j * np.pi / N * (k[:, None] * k[None, :] % N))
    a = (np.conj(dft) / N) @ (h[:, None] * dft)
    c0, c1 = a[:HALF, :HALF], a[:HALF, HALF:]
    both = [0.5 * (c0 + c1), 0.5 * (c0 - c1)]
    right = np.stack([np.block([[b.real, b.imag], [-b.imag, b.real]]) for b in both])
    left = np.stack([np.block([[b.real, -b.imag], [b.imag, b.real]]) for b in both])
    return np.stack(split_np(np.stack([right, left])))


def sincos(x):
    n = jnp.round(x * (1.0 / math.pi))
    r = x - n * 3.140625
    r = r - n * 9.670257568359375e-4
    r = r - n * 6.277114152908325e-07
    half = n * 0.5
    sign = 1.0 - 4.0 * (half - jnp.floor(half))
    y = r * r
    s = -2.3889859e-08
    for c in (2.7525562e-06, -1.98408740e-04, 8.33333310e-03, -1.66666667e-01):
        s = s * y + c
    s = r + r * y * s
    c = 2.08767570e-09 - 1.1470746e-11 * y
    for d in (-2.75573192e-07, 2.48015873e-05, -1.38888889e-03, 4.16666667e-02, -0.5, 1.0):
        c = c * y + d
    return s * sign, c * sign


def hilo(x):
    hi = x.astype(BF)
    return hi, (x - hi.astype(F32)).astype(BF)


def mm(a, b):
    return jnp.dot(a, b, preferred_element_type=F32)


def step(f_ref, p_ref, tab, out_ref, c_ref, w_ref, s_ref, sr_ref, x_ref, samp_ref, c8_ref, sr8_ref):
    iota_c = (lax.broadcasted_iota(jnp.int32, (16, 16, N), 0) * 16
              + lax.broadcasted_iota(jnp.int32, (16, 16, N), 1)).astype(F32).astype(BF)
    one = jnp.ones((16, N), BF)
    zero = jnp.zeros((16, N), BF)
    down = jnp.full((16, N), DOWN, BF)
    iota_r = lax.broadcasted_iota(jnp.int32, (WIN, N), 0).astype(F32)
    for h in range(2):
        off = p_ref[h, 2 * ROWS:3 * ROWS]
        lower = 0.5 - off
        upper = 0.5 + off
        w_ref[0] = 0.5 * lower * lower
        w_ref[1] = 0.75 - off * off
        w_ref[2] = 0.5 * upper * upper
        win0 = 0 if h == 0 else N - WIN
        field = f_ref[:, win0:win0 + WIN, :].reshape(2 * WIN, N)
        hi = field.astype(BF)
        lo = ((field - hi.astype(F32)) * UP).astype(F8)
        for k in range(ROWS):
            col = jnp.broadcast_to(p_ref[h, 4 * ROWS + k:4 * ROWS + k + 1, :], (16, N)).astype(BF)
            hot = jnp.where(iota_c == col[None], one[None], zero[None]).reshape(N, N)
            c_ref[h, :, N * k:N * k + N] = hot
            hot8 = jnp.where(iota_c == col[None], down[None], zero[None]).reshape(N, N).astype(F8)
            c8_ref[h, :, N * k:N * k + N] = hot8
            g = mm(hi, hot) + mm(lo, hot8)
            at = p_ref[h, 3 * ROWS + k:3 * ROWS + k + 1, :] - float(win0)
            w = jnp.where(iota_r == at, w_ref[1, k:k + 1, :],
                          jnp.where(iota_r == at - 1.0, w_ref[0, k:k + 1, :],
                                    jnp.where(iota_r == at + 1.0, w_ref[2, k:k + 1, :], 0.0)))
            samp_ref[0, k:k + 1, :] = jnp.sum(w * g[:WIN], 0, keepdims=True)
            samp_ref[1, k:k + 1, :] = jnp.sum(w * g[WIN:], 0, keepdims=True)
        phase = p_ref[h, :ROWS]
        sine, cosine = sincos(phase)
        energy = p_ref[h, ROWS:2 * ROWS] - 0.5 * (samp_ref[0] * cosine - samp_ref[1] * sine)
        phase = phase + energy
        p_ref[h, :ROWS] = phase
        p_ref[h, ROWS:2 * ROWS] = energy
        sine, cosine = sincos(phase)
        for z, v in ((0, cosine), (1, -sine)):
            vh = v.astype(BF).astype(F32)
            s_ref[2 * z] = vh
            s_ref[2 * z + 1] = v - vh
        for k in range(ROWS):
            at = jnp.broadcast_to(p_ref[h, 3 * ROWS + k:3 * ROWS + k + 1, :] - float(HALF * h), (16, N)).astype(BF)
            here = iota_c[:8] == at[None]
            for z in range(2):
                value = jnp.broadcast_to(s_ref[2 * z, k:k + 1, :], (16, N)).astype(BF)
                sr_ref[HALF * z:HALF * z + HALF, N * k:N * k + N] = jnp.where(here, value[None], zero[None]).reshape(HALF, N)
                value = jnp.broadcast_to(s_ref[2 * z + 1, k:k + 1, :] * UP, (16, N)).astype(BF)
                sr8_ref[HALF * z:HALF * z + HALF, N * k:N * k + N] = jnp.where(here, value[None], zero[None]).reshape(HALF, N).astype(F8)
        d = lax.dot_general(sr_ref[...], c_ref[h], (((1,), (1,)), ((), ())), preferred_element_type=F32)
        d = d + lax.dot_general(sr8_ref[...], c8_ref[h], (((1,), (1,)), ((), ())), preferred_element_type=F32)
        for z in range(2):
            x_ref[HALF * h:HALF * h + HALF, N * z:N * z + N] = (
                f_ref[z, HALF * h:HALF * h + HALF, :]
                + d[HALF * z:HALF * z + HALF])
    quads = [[], []]
    for z in range(2):
        top = x_ref[:HALF, N * z:N * z + N]
        low = x_ref[HALF:, N * z:N * z + N]
        rows = jnp.concatenate([top + low, top - low], 0)
        quads[0].append(rows[:, :HALF] + rows[:, HALF:])
        quads[1].append(rows[:, :HALF] - rows[:, HALF:])
    turned = []
    for e in range(2):
        xh, xl = hilo(jnp.concatenate(quads[e], 1))
        turned.append(mm(xh, tab[0, 0, e]) + mm(xl, tab[0, 0, e]) + mm(xh, tab[1, 0, e]))
    halves = []
    for e in range(2):
        rows = slice(HALF * e, HALF * e + HALF)
        y = jnp.concatenate([jnp.concatenate([turned[0][rows, :HALF], turned[1][rows, :HALF]], 1),
                             jnp.concatenate([turned[0][rows, HALF:], turned[1][rows, HALF:]], 1)], 0)
        yh, yl = hilo(y)
        halves.append(mm(tab[0, 1, e], yh) + mm(tab[0, 1, e], yl) + mm(tab[1, 1, e], yh))
    for e, rows in enumerate((halves[0] + halves[1], halves[0] - halves[1])):
        left, right = rows[:, :HALF], rows[:, HALF:]
        out = jnp.concatenate([left + right, left - right], 1)
        out_ref[0, HALF * e:HALF * e + HALF] = out[:HALF]
        out_ref[1, HALF * e:HALF * e + HALF] = out[HALF:]


WORK = [pltpu.VMEM((2, N, PART), BF), pltpu.VMEM((3, ROWS, N), F32), pltpu.VMEM((4, ROWS, N), F32),
        pltpu.VMEM((N, PART), BF), pltpu.VMEM((N, 2 * N), F32), pltpu.VMEM((2, ROWS, N), F32),
        pltpu.VMEM((2, N, PART), F8), pltpu.VMEM((N, PART), F8)]
FIELD = pltpu.VMEM((2, N, N), F32)
PARTS = pltpu.VMEM((2, FIELDS, N), F32)
TABLE = pltpu.VMEM((2, 2, 2, N, N), BF)
ANY = pl.BlockSpec(memory_space=pl.ANY)
VM = pl.BlockSpec(memory_space=pltpu.VMEM)
SM = pl.BlockSpec(memory_space=pltpu.SMEM)
HB = pl.BlockSpec(memory_space=pltpu.HBM)


class Copies:
    def __init__(self, sems):
        self.sems = sems
        self.used = 0
        self.open = []

    def start(self, src, dst):
        copy = pltpu.make_async_copy(src, dst, self.sems.at[self.used])
        self.used += 1
        copy.start()
        self.open.append(copy)

    def wait(self):
        for copy in self.open:
            copy.wait()
        self.open = []


def call(kernel, outs, out_specs, scratch, copies, in_specs, flops, aliases={}, vmem=40 << 20):
    return pl.pallas_call(
        kernel, out_shape=[jax.ShapeDtypeStruct(s, F32) for s in outs], in_specs=in_specs, out_specs=out_specs,
        scratch_shapes=scratch + [pltpu.SemaphoreType.DMA((copies,))],
        input_output_aliases=aliases, cost_estimate=pl.CostEstimate(flops=flops, bytes_accessed=4 << 20, transcendentals=0),
        compiler_params=pltpu.CompilerParams(vmem_limit_bytes=vmem))


def pack_kernel(meta, wave, *refs):
    sources, (all_ref, swap_ref, chain_ref, ahead_ref), (floats, ints, sems) = refs[:5], refs[5:9], refs[9:]
    r = meta[0]
    rows = 2 * N
    loads, copies = Copies(sems), Copies(sems)
    copies.used = 5
    for a, src in enumerate(sources):
        loads.start(src, floats.at[a] if a < 3 else ints.at[a - 3])
    copies.start(wave.at[pl.ds(N * (4 - 4 * r), rows)], swap_ref.at[pl.ds(0, rows)])
    copies.start(wave.at[pl.ds(N * (2 + 4 * r), rows)], chain_ref.at[pl.ds(0, rows)])
    copies.start(wave.at[pl.ds(N * (6 - 4 * r), rows)], ahead_ref.at[pl.ds(0, rows)])
    loads.wait()
    for a in range(5):
        src = floats.at[a] if a < 3 else ints.at[a - 3]
        for s in range(8):
            for k in range(ROWS):
                all_ref[s, a * ROWS + k:a * ROWS + k + 1, :] = src[s:s + 1, N * k:N * k + N].astype(F32)
    for i in range(4):
        swap_ref[rows + FIELDS * i:rows + FIELDS * i + FIELDS, :] = all_ref[4 - 4 * r + i]
    chain_ref[rows:, :] = all_ref[3 + 4 * r]
    ahead_ref[rows:, :] = all_ref[7 - 4 * r]
    copies.wait()


def field_in(copies, r, f_ref, own, own_row, other, other_row):
    for z in range(2):
        copies.start(own.at[pl.ds(own_row + HALF * z, HALF)], f_ref.at[z, pl.ds(pl.multiple_of(HALF * r, HALF), HALF)])
        copies.start(other.at[pl.ds(other_row + HALF * z, HALF)],
                     f_ref.at[z, pl.ds(pl.multiple_of(HALF - HALF * r, HALF), HALF)])


def piece_out(copies, r, z_ref, p_ref, own, away, i):
    for half, dst in ((r, own), (1 - r, away)):
        for z in range(2):
            copies.start(z_ref.at[z, pl.ds(pl.multiple_of(HALF * half, HALF), HALF)], dst.at[i, pl.ds(HALF * z, HALF)])
        copies.start(p_ref.at[half, pl.ds(0, PUSHED)], dst.at[i, pl.ds(2 * HALF, PUSHED)])


def first_kernel(meta, wave, parts, swap, table, d_ref, q_ref, own, away, f2, f3, p1, p2, z, z3, tab, *rest):
    work, sems = rest[:-1], rest[-1]
    r = meta[0]
    copies = Copies(sems)
    field_in(copies, r, f3, wave, N * (4 * r + 1), swap, N)
    for p, i in ((p2, 2), (p1, 1)):
        copies.start(parts.at[4 * r + i], p.at[r])
        copies.start(swap.at[pl.ds(2 * N + FIELDS * i, FIELDS)], p.at[1 - r])
    copies.start(table, tab)
    field_in(copies, r, f2, wave, N * 4 * r, swap, 0)
    copies.wait()
    step(f3, p2, tab, z3, *work)
    copies.start(z3, d_ref)
    step(f2, p1, tab, f3, *work)
    copies.start(p1, q_ref)
    step(f3, p2, tab, z, *work)
    piece_out(copies, r, z, p2, own, away, 0)
    copies.wait()


def second_kernel(meta, q1, parts, swap, chain, ahead, table, d_ref, q_ref, pushed, own, away,
                  f0, f1, p0, p1, pm, z0, z1, tab, *rest):
    work, sems = rest[:-1], rest[-1]
    r = meta[0]
    copies = Copies(sems)
    field_in(copies, r, f0, ahead, 0, chain, 0)
    copies.start(ahead.at[pl.ds(2 * N, FIELDS)], pm.at[r])
    copies.start(chain.at[pl.ds(2 * N, FIELDS)], pm.at[1 - r])
    copies.start(table, tab)
    field_in(copies, r, f1, ahead, N, chain, N)
    copies.start(parts.at[4 * r], p0.at[r])
    copies.start(swap.at[pl.ds(2 * N, FIELDS)], p0.at[1 - r])
    copies.start(q1, p1)
    copies.wait()

    @pl.when(meta[1] == 1)
    def _():
        f1[...] = jnp.zeros_like(f1)

    step(f0, pm, tab, z0, *work)
    copies.start(pm.at[:, pl.ds(0, PUSHED)], pushed)
    copies.start(z0, d_ref)
    step(f1, p0, tab, z1, *work)
    copies.start(p0, q_ref)
    step(z1, p1, tab, f1, *work)
    piece_out(copies, r, f1, p1, own, away, 0)
    copies.wait()


def own_out(copies, r, z_ref, wave, slot):
    for z in range(2):
        copies.start(z_ref.at[z, pl.ds(pl.multiple_of(HALF * r, HALF), HALF)],
                     wave.at[pl.ds((4 * r + slot) * N + HALF * z, HALF)])


def third_kernel(meta, d_ref, q0, own_a, own_b, back_a, table, own, away, wave, f0, p0, z0, tab, *rest):
    work, sems = rest[:-1], rest[-1]
    r = meta[0]
    copies, moves = Copies(sems), Copies(sems)
    moves.used = 16
    copies.start(d_ref, f0)
    copies.start(q0, p0)
    copies.start(table, tab)
    copies.wait()
    for ref, slot in ((own_a, 4 * r + 2), (own_b, 4 * r + 1), (back_a, 6 - 4 * r)):
        moves.start(ref.at[0, pl.ds(0, N)], wave.at[pl.ds(slot * N, N)])

    @pl.when(meta[1] == 1)
    def _():
        f0[...] = jnp.zeros_like(f0)

    step(f0, p0, tab, z0, *work)
    piece_out(copies, r, z0, p0, own, away, 0)
    own_out(moves, r, z0, wave, 0)
    copies.wait()
    moves.wait()


def fourth_kernel(meta, d_ref, parts, swap, pushed, table, wave_in, own, away, wave, f3, p3, z, tab, *rest):
    work, sems = rest[:-1], rest[-1]
    r = meta[0]
    copies = Copies(sems)
    copies.start(parts.at[4 * r + 3], p3.at[r])
    copies.start(swap.at[pl.ds(2 * N + FIELDS * 3, FIELDS)], p3.at[1 - r])
    copies.start(d_ref, f3)
    copies.start(table, tab)
    copies.wait()
    copies.start(pushed, p3.at[:, pl.ds(0, PUSHED)])
    copies.wait()
    step(f3, p3, tab, z, *work)
    piece_out(copies, r, z, p3, own, away, 0)
    own_out(copies, r, z, wave, 3)
    copies.wait()


def final_kernel(meta, *refs):
    pieces, (wave, phase, energy), (packed, sems) = refs[:8], refs[9:12], refs[12:]
    r = meta[0]
    moves, copies = Copies(sems), Copies(sems)
    copies.used = 4
    for half in range(2):
        base = 4 * r if half == 0 else 4 - 4 * r
        for n, (ref, slot) in enumerate(zip(pieces[4 * half:4 * half + 4], (2, 1, 0, 3))):
            if half == 1 and n > 0:
                moves.start(ref.at[0, pl.ds(0, N)], wave.at[pl.ds((base + slot) * N, N)])
            copies.start(ref.at[0, pl.ds(N, PUSHED)], packed.at[base + slot])
    copies.wait()
    for s in range(8):
        for k in range(ROWS):
            phase[s:s + 1, N * k:N * k + N] = packed[s, k:k + 1, :]
            energy[s:s + 1, N * k:N * k + N] = packed[s, ROWS + k:ROWS + k + 1, :]
    moves.wait()


def body(wavefront, particle_phase, particle_energy, row_offset, row_cell, col_cell):
    table = jnp.asarray(tables())
    r = lax.axis_index("row")
    nt = lax.axis_size("tm")
    both = ("tm", "row")
    swap = [(i, i ^ 1) for i in range(2 * nt)]
    chain = [(i, (i + 1) % (2 * nt)) for i in range(2 * nt)]
    ahead = [(i, (i + 2) % (2 * nt) if i % 2 == 0 else i) for i in range(2 * nt)]
    back = [(j, i) for i, j in chain]
    meta = jnp.stack([r, (lax.axis_index(both) == 0).astype(jnp.int32)]).astype(jnp.int32)
    wave = wavefront.reshape(8 * N, N)
    unit = 1 << 33

    parts, to_swap, to_chain, to_ahead = call(
        pack_kernel, [(8, FIELDS, N), (2 * N + 4 * FIELDS, N), (2 * N + FIELDS, N), (2 * N + FIELDS, N)],
        [VM] * 4, [pltpu.VMEM((3, 8, PART), F32), pltpu.VMEM((2, 8, PART), jnp.int32)],
        16, [SM] + [HB] * 6, 1 << 20, vmem=61000 << 10,
    )(meta, wave, particle_phase, particle_energy, row_offset, row_cell, col_cell)
    f_swap = lax.ppermute(to_swap, both, swap)
    f_chain = lax.ppermute(to_chain, both, chain)
    f_ahead = lax.ppermute(to_ahead, both, ahead)

    d3, q1, own_a, away_a = call(
        first_kernel, [(2, N, N), (2, FIELDS, N), (1, PIECE, N), (1, PIECE, N)], [ANY] * 4,
        [FIELD, FIELD, PARTS, PARTS, FIELD, FIELD, TABLE] + WORK, 32, [SM] + [ANY] * 4, 3 * unit,
    )(meta, wave, parts, f_swap, table)
    back_a = lax.ppermute(away_a, both, swap)
    d0, q0, pushed, own_b, away_b = call(
        second_kernel, [(2, N, N), (2, FIELDS, N), (2, PUSHED, N), (1, PIECE, N), (1, PIECE, N)], [ANY] * 5,
        [FIELD, FIELD, PARTS, PARTS, PARTS, FIELD, FIELD, TABLE] + WORK, 32, [SM] + [ANY] * 6, 3 * unit,
    )(meta, q1, parts, f_swap, f_chain, f_ahead, table)
    pushed = lax.ppermute(pushed, both, back)
    back_b = lax.ppermute(away_b, both, swap)
    own_c, away_c, wave = call(
        third_kernel, [(1, PIECE, N), (1, PIECE, N), (8 * N, N)], [ANY] * 3,
        [FIELD, PARTS, FIELD, TABLE] + WORK, 32, [SM] + [ANY] * 6, unit,
    )(meta, d0, q0, own_a, own_b, back_a, table)
    back_c = lax.ppermute(away_c, both, swap)
    own_d, away_d, wave = call(
        fourth_kernel, [(1, PIECE, N), (1, PIECE, N), (8 * N, N)], [ANY] * 3,
        [FIELD, PARTS, FIELD, TABLE] + WORK, 32, [SM] + [ANY] * 6, 2 * unit, {6: 2},
    )(meta, d3, parts, f_swap, pushed, table, wave)
    back_d = lax.ppermute(away_d, both, swap)
    wave, phase, energy = call(
        final_kernel, [(8 * N, N), (8, PART), (8, PART)], [HB, VM, VM],
        [pltpu.VMEM((8, PUSHED, N), F32)], 16, [SM] + [ANY] * 8 + [HB], 1 << 20, {9: 0},
    )(meta, own_a, own_b, own_c, own_d, back_a, back_b, back_c, back_d, wave)
    return wave.reshape(8, 2, HALF, N), phase, energy


def solution(mesh):
    P = jax.sharding.PartitionSpec
    wide, flat = P("tm", None, "row", None), P("tm", "row")
    return jax.shard_map(body, mesh=mesh, in_specs=(wide,) + (flat,) * 5,
                         out_specs=(wide, flat, flat), check_vma=False)
```

```python
import math

import jax
import jax.numpy as jnp
import ml_dtypes
import numpy as np
from jax import lax
from jax.experimental import pallas as pl
from jax.experimental.pallas import tpu as pltpu

BF = jnp.bfloat16
F32 = jnp.float32
F8 = jnp.float8_e5m2
UP = 1024.0
DOWN = 1.0 / UP
N = 256
HALF = 128
PART = 2048
ROWS = PART // N
WIN = 144
FIELDS = 5 * ROWS
PUSHED = 2 * ROWS
PIECE = 2 * HALF + PUSHED


def split_np(m):
    hi = m.astype(ml_dtypes.bfloat16)
    return hi, (m - hi.astype(np.float64)).astype(ml_dtypes.bfloat16)


def tables():
    k = np.arange(N)
    m = np.where(k < N // 2, k, k - N).astype(np.float64)
    h = np.exp(-1j * np.pi / N * m * m)
    dft = np.exp(-2j * np.pi / N * (k[:, None] * k[None, :] % N))
    a = (np.conj(dft) / N) @ (h[:, None] * dft)
    c0, c1 = a[:HALF, :HALF], a[:HALF, HALF:]
    both = [0.5 * (c0 + c1), 0.5 * (c0 - c1)]
    right = np.stack([np.block([[b.real, b.imag], [-b.imag, b.real]]) for b in both])
    left = np.stack([np.block([[b.real, -b.imag], [b.imag, b.real]]) for b in both])
    return np.stack(split_np(np.stack([right, left])))


def sincos(x):
    n = jnp.round(x * (1.0 / math.pi))
    r = x - n * 3.140625
    r = r - n * 9.670257568359375e-4
    r = r - n * 6.277114152908325e-07
    half = n * 0.5
    sign = 1.0 - 4.0 * (half - jnp.floor(half))
    y = r * r
    s = -2.3889859e-08
    for c in (2.7525562e-06, -1.98408740e-04, 8.33333310e-03, -1.66666667e-01):
        s = s * y + c
    s = r + r * y * s
    c = 2.08767570e-09 - 1.1470746e-11 * y
    for d in (-2.75573192e-07, 2.48015873e-05, -1.38888889e-03, 4.16666667e-02, -0.5, 1.0):
        c = c * y + d
    return s * sign, c * sign


def hilo(x):
    hi = x.astype(BF)
    return hi, (x - hi.astype(F32)).astype(BF)


def mm(a, b):
    return jnp.dot(a, b, preferred_element_type=F32)


def step(f_ref, p_ref, q_ref, tab, out_ref, c_ref, w_ref, s_ref, sr_ref, x_ref, samp_ref, c8_ref, sr8_ref):
    iota_c = (lax.broadcasted_iota(jnp.int32, (16, 16, N), 0) * 16
              + lax.broadcasted_iota(jnp.int32, (16, 16, N), 1)).astype(F32).astype(BF)
    one = jnp.ones((16, N), BF)
    zero = jnp.zeros((16, N), BF)
    down = jnp.full((16, N), DOWN, BF)
    iota_r = lax.broadcasted_iota(jnp.int32, (WIN, N), 0).astype(F32)
    for h in range(2):
        off = p_ref[h, 2 * ROWS:3 * ROWS]
        lower = 0.5 - off
        upper = 0.5 + off
        w_ref[0] = 0.5 * lower * lower
        w_ref[1] = 0.75 - off * off
        w_ref[2] = 0.5 * upper * upper
        win0 = 0 if h == 0 else N - WIN
        field = f_ref[:, win0:win0 + WIN, :].reshape(2 * WIN, N)
        hi = field.astype(BF)
        lo = ((field - hi.astype(F32)) * UP).astype(F8)
        for k in range(ROWS):
            col = jnp.broadcast_to(p_ref[h, 4 * ROWS + k:4 * ROWS + k + 1, :], (16, N)).astype(BF)
            hot = jnp.where(iota_c == col[None], one[None], zero[None]).reshape(N, N)
            c_ref[h, :, N * k:N * k + N] = hot
            hot8 = jnp.where(iota_c == col[None], down[None], zero[None]).reshape(N, N).astype(F8)
            c8_ref[h, :, N * k:N * k + N] = hot8
            g = mm(hi, hot) + mm(lo, hot8)
            at = p_ref[h, 3 * ROWS + k:3 * ROWS + k + 1, :] - float(win0)
            w = jnp.where(iota_r == at, w_ref[1, k:k + 1, :],
                          jnp.where(iota_r == at - 1.0, w_ref[0, k:k + 1, :],
                                    jnp.where(iota_r == at + 1.0, w_ref[2, k:k + 1, :], 0.0)))
            samp_ref[0, k:k + 1, :] = jnp.sum(w * g[:WIN], 0, keepdims=True)
            samp_ref[1, k:k + 1, :] = jnp.sum(w * g[WIN:], 0, keepdims=True)
        phase = p_ref[h, :ROWS]
        sine, cosine = sincos(phase)
        energy = p_ref[h, ROWS:2 * ROWS] - 0.5 * (samp_ref[0] * cosine - samp_ref[1] * sine)
        phase = phase + energy
        q_ref[h, :ROWS] = phase
        q_ref[h, ROWS:2 * ROWS] = energy
        sine, cosine = sincos(phase)
        for z, v in ((0, cosine), (1, -sine)):
            vh = v.astype(BF).astype(F32)
            s_ref[2 * z] = vh
            s_ref[2 * z + 1] = v - vh
        for k in range(ROWS):
            at = jnp.broadcast_to(p_ref[h, 3 * ROWS + k:3 * ROWS + k + 1, :] - float(HALF * h), (16, N)).astype(BF)
            here = iota_c[:8] == at[None]
            for z in range(2):
                value = jnp.broadcast_to(s_ref[2 * z, k:k + 1, :], (16, N)).astype(BF)
                sr_ref[HALF * z:HALF * z + HALF, N * k:N * k + N] = jnp.where(here, value[None], zero[None]).reshape(HALF, N)
                value = jnp.broadcast_to(s_ref[2 * z + 1, k:k + 1, :] * UP, (16, N)).astype(BF)
                sr8_ref[HALF * z:HALF * z + HALF, N * k:N * k + N] = jnp.where(here, value[None], zero[None]).reshape(HALF, N).astype(F8)
        d = lax.dot_general(sr_ref[...], c_ref[h], (((1,), (1,)), ((), ())), preferred_element_type=F32)
        d = d + lax.dot_general(sr8_ref[...], c8_ref[h], (((1,), (1,)), ((), ())), preferred_element_type=F32)
        for z in range(2):
            x_ref[HALF * h:HALF * h + HALF, N * z:N * z + N] = (
                f_ref[z, HALF * h:HALF * h + HALF, :]
                + d[HALF * z:HALF * z + HALF])
    quads = [[], []]
    for z in range(2):
        top = x_ref[:HALF, N * z:N * z + N]
        low = x_ref[HALF:, N * z:N * z + N]
        rows = jnp.concatenate([top + low, top - low], 0)
        quads[0].append(rows[:, :HALF] + rows[:, HALF:])
        quads[1].append(rows[:, :HALF] - rows[:, HALF:])
    turned = []
    for e in range(2):
        xh, xl = hilo(jnp.concatenate(quads[e], 1))
        turned.append(mm(xh, tab[0, 0, e]) + mm(xl, tab[0, 0, e]) + mm(xh, tab[1, 0, e]))
    halves = []
    for e in range(2):
        rows = slice(HALF * e, HALF * e + HALF)
        y = jnp.concatenate([jnp.concatenate([turned[0][rows, :HALF], turned[1][rows, :HALF]], 1),
                             jnp.concatenate([turned[0][rows, HALF:], turned[1][rows, HALF:]], 1)], 0)
        yh, yl = hilo(y)
        halves.append(mm(tab[0, 1, e], yh) + mm(tab[0, 1, e], yl) + mm(tab[1, 1, e], yh))
    for e, rows in enumerate((halves[0] + halves[1], halves[0] - halves[1])):
        left, right = rows[:, :HALF], rows[:, HALF:]
        out = jnp.concatenate([left + right, left - right], 1)
        out_ref[0, HALF * e:HALF * e + HALF] = out[:HALF]
        out_ref[1, HALF * e:HALF * e + HALF] = out[HALF:]


WORK = [pltpu.VMEM((2, N, PART), BF), pltpu.VMEM((3, ROWS, N), F32), pltpu.VMEM((4, ROWS, N), F32),
        pltpu.VMEM((N, PART), BF), pltpu.VMEM((N, 2 * N), F32), pltpu.VMEM((2, ROWS, N), F32),
        pltpu.VMEM((2, N, PART), F8), pltpu.VMEM((N, PART), F8)]
FIELD = pltpu.VMEM((2, N, N), F32)
PARTS = pltpu.VMEM((2, FIELDS, N), F32)
TABLE = pltpu.VMEM((2, 2, 2, N, N), BF)
PUSH = pltpu.VMEM((2, PUSHED, N), F32)
ANY = pl.BlockSpec(memory_space=pl.ANY)
VM = pl.BlockSpec(memory_space=pltpu.VMEM)
SM = pl.BlockSpec(memory_space=pltpu.SMEM)
HB = pl.BlockSpec(memory_space=pltpu.HBM)


class Copies:
    def __init__(self, sems):
        self.sems = sems
        self.used = 0
        self.open = []

    def start(self, src, dst):
        copy = pltpu.make_async_copy(src, dst, self.sems.at[self.used])
        self.used += 1
        copy.start()
        self.open.append(copy)

    def wait(self):
        for copy in self.open:
            copy.wait()
        self.open = []


def call(kernel, outs, out_specs, scratch, copies, in_specs, flops, aliases={}, vmem=40 << 20):
    return pl.pallas_call(
        kernel, out_shape=[jax.ShapeDtypeStruct(s, F32) for s in outs], in_specs=in_specs, out_specs=out_specs,
        scratch_shapes=scratch + [pltpu.SemaphoreType.DMA((copies,))],
        input_output_aliases=aliases, cost_estimate=pl.CostEstimate(flops=flops, bytes_accessed=4 << 20, transcendentals=0),
        compiler_params=pltpu.CompilerParams(vmem_limit_bytes=vmem))


def pack_kernel(meta, wave, *refs):
    sources, (all_ref, near_ref, swap_ref, chain_ref, ahead_ref), (floats, ints, sems) = refs[:5], refs[5:10], refs[10:]
    r = meta[0]
    loads, copies = Copies(sems), Copies(sems)
    copies.used = 5
    for a, src in enumerate(sources):
        loads.start(src, floats.at[a] if a < 3 else ints.at[a - 3])
    copies.start(wave.at[pl.ds(N * (6 - 4 * r), 2 * N)], ahead_ref.at[pl.ds(0, 2 * N)])
    copies.start(wave.at[pl.ds(N * (5 - 4 * r), N)], near_ref.at[pl.ds(0, N)])
    copies.start(wave.at[pl.ds(N * (4 - 4 * r), N)], swap_ref.at[pl.ds(0, N)])
    copies.start(wave.at[pl.ds(N * (2 + 4 * r), 2 * N)], chain_ref.at[pl.ds(0, 2 * N)])
    loads.wait()
    for a in range(5):
        src = floats.at[a] if a < 3 else ints.at[a - 3]
        for s in range(8):
            for k in range(ROWS):
                all_ref[s, a * ROWS + k:a * ROWS + k + 1, :] = src[s:s + 1, N * k:N * k + N].astype(F32)
    near_ref[N:, :] = all_ref[6 - 4 * r]
    for i, rel in enumerate((0, 1, 3)):
        swap_ref[N + FIELDS * i:N + FIELDS * i + FIELDS, :] = all_ref[4 - 4 * r + rel]
    chain_ref[2 * N:, :] = all_ref[3 + 4 * r]
    ahead_ref[2 * N:, :] = all_ref[7 - 4 * r]
    copies.wait()


def field_in(copies, r, f_ref, own, own_row, other, other_row):
    for z in range(2):
        copies.start(own.at[pl.ds(own_row + HALF * z, HALF)], f_ref.at[z, pl.ds(pl.multiple_of(HALF * r, HALF), HALF)])
        copies.start(other.at[pl.ds(other_row + HALF * z, HALF)],
                     f_ref.at[z, pl.ds(pl.multiple_of(HALF - HALF * r, HALF), HALF)])


def parts_in(copies, r, p_ref, parts, rel, other, row, first=0):
    count = FIELDS - first
    copies.start(parts.at[4 * r + rel, pl.ds(first, count)], p_ref.at[r, pl.ds(first, count)])
    copies.start(other.at[pl.ds(row + first, count)], p_ref.at[1 - r, pl.ds(first, count)])


def piece_out(r, z_ref, q_ref, own, away):
    for half, dst in ((r, own), (1 - r, away)):
        for z in range(2):
            dst[HALF * z:HALF * z + HALF, :] = z_ref[z, pl.ds(pl.multiple_of(HALF * half, HALF), HALF), :]
        dst[2 * HALF:, :] = q_ref[half, :PUSHED, :]


def moves_out(moves, wave, *items):
    for ref, slot in items:
        moves.start(ref.at[pl.ds(0, N)], wave.at[pl.ds(slot * N, N)])


def near_kernel(meta, wave, parts, near, table, d_ref, q_ref, f3, p2, tab, *rest):
    work, sems = rest[:-1], rest[-1]
    r = meta[0]
    copies = Copies(sems)
    field_in(copies, r, f3, wave, N * (4 * r + 1), near, 0)
    parts_in(copies, r, p2, parts, 2, near, N)
    copies.start(table, tab)
    copies.wait()
    step(f3, p2, p2, tab, d_ref, *work)
    q_ref[...] = p2[...]


def first_kernel(meta, q2, wave, parts, swap, table, q_ref, own, away, f2, p1, pushed, z, tab, *rest):
    work, sems = rest[:-1], rest[-1]
    r = meta[0]
    copies = Copies(sems)
    field_in(copies, r, f2, wave, N * 4 * r, swap, 0)
    parts_in(copies, r, p1, parts, 1, swap, N + FIELDS)
    copies.start(table, tab)
    copies.wait()
    step(f2, p1, p1, tab, z, *work)
    q_ref[...] = p1[...]
    step(z, q2, pushed, tab, f2, *work)
    piece_out(r, f2, pushed, own, away)


def second_kernel(meta, q1, parts, swap, chain, ahead, table, d_ref, q_ref, to_back, own, away,
                  f0, f1, p0, pm, pushed, z, tab, *rest):
    work, sems = rest[:-1], rest[-1]
    r = meta[0]
    copies = Copies(sems)
    field_in(copies, r, f0, ahead, 0, chain, 0)
    copies.start(ahead.at[pl.ds(2 * N, FIELDS)], pm.at[r])
    copies.start(chain.at[pl.ds(2 * N, FIELDS)], pm.at[1 - r])
    copies.start(table, tab)
    field_in(copies, r, f1, ahead, N, chain, N)
    parts_in(copies, r, p0, parts, 0, swap, N)
    copies.wait()

    @pl.when(meta[1] == 1)
    def _():
        f1[...] = jnp.zeros_like(f1)

    step(f0, pm, to_back, tab, d_ref, *work)
    step(f1, p0, p0, tab, z, *work)
    q_ref[...] = p0[...]
    step(z, q1, pushed, tab, f1, *work)
    piece_out(r, f1, pushed, own, away)


def third_kernel(meta, d_ref, q0, own_a, own_b, back_a, table, own, away, wave, f0, pushed, z, tab, *rest):
    work, sems = rest[:-1], rest[-1]
    r = meta[0]
    copies, moves = Copies(sems), Copies(sems)
    moves.used = 2
    copies.start(d_ref, f0)
    copies.start(table, tab)
    moves_out(moves, wave, (own_a, 4 * r + 2), (own_b, 4 * r + 1), (back_a, 6 - 4 * r))
    copies.wait()

    @pl.when(meta[1] == 1)
    def _():
        f0[...] = jnp.zeros_like(f0)

    step(f0, q0, pushed, tab, z, *work)
    piece_out(r, z, pushed, own, away)
    moves.wait()


def fourth_kernel(meta, d_ref, parts, swap, from_back, own_c, table, wave_in, own, away, wave,
                  p3, pushed, z, tab, *rest):
    work, sems = rest[:-1], rest[-1]
    r = meta[0]
    copies, moves = Copies(sems), Copies(sems)
    moves.used = 8
    parts_in(copies, r, p3, parts, 3, swap, N + 2 * FIELDS, PUSHED)
    copies.start(from_back, p3.at[:, pl.ds(0, PUSHED)])
    copies.start(table, tab)
    moves_out(moves, wave, (own_c, 4 * r))
    copies.wait()
    step(d_ref, p3, pushed, tab, z, *work)
    piece_out(r, z, pushed, own, away)
    moves.wait()


def late_kernel(meta, back_b, back_c, own_d, wave_in, wave, sems):
    r = meta[0]
    moves = Copies(sems)
    moves_out(moves, wave, (back_b, 5 - 4 * r), (back_c, 4 - 4 * r), (own_d, 4 * r + 3))
    moves.wait()


def final_kernel(meta, *refs):
    pieces, (wave, phase, energy), (packed, sems) = refs[:8], refs[9:12], refs[12:]
    r = meta[0]
    moves, copies = Copies(sems), Copies(sems)
    copies.used = 4
    own, other = 4 * r, 4 - 4 * r
    for base, group in ((own, pieces[:4]), (other, pieces[4:])):
        for ref, slot in zip(group, (2, 1, 0, 3)):
            copies.start(ref.at[pl.ds(N, PUSHED)], packed.at[base + slot])
    moves_out(moves, wave, (pieces[7], other + 3))
    copies.wait()
    for s in range(8):
        for k in range(ROWS):
            phase[s:s + 1, N * k:N * k + N] = packed[s, k:k + 1, :]
            energy[s:s + 1, N * k:N * k + N] = packed[s, ROWS + k:ROWS + k + 1, :]
    moves.wait()


def body(wavefront, particle_phase, particle_energy, row_offset, row_cell, col_cell):
    table = jnp.asarray(tables())
    r = lax.axis_index("row")
    nt = lax.axis_size("tm")
    both = ("tm", "row")
    swap = [(i, i ^ 1) for i in range(2 * nt)]
    chain = [(i, (i + 1) % (2 * nt)) for i in range(2 * nt)]
    ahead = [(i, (i + 2) % (2 * nt) if i % 2 == 0 else i) for i in range(2 * nt)]
    back = [(j, i) for i, j in chain]
    meta = jnp.stack([r, (lax.axis_index(both) == 0).astype(jnp.int32)]).astype(jnp.int32)
    wave = wavefront.reshape(8 * N, N)
    unit = 1 << 33

    full, field = (2, FIELDS, N), (2, N, N)
    pieces = [(PIECE, N), (PIECE, N)]
    parts, to_near, to_swap, to_chain, to_ahead = call(
        pack_kernel, [(8, FIELDS, N), (N + FIELDS, N), (N + 3 * FIELDS, N), (2 * N + FIELDS, N), (2 * N + FIELDS, N)],
        [VM] * 5, [pltpu.VMEM((3, 8, PART), F32), pltpu.VMEM((2, 8, PART), jnp.int32)],
        16, [SM] + [HB] * 6, 1 << 20, vmem=61000 << 10,
    )(meta, wave, particle_phase, particle_energy, row_offset, row_cell, col_cell)
    f_ahead = lax.ppermute(to_ahead, both, ahead)
    f_near = lax.ppermute(to_near, both, swap)
    f_swap = lax.ppermute(to_swap, both, swap)
    f_chain = lax.ppermute(to_chain, both, chain)

    d3, q2 = call(
        near_kernel, [field, full], [VM, VM], [FIELD, PARTS, TABLE] + WORK, 8, [SM] + [ANY] * 4, unit, vmem=59000 << 10,
    )(meta, wave, parts, f_near, table)
    q1, own_a, away_a = call(
        first_kernel, [full] + pieces, [VM] * 3, [FIELD, PARTS, PUSH, FIELD, TABLE] + WORK, 8,
        [SM, VM] + [ANY] * 4, 2 * unit,
    )(meta, q2, wave, parts, f_swap, table)
    back_a = lax.ppermute(away_a, both, swap)
    d0, q0, to_back, own_b, away_b = call(
        second_kernel, [field, full, (2, PUSHED, N)] + pieces, [VM] * 5,
        [FIELD, FIELD, PARTS, PARTS, PUSH, FIELD, TABLE] + WORK, 16, [SM, VM] + [ANY] * 5, 3 * unit,
    )(meta, q1, parts, f_swap, f_chain, f_ahead, table)
    from_back = lax.ppermute(to_back, both, back)
    back_b = lax.ppermute(away_b, both, swap)
    own_c, away_c, wave = call(
        third_kernel, pieces + [(8 * N, N)], [VM, VM, ANY],
        [FIELD, PUSH, FIELD, TABLE] + WORK, 8, [SM, ANY, VM] + [ANY] * 4, unit,
    )(meta, d0, q0, own_a, own_b, back_a, table)
    back_c = lax.ppermute(away_c, both, swap)
    own_d, away_d, wave = call(
        fourth_kernel, pieces + [(8 * N, N)], [VM, VM, ANY],
        [PARTS, PUSH, FIELD, TABLE] + WORK, 12, [SM, VM] + [ANY] * 6, 2 * unit, {7: 2},
    )(meta, d3, parts, f_swap, from_back, own_c, table, wave)
    back_d = lax.ppermute(away_d, both, swap)
    wave, = call(
        late_kernel, [(8 * N, N)], [ANY], [], 4, [SM] + [ANY] * 4, 1 << 20, {4: 0},
    )(meta, back_b, back_c, own_d, wave)
    wave, phase, energy = call(
        final_kernel, [(8 * N, N), (8, PART), (8, PART)], [HB, VM, VM],
        [pltpu.VMEM((8, PUSHED, N), F32)], 16, [SM] + [ANY] * 8 + [HB], 1 << 20, {9: 0},
    )(meta, own_a, own_b, own_c, own_d, back_a, back_b, back_c, back_d, wave)
    return wave.reshape(8, 2, HALF, N), phase, energy


def solution(mesh):
    P = jax.sharding.PartitionSpec
    wide, flat = P("tm", None, "row", None), P("tm", "row")
    return jax.shard_map(body, mesh=mesh, in_specs=(wide,) + (flat,) * 5,
                         out_specs=(wide, flat, flat), check_vma=False)
```

```python
import math

import jax
import jax.numpy as jnp
import ml_dtypes
import numpy as np
from jax import lax
from jax.experimental import pallas as pl
from jax.experimental.pallas import tpu as pltpu

BF = jnp.bfloat16
F32 = jnp.float32
F8 = jnp.float8_e5m2
UP = 1024.0
DOWN = 1.0 / UP
N = 256
HALF = 128
PART = 2048
ROWS = PART // N
WIN = 144
FIELDS = 5 * ROWS
PUSHED = 2 * ROWS
PIECE = 2 * HALF + PUSHED


def split_np(m):
    hi = m.astype(ml_dtypes.bfloat16)
    return hi, (m - hi.astype(np.float64)).astype(ml_dtypes.bfloat16)


def tables():
    k = np.arange(N)
    m = np.where(k < N // 2, k, k - N).astype(np.float64)
    h = np.exp(-1j * np.pi / N * m * m)
    dft = np.exp(-2j * np.pi / N * (k[:, None] * k[None, :] % N))
    a = (np.conj(dft) / N) @ (h[:, None] * dft)
    c0, c1 = a[:HALF, :HALF], a[:HALF, HALF:]
    both = [0.5 * (c0 + c1), 0.5 * (c0 - c1)]
    right = np.stack([np.block([[b.real, b.imag], [-b.imag, b.real]]) for b in both])
    left = np.stack([np.block([[b.real, -b.imag], [b.imag, b.real]]) for b in both])
    return np.stack(split_np(np.stack([right, left])))


def sincos(x):
    n = jnp.round(x * (1.0 / math.pi))
    r = x - n * 3.140625
    r = r - n * 9.670257568359375e-4
    r = r - n * 6.277114152908325e-07
    half = n * 0.5
    sign = 1.0 - 4.0 * (half - jnp.floor(half))
    y = r * r
    s = -2.3889859e-08
    for c in (2.7525562e-06, -1.98408740e-04, 8.33333310e-03, -1.66666667e-01):
        s = s * y + c
    s = r + r * y * s
    c = 2.08767570e-09 - 1.1470746e-11 * y
    for d in (-2.75573192e-07, 2.48015873e-05, -1.38888889e-03, 4.16666667e-02, -0.5, 1.0):
        c = c * y + d
    return s * sign, c * sign


def hilo(x):
    hi = x.astype(BF)
    return hi, (x - hi.astype(F32)).astype(BF)


def mm(a, b):
    return jnp.dot(a, b, preferred_element_type=F32)


def step(f_ref, p_ref, q_ref, tab, out_ref, c_ref, w_ref, s_ref, sr_ref, x_ref, samp_ref, c8_ref, sr8_ref, ready=None):
    iota_c = (lax.broadcasted_iota(jnp.int32, (16, 16, N), 0) * 16
              + lax.broadcasted_iota(jnp.int32, (16, 16, N), 1)).astype(F32).astype(BF)
    one = jnp.ones((16, N), BF)
    zero = jnp.zeros((16, N), BF)
    down = jnp.full((16, N), DOWN, BF)
    iota_r = lax.broadcasted_iota(jnp.int32, (WIN, N), 0).astype(F32)
    for h in range(2):
        off = p_ref[h, 2 * ROWS:3 * ROWS]
        lower = 0.5 - off
        upper = 0.5 + off
        w_ref[0] = 0.5 * lower * lower
        w_ref[1] = 0.75 - off * off
        w_ref[2] = 0.5 * upper * upper
        win0 = 0 if h == 0 else N - WIN
        field = f_ref[:, win0:win0 + WIN, :].reshape(2 * WIN, N)
        hi = field.astype(BF)
        lo = ((field - hi.astype(F32)) * UP).astype(F8)
        for k in range(ROWS):
            col = jnp.broadcast_to(p_ref[h, 4 * ROWS + k:4 * ROWS + k + 1, :], (16, N)).astype(BF)
            hot = jnp.where(iota_c == col[None], one[None], zero[None]).reshape(N, N)
            c_ref[h, :, N * k:N * k + N] = hot
            hot8 = jnp.where(iota_c == col[None], down[None], zero[None]).reshape(N, N).astype(F8)
            c8_ref[h, :, N * k:N * k + N] = hot8
            g = mm(hi, hot) + mm(lo, hot8)
            at = p_ref[h, 3 * ROWS + k:3 * ROWS + k + 1, :] - float(win0)
            w = jnp.where(iota_r == at, w_ref[1, k:k + 1, :],
                          jnp.where(iota_r == at - 1.0, w_ref[0, k:k + 1, :],
                                    jnp.where(iota_r == at + 1.0, w_ref[2, k:k + 1, :], 0.0)))
            samp_ref[0, k:k + 1, :] = jnp.sum(w * g[:WIN], 0, keepdims=True)
            samp_ref[1, k:k + 1, :] = jnp.sum(w * g[WIN:], 0, keepdims=True)
        phase = p_ref[h, :ROWS]
        sine, cosine = sincos(phase)
        energy = p_ref[h, ROWS:2 * ROWS] - 0.5 * (samp_ref[0] * cosine - samp_ref[1] * sine)
        phase = phase + energy
        q_ref[h, :ROWS] = phase
        q_ref[h, ROWS:2 * ROWS] = energy
        sine, cosine = sincos(phase)
        for z, v in ((0, cosine), (1, -sine)):
            vh = v.astype(BF).astype(F32)
            s_ref[2 * z] = vh
            s_ref[2 * z + 1] = v - vh
        for k in range(ROWS):
            at = jnp.broadcast_to(p_ref[h, 3 * ROWS + k:3 * ROWS + k + 1, :] - float(HALF * h), (16, N)).astype(BF)
            here = iota_c[:8] == at[None]
            for z in range(2):
                value = jnp.broadcast_to(s_ref[2 * z, k:k + 1, :], (16, N)).astype(BF)
                sr_ref[HALF * z:HALF * z + HALF, N * k:N * k + N] = jnp.where(here, value[None], zero[None]).reshape(HALF, N)
                value = jnp.broadcast_to(s_ref[2 * z + 1, k:k + 1, :] * UP, (16, N)).astype(BF)
                sr8_ref[HALF * z:HALF * z + HALF, N * k:N * k + N] = jnp.where(here, value[None], zero[None]).reshape(HALF, N).astype(F8)
        d = lax.dot_general(sr_ref[...], c_ref[h], (((1,), (1,)), ((), ())), preferred_element_type=F32)
        d = d + lax.dot_general(sr8_ref[...], c8_ref[h], (((1,), (1,)), ((), ())), preferred_element_type=F32)
        for z in range(2):
            x_ref[HALF * h:HALF * h + HALF, N * z:N * z + N] = (
                f_ref[z, HALF * h:HALF * h + HALF, :]
                + d[HALF * z:HALF * z + HALF])
    if ready is not None:
        ready.wait()
    quads = [[], []]
    for z in range(2):
        top = x_ref[:HALF, N * z:N * z + N]
        low = x_ref[HALF:, N * z:N * z + N]
        rows = jnp.concatenate([top + low, top - low], 0)
        quads[0].append(rows[:, :HALF] + rows[:, HALF:])
        quads[1].append(rows[:, :HALF] - rows[:, HALF:])
    turned = []
    for e in range(2):
        xh, xl = hilo(jnp.concatenate(quads[e], 1))
        turned.append(mm(xh, tab[0, 0, e]) + mm(xl, tab[0, 0, e]) + mm(xh, tab[1, 0, e]))
    halves = []
    for e in range(2):
        rows = slice(HALF * e, HALF * e + HALF)
        y = jnp.concatenate([jnp.concatenate([turned[0][rows, :HALF], turned[1][rows, :HALF]], 1),
                             jnp.concatenate([turned[0][rows, HALF:], turned[1][rows, HALF:]], 1)], 0)
        yh, yl = hilo(y)
        halves.append(mm(tab[0, 1, e], yh) + mm(tab[0, 1, e], yl) + mm(tab[1, 1, e], yh))
    for e, rows in enumerate((halves[0] + halves[1], halves[0] - halves[1])):
        left, right = rows[:, :HALF], rows[:, HALF:]
        out = jnp.concatenate([left + right, left - right], 1)
        out_ref[0, HALF * e:HALF * e + HALF] = out[:HALF]
        out_ref[1, HALF * e:HALF * e + HALF] = out[HALF:]


WORK = [pltpu.VMEM((2, N, PART), BF), pltpu.VMEM((3, ROWS, N), F32), pltpu.VMEM((4, ROWS, N), F32),
        pltpu.VMEM((N, PART), BF), pltpu.VMEM((N, 2 * N), F32), pltpu.VMEM((2, ROWS, N), F32),
        pltpu.VMEM((2, N, PART), F8), pltpu.VMEM((N, PART), F8)]
FIELD = pltpu.VMEM((2, N, N), F32)
PARTS = pltpu.VMEM((2, FIELDS, N), F32)
TABLE = pltpu.VMEM((2, 2, 2, N, N), BF)
PUSH = pltpu.VMEM((2, PUSHED, N), F32)
ANY = pl.BlockSpec(memory_space=pl.ANY)
VM = pl.BlockSpec(memory_space=pltpu.VMEM)
SM = pl.BlockSpec(memory_space=pltpu.SMEM)
HB = pl.BlockSpec(memory_space=pltpu.HBM)


class Copies:
    def __init__(self, sems):
        self.sems = sems
        self.used = 0
        self.open = []

    def start(self, src, dst):
        copy = pltpu.make_async_copy(src, dst, self.sems.at[self.used])
        self.used += 1
        copy.start()
        self.open.append(copy)

    def wait(self):
        for copy in self.open:
            copy.wait()
        self.open = []


def call(kernel, outs, out_specs, scratch, copies, in_specs, flops, aliases={}, vmem=40 << 20):
    return pl.pallas_call(
        kernel, out_shape=[jax.ShapeDtypeStruct(s, F32) for s in outs], in_specs=in_specs, out_specs=out_specs,
        scratch_shapes=scratch + [pltpu.SemaphoreType.DMA((copies,))],
        input_output_aliases=aliases, cost_estimate=pl.CostEstimate(flops=flops, bytes_accessed=4 << 20, transcendentals=0),
        compiler_params=pltpu.CompilerParams(vmem_limit_bytes=vmem))


def pack_kernel(meta, wave, *refs):
    sources, (all_ref, near_ref, swap_ref, chain_ref, ahead_ref), (floats, ints, sems) = refs[:5], refs[5:10], refs[10:]
    r = meta[0]
    loads, copies = Copies(sems), Copies(sems)
    copies.used = 5
    for a, src in enumerate(sources):
        loads.start(src, floats.at[a] if a < 3 else ints.at[a - 3])
    copies.start(wave.at[pl.ds(N * (6 - 4 * r), 2 * N)], ahead_ref.at[pl.ds(0, 2 * N)])
    copies.start(wave.at[pl.ds(N * (5 - 4 * r), N)], near_ref.at[pl.ds(0, N)])
    copies.start(wave.at[pl.ds(N * (4 - 4 * r), N)], swap_ref.at[pl.ds(0, N)])
    copies.start(wave.at[pl.ds(N * (2 + 4 * r), 2 * N)], chain_ref.at[pl.ds(0, 2 * N)])
    loads.wait()
    for a in range(5):
        src = floats.at[a] if a < 3 else ints.at[a - 3]
        for s in range(8):
            for k in range(ROWS):
                all_ref[s, a * ROWS + k:a * ROWS + k + 1, :] = src[s:s + 1, N * k:N * k + N].astype(F32)
    near_ref[N:, :] = all_ref[6 - 4 * r]
    for i, rel in enumerate((0, 1, 3)):
        swap_ref[N + FIELDS * i:N + FIELDS * i + FIELDS, :] = all_ref[4 - 4 * r + rel]
    chain_ref[2 * N:, :] = all_ref[3 + 4 * r]
    ahead_ref[2 * N:, :] = all_ref[7 - 4 * r]
    copies.wait()


def field_in(copies, r, f_ref, own, own_row, other, other_row):
    for z in range(2):
        copies.start(own.at[pl.ds(own_row + HALF * z, HALF)], f_ref.at[z, pl.ds(pl.multiple_of(HALF * r, HALF), HALF)])
        copies.start(other.at[pl.ds(other_row + HALF * z, HALF)],
                     f_ref.at[z, pl.ds(pl.multiple_of(HALF - HALF * r, HALF), HALF)])


def parts_in(copies, r, p_ref, parts, rel, other, row, first=0):
    count = FIELDS - first
    copies.start(parts.at[4 * r + rel, pl.ds(first, count)], p_ref.at[r, pl.ds(first, count)])
    copies.start(other.at[pl.ds(row + first, count)], p_ref.at[1 - r, pl.ds(first, count)])


def piece_out(r, z_ref, q_ref, own, away):
    for half, dst in ((r, own), (1 - r, away)):
        for z in range(2):
            dst[HALF * z:HALF * z + HALF, :] = z_ref[z, pl.ds(pl.multiple_of(HALF * half, HALF), HALF), :]
        dst[2 * HALF:, :] = q_ref[half, :PUSHED, :]


def moves_out(moves, wave, *items):
    for ref, slot in items:
        moves.start(ref.at[pl.ds(0, N)], wave.at[pl.ds(slot * N, N)])


def near_kernel(meta, wave, parts, near, table, d_ref, q_ref, f3, p2, tab, *rest):
    work, sems = rest[:-1], rest[-1]
    r = meta[0]
    copies, later = Copies(sems), Copies(sems)
    later.used = 7
    field_in(copies, r, f3, wave, N * (4 * r + 1), near, 0)
    parts_in(copies, r, p2, parts, 2, near, N)
    later.start(table, tab)
    copies.wait()
    step(f3, p2, p2, tab, d_ref, *work, ready=later)
    q_ref[...] = p2[...]


def first_kernel(meta, q2, wave, parts, swap, table, q_ref, own, away, f2, p1, pushed, z, tab, *rest):
    work, sems = rest[:-1], rest[-1]
    r = meta[0]
    copies, later = Copies(sems), Copies(sems)
    later.used = 7
    field_in(copies, r, f2, wave, N * 4 * r, swap, 0)
    parts_in(copies, r, p1, parts, 1, swap, N + FIELDS)
    later.start(table, tab)
    copies.wait()
    step(f2, p1, p1, tab, z, *work, ready=later)
    q_ref[...] = p1[...]
    step(z, q2, pushed, tab, f2, *work)
    piece_out(r, f2, pushed, own, away)


def second_kernel(meta, q1, parts, swap, chain, ahead, relay, table, d_ref, q_ref, to_back, own, away,
                  f0, f1, p0, pm, pushed, z, tab, *rest):
    work, sems = rest[:-1], rest[-1]
    r = meta[0]
    copies, later = Copies(sems), Copies(sems)
    later.used = 23
    field_in(copies, r, f0, ahead, 0, chain, 0)
    copies.start(ahead.at[pl.ds(2 * N, FIELDS)], pm.at[r])
    copies.start(chain.at[pl.ds(2 * N, FIELDS)], pm.at[1 - r])
    later.start(table, tab)
    field_in(copies, r, f1, ahead, N, chain, N)
    parts_in(copies, r, p0, parts, 0, swap, N)
    copies.wait()

    @pl.when(meta[2] == 1)
    def _():
        again = Copies(sems)
        again.used = 15
        for i, f in enumerate((f0, f1)):
            for z in range(2):
                again.start(relay.at[pl.ds(N * i + HALF * z, HALF)],
                            f.at[z, pl.ds(pl.multiple_of(HALF * r, HALF), HALF)])
        again.start(relay.at[pl.ds(2 * N, FIELDS)], pm.at[r])
        again.wait()

    @pl.when(meta[1] == 1)
    def _():
        f1[...] = jnp.zeros_like(f1)

    step(f0, pm, to_back, tab, d_ref, *work, ready=later)
    step(f1, p0, p0, tab, z, *work)
    q_ref[...] = p0[...]
    step(z, q1, pushed, tab, f1, *work)
    piece_out(r, f1, pushed, own, away)


def third_kernel(meta, d_ref, q0, own_a, own_b, back_a, table, own, away, wave, f0, pushed, z, tab, *rest):
    work, sems = rest[:-1], rest[-1]
    r = meta[0]
    copies, moves, later = Copies(sems), Copies(sems), Copies(sems)
    later.used = 11
    moves.used = 2
    copies.start(d_ref, f0)
    later.start(table, tab)
    moves_out(moves, wave, (own_a, 4 * r + 2), (own_b, 4 * r + 1), (back_a, 6 - 4 * r))
    copies.wait()

    @pl.when(meta[1] == 1)
    def _():
        f0[...] = jnp.zeros_like(f0)

    step(f0, q0, pushed, tab, z, *work, ready=later)
    piece_out(r, z, pushed, own, away)
    moves.wait()


def fourth_kernel(meta, d_ref, parts, swap, from_back, own_c, table, wave_in, own, away, wave,
                  p3, pushed, z, tab, *rest):
    work, sems = rest[:-1], rest[-1]
    r = meta[0]
    copies, moves, later = Copies(sems), Copies(sems), Copies(sems)
    later.used = 11
    moves.used = 8
    parts_in(copies, r, p3, parts, 3, swap, N + 2 * FIELDS, PUSHED)
    copies.start(from_back, p3.at[:, pl.ds(0, PUSHED)])
    later.start(table, tab)
    moves_out(moves, wave, (own_c, 4 * r))
    copies.wait()
    step(d_ref, p3, pushed, tab, z, *work, ready=later)
    piece_out(r, z, pushed, own, away)
    moves.wait()


def late_kernel(meta, back_b, back_c, own_d, wave_in, wave, sems):
    r = meta[0]
    moves = Copies(sems)
    moves_out(moves, wave, (back_b, 5 - 4 * r), (back_c, 4 - 4 * r), (own_d, 4 * r + 3))
    moves.wait()


def final_kernel(meta, *refs):
    pieces, (wave, phase, energy), (packed, sems) = refs[:8], refs[9:12], refs[12:]
    r = meta[0]
    moves, copies = Copies(sems), Copies(sems)
    copies.used = 4
    own, other = 4 * r, 4 - 4 * r
    for base, group in ((own, pieces[:4]), (other, pieces[4:])):
        for ref, slot in zip(group, (2, 1, 0, 3)):
            copies.start(ref.at[pl.ds(N, PUSHED)], packed.at[base + slot])
    moves_out(moves, wave, (pieces[7], other + 3))
    copies.wait()
    for s in range(8):
        for k in range(ROWS):
            phase[s:s + 1, N * k:N * k + N] = packed[s, k:k + 1, :]
            energy[s:s + 1, N * k:N * k + N] = packed[s, ROWS + k:ROWS + k + 1, :]
    moves.wait()


def body(wavefront, particle_phase, particle_energy, row_offset, row_cell, col_cell):
    table = jnp.asarray(tables())
    r = lax.axis_index("row")
    nt = lax.axis_size("tm")
    both = ("tm", "row")
    swap = [(i, i ^ 1) for i in range(2 * nt)]
    chain = [(i, (i + 1) % (2 * nt)) for i in range(2 * nt)]
    far = [2 * t for t in range(nt) if (t + 1) % (nt // 2) == 0]
    ahead = [(i, i + 2 if i % 2 == 0 else i) for i in range(2 * nt) if i not in far]
    around = [(i, (i + 3) % (2 * nt)) for i in far]
    onward = [(j, j - 1) for i, j in around]
    back = [(j, i) for i, j in chain]
    index = lax.axis_index(both)
    meta = jnp.stack([r, (index == 0).astype(jnp.int32), (index % nt == 0).astype(jnp.int32)]).astype(jnp.int32)
    wave = wavefront.reshape(8 * N, N)
    unit = 1 << 33

    full, field = (2, FIELDS, N), (2, N, N)
    pieces = [(PIECE, N), (PIECE, N)]
    parts, to_near, to_swap, to_chain, to_ahead = call(
        pack_kernel, [(8, FIELDS, N), (N + FIELDS, N), (N + 3 * FIELDS, N), (2 * N + FIELDS, N), (2 * N + FIELDS, N)],
        [VM] * 5, [pltpu.VMEM((3, 8, PART), F32), pltpu.VMEM((2, 8, PART), jnp.int32)],
        16, [SM] + [HB] * 6, 1 << 20, vmem=61000 << 10,
    )(meta, wave, particle_phase, particle_energy, row_offset, row_cell, col_cell)
    f_ahead = lax.ppermute(to_ahead, both, ahead)
    f_around = lax.ppermute(to_ahead, both, around)
    f_near = lax.ppermute(to_near, both, swap)
    f_swap = lax.ppermute(to_swap, both, swap)
    f_chain = lax.ppermute(to_chain, both, chain)

    d3, q2 = call(
        near_kernel, [field, full], [VM, VM], [FIELD, PARTS, TABLE] + WORK, 8, [SM] + [ANY] * 4, unit, vmem=59000 << 10,
    )(meta, wave, parts, f_near, table)
    q2, f_around = lax.optimization_barrier((q2, f_around))
    f_relay = lax.ppermute(f_around, both, onward)
    q1, own_a, away_a = call(
        first_kernel, [full] + pieces, [VM] * 3, [FIELD, PARTS, PUSH, FIELD, TABLE] + WORK, 8,
        [SM, VM] + [ANY] * 4, 2 * unit,
    )(meta, q2, wave, parts, f_swap, table)
    back_a = lax.ppermute(away_a, both, swap)
    d0, q0, to_back, own_b, away_b = call(
        second_kernel, [field, full, (2, PUSHED, N)] + pieces, [VM] * 5,
        [FIELD, FIELD, PARTS, PARTS, PUSH, FIELD, TABLE] + WORK, 24, [SM, VM] + [ANY] * 6, 3 * unit,
    )(meta, q1, parts, f_swap, f_chain, f_ahead, f_relay, table)
    from_back = lax.ppermute(to_back, both, back)
    back_b = lax.ppermute(away_b, both, swap)
    own_c, away_c, wave = call(
        third_kernel, pieces + [(8 * N, N)], [VM, VM, ANY],
        [FIELD, PUSH, FIELD, TABLE] + WORK, 12, [SM, ANY, VM] + [ANY] * 4, unit,
    )(meta, d0, q0, own_a, own_b, back_a, table)
    back_c = lax.ppermute(away_c, both, swap)
    own_d, away_d, wave = call(
        fourth_kernel, pieces + [(8 * N, N)], [VM, VM, ANY],
        [PARTS, PUSH, FIELD, TABLE] + WORK, 12, [SM, VM] + [ANY] * 6, 2 * unit, {7: 2},
    )(meta, d3, parts, f_swap, from_back, own_c, table, wave)
    back_d = lax.ppermute(away_d, both, swap)
    wave, = call(
        late_kernel, [(8 * N, N)], [ANY], [], 4, [SM] + [ANY] * 4, 1 << 20, {4: 0},
    )(meta, back_b, back_c, own_d, wave)
    wave, phase, energy = call(
        final_kernel, [(8 * N, N), (8, PART), (8, PART)], [HB, VM, VM],
        [pltpu.VMEM((8, PUSHED, N), F32)], 16, [SM] + [ANY] * 8 + [HB], 1 << 20, {9: 0},
    )(meta, own_a, own_b, own_c, own_d, back_a, back_b, back_c, back_d, wave)
    return wave.reshape(8, 2, HALF, N), phase, energy


def solution(mesh):
    P = jax.sharding.PartitionSpec
    wide, flat = P("tm", None, "row", None), P("tm", "row")
    return jax.shard_map(body, mesh=mesh, in_specs=(wide,) + (flat,) * 5,
                         out_specs=(wide, flat, flat), check_vma=False)
```

```python
import math

import jax
import jax.numpy as jnp
import ml_dtypes
import numpy as np
from jax import lax
from jax.experimental import pallas as pl
from jax.experimental.pallas import tpu as pltpu

BF = jnp.bfloat16
F32 = jnp.float32
F8 = jnp.float8_e5m2
UP = 1024.0
DOWN = 1.0 / UP
N = 256
HALF = 128
PART = 2048
ROWS = PART // N
WIN = 144
FIELDS = 5 * ROWS
PUSHED = 2 * ROWS
PIECE = 2 * HALF + PUSHED
BOTH = ("tm", "row")


def split_np(m):
    hi = m.astype(ml_dtypes.bfloat16)
    return hi, (m - hi.astype(np.float64)).astype(ml_dtypes.bfloat16)


def tables():
    k = np.arange(N)
    m = np.where(k < N // 2, k, k - N).astype(np.float64)
    h = np.exp(-1j * np.pi / N * m * m)
    dft = np.exp(-2j * np.pi / N * (k[:, None] * k[None, :] % N))
    a = (np.conj(dft) / N) @ (h[:, None] * dft)
    c0, c1 = a[:HALF, :HALF], a[:HALF, HALF:]
    both = [0.5 * (c0 + c1), 0.5 * (c0 - c1)]
    right = np.stack([np.block([[b.real, b.imag], [-b.imag, b.real]]) for b in both])
    left = np.stack([np.block([[b.real, -b.imag], [b.imag, b.real]]) for b in both])
    return np.stack(split_np(np.stack([right, left])))


def sincos(x):
    n = jnp.round(x * (1.0 / math.pi))
    r = x - n * 3.140625
    r = r - n * 9.670257568359375e-4
    r = r - n * 6.277114152908325e-07
    half = n * 0.5
    sign = 1.0 - 4.0 * (half - jnp.floor(half))
    y = r * r
    s = -2.3889859e-08
    for c in (2.7525562e-06, -1.98408740e-04, 8.33333310e-03, -1.66666667e-01):
        s = s * y + c
    s = r + r * y * s
    c = 2.08767570e-09 - 1.1470746e-11 * y
    for d in (-2.75573192e-07, 2.48015873e-05, -1.38888889e-03, 4.16666667e-02, -0.5, 1.0):
        c = c * y + d
    return s * sign, c * sign


def hilo(x):
    hi = x.astype(BF)
    return hi, (x - hi.astype(F32)).astype(BF)


def mm(a, b):
    return jnp.dot(a, b, preferred_element_type=F32)


def step(f_ref, p_ref, q_ref, tab, out_ref, c_ref, w_ref, s_ref, sr_ref, x_ref, samp_ref, c8_ref, sr8_ref, ready=None):
    iota_c = (lax.broadcasted_iota(jnp.int32, (16, 16, N), 0) * 16
              + lax.broadcasted_iota(jnp.int32, (16, 16, N), 1)).astype(F32).astype(BF)
    one = jnp.ones((16, N), BF)
    zero = jnp.zeros((16, N), BF)
    down = jnp.full((16, N), DOWN, BF)
    iota_r = lax.broadcasted_iota(jnp.int32, (WIN, N), 0).astype(F32)
    for h in range(2):
        off = p_ref[h, 2 * ROWS:3 * ROWS]
        lower = 0.5 - off
        upper = 0.5 + off
        w_ref[0] = 0.5 * lower * lower
        w_ref[1] = 0.75 - off * off
        w_ref[2] = 0.5 * upper * upper
        win0 = 0 if h == 0 else N - WIN
        field = f_ref[:, win0:win0 + WIN, :].reshape(2 * WIN, N)
        hi = field.astype(BF)
        lo = ((field - hi.astype(F32)) * UP).astype(F8)
        for k in range(ROWS):
            col = jnp.broadcast_to(p_ref[h, 4 * ROWS + k:4 * ROWS + k + 1, :], (16, N)).astype(BF)
            hot = jnp.where(iota_c == col[None], one[None], zero[None]).reshape(N, N)
            c_ref[h, :, N * k:N * k + N] = hot
            hot8 = jnp.where(iota_c == col[None], down[None], zero[None]).reshape(N, N).astype(F8)
            c8_ref[h, :, N * k:N * k + N] = hot8
            g = mm(hi, hot) + mm(lo, hot8)
            at = p_ref[h, 3 * ROWS + k:3 * ROWS + k + 1, :] - float(win0)
            w = jnp.where(iota_r == at, w_ref[1, k:k + 1, :],
                          jnp.where(iota_r == at - 1.0, w_ref[0, k:k + 1, :],
                                    jnp.where(iota_r == at + 1.0, w_ref[2, k:k + 1, :], 0.0)))
            samp_ref[0, k:k + 1, :] = jnp.sum(w * g[:WIN], 0, keepdims=True)
            samp_ref[1, k:k + 1, :] = jnp.sum(w * g[WIN:], 0, keepdims=True)
        phase = p_ref[h, :ROWS]
        sine, cosine = sincos(phase)
        energy = p_ref[h, ROWS:2 * ROWS] - 0.5 * (samp_ref[0] * cosine - samp_ref[1] * sine)
        phase = phase + energy
        q_ref[h, :ROWS] = phase
        q_ref[h, ROWS:2 * ROWS] = energy
        sine, cosine = sincos(phase)
        for z, v in ((0, cosine), (1, -sine)):
            vh = v.astype(BF).astype(F32)
            s_ref[2 * z] = vh
            s_ref[2 * z + 1] = v - vh
        for k in range(ROWS):
            at = jnp.broadcast_to(p_ref[h, 3 * ROWS + k:3 * ROWS + k + 1, :] - float(HALF * h), (16, N)).astype(BF)
            here = iota_c[:8] == at[None]
            for z in range(2):
                value = jnp.broadcast_to(s_ref[2 * z, k:k + 1, :], (16, N)).astype(BF)
                sr_ref[HALF * z:HALF * z + HALF, N * k:N * k + N] = jnp.where(here, value[None], zero[None]).reshape(HALF, N)
                value = jnp.broadcast_to(s_ref[2 * z + 1, k:k + 1, :] * UP, (16, N)).astype(BF)
                sr8_ref[HALF * z:HALF * z + HALF, N * k:N * k + N] = jnp.where(here, value[None], zero[None]).reshape(HALF, N).astype(F8)
        d = lax.dot_general(sr_ref[...], c_ref[h], (((1,), (1,)), ((), ())), preferred_element_type=F32)
        d = d + lax.dot_general(sr8_ref[...], c8_ref[h], (((1,), (1,)), ((), ())), preferred_element_type=F32)
        for z in range(2):
            x_ref[HALF * h:HALF * h + HALF, N * z:N * z + N] = (
                f_ref[z, HALF * h:HALF * h + HALF, :]
                + d[HALF * z:HALF * z + HALF])
    if ready is not None:
        ready.wait()
    quads = [[], []]
    for z in range(2):
        top = x_ref[:HALF, N * z:N * z + N]
        low = x_ref[HALF:, N * z:N * z + N]
        rows = jnp.concatenate([top + low, top - low], 0)
        quads[0].append(rows[:, :HALF] + rows[:, HALF:])
        quads[1].append(rows[:, :HALF] - rows[:, HALF:])
    turned = []
    for e in range(2):
        xh, xl = hilo(jnp.concatenate(quads[e], 1))
        t = mm(jnp.concatenate([xh, xl], 0), tab[0, 0, e])
        turned.append(t[:N] + t[N:] + mm(xh, tab[1, 0, e]))
    halves = []
    for e in range(2):
        rows = slice(HALF * e, HALF * e + HALF)
        y = jnp.concatenate([jnp.concatenate([turned[0][rows, :HALF], turned[1][rows, :HALF]], 1),
                             jnp.concatenate([turned[0][rows, HALF:], turned[1][rows, HALF:]], 1)], 0)
        yh, yl = hilo(y)
        t = mm(jnp.concatenate([tab[0, 1, e], tab[1, 1, e]], 0), yh)
        halves.append(t[:N] + t[N:] + mm(tab[0, 1, e], yl))
    for e, rows in enumerate((halves[0] + halves[1], halves[0] - halves[1])):
        left, right = rows[:, :HALF], rows[:, HALF:]
        out = jnp.concatenate([left + right, left - right], 1)
        out_ref[0, HALF * e:HALF * e + HALF] = out[:HALF]
        out_ref[1, HALF * e:HALF * e + HALF] = out[HALF:]


WORK = [pltpu.VMEM((2, N, PART), BF), pltpu.VMEM((3, ROWS, N), F32), pltpu.VMEM((4, ROWS, N), F32),
        pltpu.VMEM((N, PART), BF), pltpu.VMEM((N, 2 * N), F32), pltpu.VMEM((2, ROWS, N), F32),
        pltpu.VMEM((2, N, PART), F8), pltpu.VMEM((N, PART), F8)]
FIELD = pltpu.VMEM((2, N, N), F32)
PARTS = pltpu.VMEM((2, FIELDS, N), F32)
TABLE = pltpu.VMEM((2, 2, 2, N, N), BF)
PUSH = pltpu.VMEM((2, PUSHED, N), F32)
ANY = pl.BlockSpec(memory_space=pl.ANY)
VM = pl.BlockSpec(memory_space=pltpu.VMEM)
HB = pl.BlockSpec(memory_space=pltpu.HBM)


class Copies:
    def __init__(self, sems):
        self.sems = sems
        self.used = 0
        self.open = []

    def start(self, src, dst):
        copy = pltpu.make_async_copy(src, dst, self.sems.at[self.used])
        self.used += 1
        copy.start()
        self.open.append(copy)

    def wait(self):
        for copy in self.open:
            copy.wait()
        self.open = []


def call(kernel, outs, out_specs, scratch, copies, in_specs, flops, aliases={}, vmem=40 << 20):
    return pl.pallas_call(
        kernel, out_shape=[jax.ShapeDtypeStruct(s, F32) for s in outs], in_specs=in_specs, out_specs=out_specs,
        scratch_shapes=scratch + [pltpu.SemaphoreType.DMA((copies,))],
        input_output_aliases=aliases, cost_estimate=pl.CostEstimate(flops=flops, bytes_accessed=4 << 20, transcendentals=0),
        compiler_params=pltpu.CompilerParams(vmem_limit_bytes=vmem))


def load_all(copies, sources, floats, ints):
    for a, src in enumerate(sources):
        copies.start(src, floats.at[a] if a < 3 else ints.at[a - 3])


def pack_slice(floats, ints, index, dst, row):
    for a in range(5):
        src = floats.at[a] if a < 3 else ints.at[a - 3]
        for k in range(ROWS):
            at = row + a * ROWS + k
            dst[at:at + 1, :] = src[pl.ds(index, 1), N * k:N * k + N].astype(F32)


def early_pack_kernel(wave, *refs):
    sources, (near_ref, ahead_ref), (floats, ints, sems) = refs[:5], refs[5:7], refs[7:]
    r = lax.axis_index("row")
    loads, copies = Copies(sems), Copies(sems)
    copies.used = 5
    load_all(loads, sources, floats, ints)
    copies.start(wave.at[pl.ds(N * (5 - 4 * r), N)], near_ref.at[pl.ds(0, N)])
    copies.start(wave.at[pl.ds(N * (6 - 4 * r), 2 * N)], ahead_ref.at[pl.ds(0, 2 * N)])
    loads.wait()
    pack_slice(floats, ints, 6 - 4 * r, near_ref, N)
    pack_slice(floats, ints, 7 - 4 * r, ahead_ref, 2 * N)
    copies.wait()


def pack_kernel(near, wave, *refs):
    sources, (all_ref, swap_ref, chain_ref), (floats, ints, sems) = refs[:5], refs[5:8], refs[8:]
    r = lax.axis_index("row")
    loads, copies = Copies(sems), Copies(sems)
    copies.used = 5
    load_all(loads, sources, floats, ints)
    copies.start(wave.at[pl.ds(N * (4 - 4 * r), N)], swap_ref.at[pl.ds(0, N)])
    copies.start(wave.at[pl.ds(N * (2 + 4 * r), 2 * N)], chain_ref.at[pl.ds(0, 2 * N)])
    loads.wait()
    for s in range(8):
        pack_slice(floats, ints, s, all_ref.at[s], 0)
    for i, rel in enumerate((0, 1, 3)):
        swap_ref[N + FIELDS * i:N + FIELDS * i + FIELDS, :] = all_ref[4 - 4 * r + rel]
    chain_ref[2 * N:, :] = all_ref[3 + 4 * r]
    copies.wait()


def field_in(copies, r, f_ref, own, own_row, other, other_row):
    for z in range(2):
        copies.start(own.at[pl.ds(own_row + HALF * z, HALF)], f_ref.at[z, pl.ds(pl.multiple_of(HALF * r, HALF), HALF)])
        copies.start(other.at[pl.ds(other_row + HALF * z, HALF)],
                     f_ref.at[z, pl.ds(pl.multiple_of(HALF - HALF * r, HALF), HALF)])


def parts_in(copies, r, p_ref, parts, rel, other, row, first=0):
    count = FIELDS - first
    copies.start(parts.at[4 * r + rel, pl.ds(first, count)], p_ref.at[r, pl.ds(first, count)])
    copies.start(other.at[pl.ds(row + first, count)], p_ref.at[1 - r, pl.ds(first, count)])


def piece_out(r, z_ref, q_ref, own, away):
    for half, dst in ((r, own), (1 - r, away)):
        for z in range(2):
            dst[HALF * z:HALF * z + HALF, :] = z_ref[z, pl.ds(pl.multiple_of(HALF * half, HALF), HALF), :]
        dst[2 * HALF:, :] = q_ref[half, :PUSHED, :]


def moves_out(moves, wave, *items):
    for ref, slot in items:
        moves.start(ref.at[pl.ds(0, N)], wave.at[pl.ds(slot * N, N)])


def near_kernel(wave, parts, near, table, d_ref, q_ref, f3, p2, tab, *rest):
    work, sems = rest[:-1], rest[-1]
    r = lax.axis_index("row")
    copies, later = Copies(sems), Copies(sems)
    later.used = 7
    field_in(copies, r, f3, wave, N * (4 * r + 1), near, 0)
    parts_in(copies, r, p2, parts, 2, near, N)
    later.start(table, tab)
    copies.wait()
    step(f3, p2, p2, tab, d_ref, *work, ready=later)
    q_ref[...] = p2[...]


def first_kernel(q2, wave, parts, swap, table, q_ref, own, away, f2, p1, pushed, z, tab, *rest):
    work, sems = rest[:-1], rest[-1]
    r = lax.axis_index("row")
    copies, later = Copies(sems), Copies(sems)
    later.used = 7
    field_in(copies, r, f2, wave, N * 4 * r, swap, 0)
    parts_in(copies, r, p1, parts, 1, swap, N + FIELDS)
    later.start(table, tab)
    copies.wait()
    step(f2, p1, p1, tab, z, *work, ready=later)
    q_ref[...] = p1[...]
    step(z, q2, pushed, tab, f2, *work)
    piece_out(r, f2, pushed, own, away)


def second_kernel(q1, parts, swap, chain, ahead, relay, table, d_ref, q_ref, to_back, own, away,
                  f0, f1, p0, pm, pushed, z, tab, *rest):
    work, sems = rest[:-1], rest[-1]
    r = lax.axis_index("row")
    copies, later = Copies(sems), Copies(sems)
    later.used = 23
    field_in(copies, r, f0, ahead, 0, chain, 0)
    copies.start(ahead.at[pl.ds(2 * N, FIELDS)], pm.at[r])
    copies.start(chain.at[pl.ds(2 * N, FIELDS)], pm.at[1 - r])
    later.start(table, tab)
    field_in(copies, r, f1, ahead, N, chain, N)
    parts_in(copies, r, p0, parts, 0, swap, N)
    copies.wait()

    @pl.when((r == 0) & (lax.rem(lax.axis_index("tm"), lax.axis_size("tm") // 2) == 0))
    def _():
        again = Copies(sems)
        again.used = 15
        for i, f in enumerate((f0, f1)):
            for z in range(2):
                again.start(relay.at[pl.ds(N * i + HALF * z, HALF)],
                            f.at[z, pl.ds(pl.multiple_of(HALF * r, HALF), HALF)])
        again.start(relay.at[pl.ds(2 * N, FIELDS)], pm.at[r])
        again.wait()

    @pl.when((r == 0) & (lax.axis_index("tm") == 0))
    def _():
        f1[...] = jnp.zeros_like(f1)

    step(f0, pm, to_back, tab, d_ref, *work, ready=later)
    step(f1, p0, p0, tab, z, *work)
    q_ref[...] = p0[...]
    step(z, q1, pushed, tab, f1, *work)
    piece_out(r, f1, pushed, own, away)


def third_kernel(d_ref, q0, own_a, own_b, back_a, table, own, away, wave, f0, pushed, z, tab, *rest):
    work, sems = rest[:-1], rest[-1]
    r = lax.axis_index("row")
    copies, moves, later = Copies(sems), Copies(sems), Copies(sems)
    later.used = 11
    moves.used = 2
    copies.start(d_ref, f0)
    later.start(table, tab)
    moves_out(moves, wave, (own_a, 4 * r + 2), (own_b, 4 * r + 1), (back_a, 6 - 4 * r))
    copies.wait()

    @pl.when((r == 0) & (lax.axis_index("tm") == 0))
    def _():
        f0[...] = jnp.zeros_like(f0)

    step(f0, q0, pushed, tab, z, *work, ready=later)
    piece_out(r, z, pushed, own, away)
    moves.wait()


def fourth_kernel(d_ref, parts, swap, from_back, own_c, table, wave_in, own, away, wave,
                  p3, pushed, z, tab, *rest):
    work, sems = rest[:-1], rest[-1]
    r = lax.axis_index("row")
    copies, moves, later = Copies(sems), Copies(sems), Copies(sems)
    later.used = 11
    moves.used = 8
    parts_in(copies, r, p3, parts, 3, swap, N + 2 * FIELDS, PUSHED)
    copies.start(from_back, p3.at[:, pl.ds(0, PUSHED)])
    later.start(table, tab)
    moves_out(moves, wave, (own_c, 4 * r))
    copies.wait()
    step(d_ref, p3, pushed, tab, z, *work, ready=later)
    piece_out(r, z, pushed, own, away)
    moves.wait()


def late_kernel(own_a, own_b, own_c, own_d, back_a, back_b, back_c, wave_in, wave, phase, energy, packed, sems):
    r = lax.axis_index("row")
    own, other = 4 * r, 4 - 4 * r
    moves, copies = Copies(sems), Copies(sems)
    copies.used = 4
    for base, group in ((own, (own_a, own_b, own_c, own_d)), (other, (back_a, back_b, back_c, back_c))):
        for ref, slot in zip(group, (2, 1, 0, 3)):
            copies.start(ref.at[pl.ds(N, PUSHED)], packed.at[base + slot])
    moves_out(moves, wave, (back_b, other + 1), (back_c, other), (own_d, own + 3))
    copies.wait()
    for s in range(8):
        for k in range(ROWS):
            phase[s:s + 1, N * k:N * k + N] = packed[s, k:k + 1, :]
            energy[s:s + 1, N * k:N * k + N] = packed[s, ROWS + k:ROWS + k + 1, :]
    moves.wait()


def final_kernel(back_d, wave_in, phase_in, energy_in, wave, phase, energy, sems):
    r = lax.axis_index("row")
    last = 7 - 4 * r
    moves = Copies(sems)
    moves_out(moves, wave, (back_d, last))
    phase[...] = phase_in[...]
    energy[...] = energy_in[...]
    for k in range(ROWS):
        phase[pl.ds(last, 1), N * k:N * k + N] = back_d[N + k:N + k + 1, :]
        energy[pl.ds(last, 1), N * k:N * k + N] = back_d[N + ROWS + k:N + ROWS + k + 1, :]
    moves.wait()


def body(wavefront, particle_phase, particle_energy, row_offset, row_cell, col_cell):
    table = jnp.asarray(tables())
    r = lax.axis_index("row")
    nt = lax.axis_size("tm")
    both = BOTH
    swap = [(i, i ^ 1) for i in range(2 * nt)]
    chain = [(i, (i + 1) % (2 * nt)) for i in range(2 * nt)]
    far = [2 * t for t in range(nt) if (t + 1) % (nt // 2) == 0]
    ahead = [(i, i + 2 if i % 2 == 0 else i) for i in range(2 * nt) if i not in far]
    around = [(i, (i + 3) % (2 * nt)) for i in far]
    onward = [(j, j - 1) for i, j in around]
    back = [(j, i) for i, j in chain]
    wave = wavefront.reshape(8 * N, N)
    unit = 1 << 33

    full, field = (2, FIELDS, N), (2, N, N)
    pieces = [(PIECE, N), (PIECE, N)]
    raw = (wave, particle_phase, particle_energy, row_offset, row_cell, col_cell)
    stage = [pltpu.VMEM((3, 8, PART), F32), pltpu.VMEM((2, 8, PART), jnp.int32)]
    to_near, to_ahead = call(
        early_pack_kernel, [(N + FIELDS, N), (2 * N + FIELDS, N)], [VM, VM], stage, 8, [HB] * 6, 1 << 20,
        vmem=61000 << 10,
    )(*raw)
    f_near = lax.ppermute(to_near, both, swap)
    f_around = lax.ppermute(to_ahead, both, around)
    parts, to_swap, to_chain = call(
        pack_kernel, [(8, FIELDS, N), (N + 3 * FIELDS, N), (2 * N + FIELDS, N)],
        [VM] * 3, stage, 8, [ANY] + [HB] * 6, 4 * unit, vmem=61000 << 10,
    )(to_near, *raw)
    f_swap = lax.ppermute(to_swap, both, swap)
    to_ahead, to_chain = lax.optimization_barrier((to_ahead, to_chain))
    f_ahead = lax.ppermute(to_ahead, both, ahead)
    f_chain = lax.ppermute(to_chain, both, chain)
    f_near, f_around = lax.optimization_barrier((f_near, f_around))
    f_relay = lax.ppermute(f_around, both, onward)

    d3, q2 = call(
        near_kernel, [field, full], [VM, VM], [FIELD, PARTS, TABLE] + WORK, 8, [ANY] * 4, unit, vmem=50000 << 10,
    )(wave, parts, f_near, table)
    q1, own_a, away_a = call(
        first_kernel, [full] + pieces, [VM] * 3, [FIELD, PARTS, PUSH, FIELD, TABLE] + WORK, 8,
        [VM] + [ANY] * 4, 2 * unit,
    )(q2, wave, parts, f_swap, table)
    back_a = lax.ppermute(away_a, both, swap)
    d0, q0, to_back, own_b, away_b = call(
        second_kernel, [field, full, (2, PUSHED, N)] + pieces, [VM] * 5,
        [FIELD, FIELD, PARTS, PARTS, PUSH, FIELD, TABLE] + WORK, 24, [VM] + [ANY] * 6, 3 * unit,
    )(q1, parts, f_swap, f_chain, f_ahead, f_relay, table)
    from_back = lax.ppermute(to_back, both, back)
    back_b = lax.ppermute(away_b, both, swap)
    own_c, away_c, wave = call(
        third_kernel, pieces + [(8 * N, N)], [VM, VM, ANY],
        [FIELD, PUSH, FIELD, TABLE] + WORK, 12, [ANY, VM] + [ANY] * 4, unit,
    )(d0, q0, own_a, own_b, back_a, table)
    back_c = lax.ppermute(away_c, both, swap)
    own_d, away_d, wave = call(
        fourth_kernel, pieces + [(8 * N, N)], [VM, VM, ANY],
        [PARTS, PUSH, FIELD, TABLE] + WORK, 12, [VM] + [ANY] * 6, 2 * unit, {6: 2},
    )(d3, parts, f_swap, from_back, own_c, table, wave)
    back_d = lax.ppermute(away_d, both, swap)
    particles = [(8, PART), (8, PART)]
    wave, phase, energy = call(
        late_kernel, [(8 * N, N)] + particles, [ANY, VM, VM], [pltpu.VMEM((8, PUSHED, N), F32)], 16,
        [ANY] * 8, 1 << 20, {7: 0},
    )(own_a, own_b, own_c, own_d, back_a, back_b, back_c, wave)
    wave, phase, energy = call(
        final_kernel, [(8 * N, N)] + particles, [HB, VM, VM], [], 4, [VM, HB, VM, VM], 1 << 20, {1: 0},
    )(back_d, wave, phase, energy)
    return wave.reshape(8, 2, HALF, N), phase, energy


def solution(mesh):
    P = jax.sharding.PartitionSpec
    wide, flat = P("tm", None, "row", None), P("tm", "row")
    return jax.shard_map(body, mesh=mesh, in_specs=(wide,) + (flat,) * 5,
                         out_specs=(wide, flat, flat), check_vma=False)
```

```python
import math

import jax
import jax.numpy as jnp
import ml_dtypes
import numpy as np
from jax import lax
from jax.experimental import pallas as pl
from jax.experimental.pallas import tpu as pltpu

BF = jnp.bfloat16
F32 = jnp.float32
F8 = jnp.float8_e5m2
UP = 1024.0
DOWN = 1.0 / UP
N = 256
HALF = 128
PART = 2048
ROWS = PART // N
WIN = 144
FIELDS = 5 * ROWS
PUSHED = 2 * ROWS
PIECE = 2 * HALF + PUSHED
BOTH = ("tm", "row")


def split_np(m):
    hi = m.astype(ml_dtypes.bfloat16)
    return hi, (m - hi.astype(np.float64)).astype(ml_dtypes.bfloat16)


def tables():
    k = np.arange(N)
    m = np.where(k < N // 2, k, k - N).astype(np.float64)
    h = np.exp(-1j * np.pi / N * m * m)
    dft = np.exp(-2j * np.pi / N * (k[:, None] * k[None, :] % N))
    a = (np.conj(dft) / N) @ (h[:, None] * dft)
    c0, c1 = a[:HALF, :HALF], a[:HALF, HALF:]
    both = [0.5 * (c0 + c1), 0.5 * (c0 - c1)]
    right = np.stack([np.block([[b.real, b.imag], [-b.imag, b.real]]) for b in both])
    left = np.stack([np.block([[b.real, -b.imag], [b.imag, b.real]]) for b in both])
    return np.stack(split_np(np.stack([right, left])))


def sincos(x):
    n = jnp.round(x * (1.0 / math.pi))
    r = x - n * 3.140625
    r = r - n * 9.670257568359375e-4
    r = r - n * 6.277114152908325e-07
    half = n * 0.5
    sign = 1.0 - 4.0 * (half - jnp.floor(half))
    y = r * r
    s = -2.3889859e-08
    for c in (2.7525562e-06, -1.98408740e-04, 8.33333310e-03, -1.66666667e-01):
        s = s * y + c
    s = r + r * y * s
    c = 2.08767570e-09 - 1.1470746e-11 * y
    for d in (-2.75573192e-07, 2.48015873e-05, -1.38888889e-03, 4.16666667e-02, -0.5, 1.0):
        c = c * y + d
    return s * sign, c * sign


def hilo(x):
    hi = x.astype(BF)
    return hi, (x - hi.astype(F32)).astype(BF)


def mm(a, b):
    return jnp.dot(a, b, preferred_element_type=F32)


def step(f_ref, p_ref, q_ref, tab, out_ref, c_ref, w_ref, s_ref, sr_ref, x_ref, samp_ref, c8_ref, sr8_ref, ready=None):
    iota_c = (lax.broadcasted_iota(jnp.int32, (16, 16, N), 0) * 16
              + lax.broadcasted_iota(jnp.int32, (16, 16, N), 1)).astype(F32).astype(BF)
    one = jnp.ones((16, N), BF)
    zero = jnp.zeros((16, N), BF)
    down = jnp.full((16, N), DOWN, BF)
    iota_r = lax.broadcasted_iota(jnp.int32, (WIN, N), 0).astype(F32)
    for h in range(2):
        off = p_ref[h, 2 * ROWS:3 * ROWS]
        lower = 0.5 - off
        upper = 0.5 + off
        w_ref[0] = 0.5 * lower * lower
        w_ref[1] = 0.75 - off * off
        w_ref[2] = 0.5 * upper * upper
        win0 = 0 if h == 0 else N - WIN
        field = f_ref[:, win0:win0 + WIN, :].reshape(2 * WIN, N)
        hi = field.astype(BF)
        lo = ((field - hi.astype(F32)) * UP).astype(F8)
        for k in range(ROWS):
            col = jnp.broadcast_to(p_ref[h, 4 * ROWS + k:4 * ROWS + k + 1, :], (16, N)).astype(BF)
            hot = jnp.where(iota_c == col[None], one[None], zero[None]).reshape(N, N)
            c_ref[h, :, N * k:N * k + N] = hot
            hot8 = jnp.where(iota_c == col[None], down[None], zero[None]).reshape(N, N).astype(F8)
            c8_ref[h, :, N * k:N * k + N] = hot8
            g = mm(hi, hot) + mm(lo, hot8)
            at = p_ref[h, 3 * ROWS + k:3 * ROWS + k + 1, :] - float(win0)
            w = jnp.where(iota_r == at, w_ref[1, k:k + 1, :],
                          jnp.where(iota_r == at - 1.0, w_ref[0, k:k + 1, :],
                                    jnp.where(iota_r == at + 1.0, w_ref[2, k:k + 1, :], 0.0)))
            samp_ref[0, k:k + 1, :] = jnp.sum(w * g[:WIN], 0, keepdims=True)
            samp_ref[1, k:k + 1, :] = jnp.sum(w * g[WIN:], 0, keepdims=True)
        phase = p_ref[h, :ROWS]
        sine, cosine = sincos(phase)
        energy = p_ref[h, ROWS:2 * ROWS] - 0.5 * (samp_ref[0] * cosine - samp_ref[1] * sine)
        phase = phase + energy
        q_ref[h, :ROWS] = phase
        q_ref[h, ROWS:2 * ROWS] = energy
        sine, cosine = sincos(phase)
        for z, v in ((0, cosine), (1, -sine)):
            vh = v.astype(BF).astype(F32)
            s_ref[2 * z] = vh
            s_ref[2 * z + 1] = v - vh
        for k in range(ROWS):
            at = jnp.broadcast_to(p_ref[h, 3 * ROWS + k:3 * ROWS + k + 1, :] - float(HALF * h), (16, N)).astype(BF)
            here = iota_c[:8] == at[None]
            for z in range(2):
                value = jnp.broadcast_to(s_ref[2 * z, k:k + 1, :], (16, N)).astype(BF)
                sr_ref[HALF * z:HALF * z + HALF, N * k:N * k + N] = jnp.where(here, value[None], zero[None]).reshape(HALF, N)
                value = jnp.broadcast_to(s_ref[2 * z + 1, k:k + 1, :] * UP, (16, N)).astype(BF)
                sr8_ref[HALF * z:HALF * z + HALF, N * k:N * k + N] = jnp.where(here, value[None], zero[None]).reshape(HALF, N).astype(F8)
        d = lax.dot_general(sr_ref[...], c_ref[h], (((1,), (1,)), ((), ())), preferred_element_type=F32)
        d = d + lax.dot_general(sr8_ref[...], c8_ref[h], (((1,), (1,)), ((), ())), preferred_element_type=F32)
        for z in range(2):
            x_ref[HALF * h:HALF * h + HALF, N * z:N * z + N] = (
                f_ref[z, HALF * h:HALF * h + HALF, :]
                + d[HALF * z:HALF * z + HALF])
    if ready is not None:
        ready.wait()
    quads = [[], []]
    for z in range(2):
        top = x_ref[:HALF, N * z:N * z + N]
        low = x_ref[HALF:, N * z:N * z + N]
        rows = jnp.concatenate([top + low, top - low], 0)
        quads[0].append(rows[:, :HALF] + rows[:, HALF:])
        quads[1].append(rows[:, :HALF] - rows[:, HALF:])
    turned = []
    for e in range(2):
        xh, xl = hilo(jnp.concatenate(quads[e], 1))
        t = mm(jnp.concatenate([xh, xl], 0), tab[0, 0, e])
        turned.append(t[:N] + t[N:] + mm(xh, tab[1, 0, e]))
    halves = []
    for e in range(2):
        rows = slice(HALF * e, HALF * e + HALF)
        y = jnp.concatenate([jnp.concatenate([turned[0][rows, :HALF], turned[1][rows, :HALF]], 1),
                             jnp.concatenate([turned[0][rows, HALF:], turned[1][rows, HALF:]], 1)], 0)
        yh, yl = hilo(y)
        t = mm(jnp.concatenate([tab[0, 1, e], tab[1, 1, e]], 0), yh)
        halves.append(t[:N] + t[N:] + mm(tab[0, 1, e], yl))
    for e, rows in enumerate((halves[0] + halves[1], halves[0] - halves[1])):
        left, right = rows[:, :HALF], rows[:, HALF:]
        out = jnp.concatenate([left + right, left - right], 1)
        out_ref[0, HALF * e:HALF * e + HALF] = out[:HALF]
        out_ref[1, HALF * e:HALF * e + HALF] = out[HALF:]


WORK = [pltpu.VMEM((2, N, PART), BF), pltpu.VMEM((3, ROWS, N), F32), pltpu.VMEM((4, ROWS, N), F32),
        pltpu.VMEM((N, PART), BF), pltpu.VMEM((N, 2 * N), F32), pltpu.VMEM((2, ROWS, N), F32),
        pltpu.VMEM((2, N, PART), F8), pltpu.VMEM((N, PART), F8)]
FIELD = pltpu.VMEM((2, N, N), F32)
PARTS = pltpu.VMEM((2, FIELDS, N), F32)
TABLE = pltpu.VMEM((2, 2, 2, N, N), BF)
PUSH = pltpu.VMEM((2, PUSHED, N), F32)
ANY = pl.BlockSpec(memory_space=pl.ANY)
VM = pl.BlockSpec(memory_space=pltpu.VMEM)
HB = pl.BlockSpec(memory_space=pltpu.HBM)


class Copies:
    def __init__(self, sems):
        self.sems = sems
        self.used = 0
        self.open = []

    def start(self, src, dst):
        copy = pltpu.make_async_copy(src, dst, self.sems.at[self.used])
        self.used += 1
        copy.start()
        self.open.append(copy)

    def wait(self):
        for copy in self.open:
            copy.wait()
        self.open = []


def call(kernel, outs, out_specs, scratch, copies, in_specs, flops, aliases={}, vmem=40 << 20):
    return pl.pallas_call(
        kernel, out_shape=[jax.ShapeDtypeStruct(s, F32) for s in outs], in_specs=in_specs, out_specs=out_specs,
        scratch_shapes=scratch + [pltpu.SemaphoreType.DMA((copies,))],
        input_output_aliases=aliases, cost_estimate=pl.CostEstimate(flops=flops, bytes_accessed=4 << 20, transcendentals=0),
        compiler_params=pltpu.CompilerParams(vmem_limit_bytes=vmem))


def load_all(copies, sources, floats, ints):
    for a, src in enumerate(sources):
        copies.start(src, floats.at[a] if a < 3 else ints.at[a - 3])


def pack_slice(floats, ints, index, dst, row):
    for a in range(5):
        src = floats.at[a] if a < 3 else ints.at[a - 3]
        for k in range(ROWS):
            at = row + a * ROWS + k
            dst[at:at + 1, :] = src[pl.ds(index, 1), N * k:N * k + N].astype(F32)


def early_pack_kernel(wave, *refs):
    sources, (near_ref, ahead_ref, mine_ref), (floats, ints, sems) = refs[:5], refs[5:8], refs[8:]
    r = lax.axis_index("row")
    loads, copies = Copies(sems), Copies(sems)
    copies.used = 5
    load_all(loads, sources, floats, ints)
    copies.start(wave.at[pl.ds(N * (5 - 4 * r), N)], near_ref.at[pl.ds(0, N)])
    copies.start(wave.at[pl.ds(N * (6 - 4 * r), 2 * N)], ahead_ref.at[pl.ds(0, 2 * N)])
    loads.wait()
    pack_slice(floats, ints, 6 - 4 * r, near_ref, N)
    pack_slice(floats, ints, 2 + 4 * r, mine_ref, 0)
    pack_slice(floats, ints, 7 - 4 * r, ahead_ref, 2 * N)
    copies.wait()


def pack_kernel(near, wave, *refs):
    sources, (all_ref, swap_ref, chain_ref), (floats, ints, sems) = refs[:5], refs[5:8], refs[8:]
    r = lax.axis_index("row")
    loads, copies = Copies(sems), Copies(sems)
    copies.used = 5
    load_all(loads, sources, floats, ints)
    copies.start(wave.at[pl.ds(N * (4 - 4 * r), N)], swap_ref.at[pl.ds(0, N)])
    copies.start(wave.at[pl.ds(N * (2 + 4 * r), 2 * N)], chain_ref.at[pl.ds(0, 2 * N)])
    loads.wait()
    for s in range(8):
        pack_slice(floats, ints, s, all_ref.at[s], 0)
    for i, rel in enumerate((0, 1, 3)):
        swap_ref[N + FIELDS * i:N + FIELDS * i + FIELDS, :] = all_ref[4 - 4 * r + rel]
    chain_ref[2 * N:, :] = all_ref[3 + 4 * r]
    copies.wait()


def field_in(copies, r, f_ref, own, own_row, other, other_row):
    for z in range(2):
        copies.start(own.at[pl.ds(own_row + HALF * z, HALF)], f_ref.at[z, pl.ds(pl.multiple_of(HALF * r, HALF), HALF)])
        copies.start(other.at[pl.ds(other_row + HALF * z, HALF)],
                     f_ref.at[z, pl.ds(pl.multiple_of(HALF - HALF * r, HALF), HALF)])


def parts_in(copies, r, p_ref, parts, rel, other, row, first=0):
    count = FIELDS - first
    copies.start(parts.at[4 * r + rel, pl.ds(first, count)], p_ref.at[r, pl.ds(first, count)])
    copies.start(other.at[pl.ds(row + first, count)], p_ref.at[1 - r, pl.ds(first, count)])


def piece_out(r, z_ref, q_ref, own, away):
    for half, dst in ((r, own), (1 - r, away)):
        for z in range(2):
            dst[HALF * z:HALF * z + HALF, :] = z_ref[z, pl.ds(pl.multiple_of(HALF * half, HALF), HALF), :]
        dst[2 * HALF:, :] = q_ref[half, :PUSHED, :]


def moves_out(moves, wave, *items):
    for ref, slot in items:
        moves.start(ref.at[pl.ds(0, N)], wave.at[pl.ds(slot * N, N)])


def near_kernel(wave, mine, near, table, d_ref, q_ref, f3, p2, tab, *rest):
    work, sems = rest[:-1], rest[-1]
    r = lax.axis_index("row")
    copies, later = Copies(sems), Copies(sems)
    later.used = 7
    field_in(copies, r, f3, wave, N * (4 * r + 1), near, 0)
    copies.start(mine, p2.at[r])
    copies.start(near.at[pl.ds(N, FIELDS)], p2.at[1 - r])
    later.start(table, tab)
    copies.wait()
    step(f3, p2, p2, tab, d_ref, *work, ready=later)
    q_ref[...] = p2[...]


def first_kernel(q2, wave, parts, swap, table, q_ref, own, away, f2, p1, pushed, z, tab, *rest):
    work, sems = rest[:-1], rest[-1]
    r = lax.axis_index("row")
    copies, later = Copies(sems), Copies(sems)
    later.used = 7
    field_in(copies, r, f2, wave, N * 4 * r, swap, 0)
    parts_in(copies, r, p1, parts, 1, swap, N + FIELDS)
    later.start(table, tab)
    copies.wait()
    step(f2, p1, p1, tab, z, *work, ready=later)
    q_ref[...] = p1[...]
    step(z, q2, pushed, tab, f2, *work)
    piece_out(r, f2, pushed, own, away)


def second_kernel(q1, parts, swap, chain, ahead, relay, table, d_ref, q_ref, to_back, own, away,
                  f0, f1, p0, pm, pushed, z, tab, *rest):
    work, sems = rest[:-1], rest[-1]
    r = lax.axis_index("row")
    copies, later = Copies(sems), Copies(sems)
    later.used = 23
    field_in(copies, r, f0, ahead, 0, chain, 0)
    copies.start(ahead.at[pl.ds(2 * N, FIELDS)], pm.at[r])
    copies.start(chain.at[pl.ds(2 * N, FIELDS)], pm.at[1 - r])
    later.start(table, tab)
    field_in(copies, r, f1, ahead, N, chain, N)
    parts_in(copies, r, p0, parts, 0, swap, N)
    copies.wait()

    @pl.when((r == 0) & (lax.rem(lax.axis_index("tm"), lax.axis_size("tm") // 2) == 0))
    def _():
        again = Copies(sems)
        again.used = 15
        for i, f in enumerate((f0, f1)):
            for z in range(2):
                again.start(relay.at[pl.ds(N * i + HALF * z, HALF)],
                            f.at[z, pl.ds(pl.multiple_of(HALF * r, HALF), HALF)])
        again.start(relay.at[pl.ds(2 * N, FIELDS)], pm.at[r])
        again.wait()

    @pl.when((r == 0) & (lax.axis_index("tm") == 0))
    def _():
        f1[...] = jnp.zeros_like(f1)

    step(f0, pm, to_back, tab, d_ref, *work, ready=later)
    step(f1, p0, p0, tab, z, *work)
    q_ref[...] = p0[...]
    step(z, q1, pushed, tab, f1, *work)
    piece_out(r, f1, pushed, own, away)


def third_kernel(d_ref, q0, own_a, own_b, back_a, table, own, away, wave, f0, pushed, z, tab, *rest):
    work, sems = rest[:-1], rest[-1]
    r = lax.axis_index("row")
    copies, moves, later = Copies(sems), Copies(sems), Copies(sems)
    later.used = 11
    moves.used = 2
    copies.start(d_ref, f0)
    later.start(table, tab)
    moves_out(moves, wave, (own_a, 4 * r + 2), (own_b, 4 * r + 1), (back_a, 6 - 4 * r))
    copies.wait()

    @pl.when((r == 0) & (lax.axis_index("tm") == 0))
    def _():
        f0[...] = jnp.zeros_like(f0)

    step(f0, q0, pushed, tab, z, *work, ready=later)
    piece_out(r, z, pushed, own, away)
    moves.wait()


def fourth_kernel(d_ref, parts, swap, from_back, own_c, table, wave_in, own, away, wave,
                  p3, pushed, z, tab, *rest):
    work, sems = rest[:-1], rest[-1]
    r = lax.axis_index("row")
    copies, moves, later = Copies(sems), Copies(sems), Copies(sems)
    later.used = 11
    moves.used = 8
    parts_in(copies, r, p3, parts, 3, swap, N + 2 * FIELDS, PUSHED)
    copies.start(from_back, p3.at[:, pl.ds(0, PUSHED)])
    later.start(table, tab)
    moves_out(moves, wave, (own_c, 4 * r))
    copies.wait()
    step(d_ref, p3, pushed, tab, z, *work, ready=later)
    piece_out(r, z, pushed, own, away)
    moves.wait()


def late_kernel(own_a, own_b, own_c, own_d, back_a, back_b, back_c, wave_in, wave, phase, energy, packed, sems):
    r = lax.axis_index("row")
    own, other = 4 * r, 4 - 4 * r
    moves, copies = Copies(sems), Copies(sems)
    copies.used = 4
    for base, group in ((own, (own_a, own_b, own_c, own_d)), (other, (back_a, back_b, back_c, back_c))):
        for ref, slot in zip(group, (2, 1, 0, 3)):
            copies.start(ref.at[pl.ds(N, PUSHED)], packed.at[base + slot])
    moves_out(moves, wave, (back_b, other + 1), (back_c, other), (own_d, own + 3))
    copies.wait()
    for s in range(8):
        for k in range(ROWS):
            phase[s:s + 1, N * k:N * k + N] = packed[s, k:k + 1, :]
            energy[s:s + 1, N * k:N * k + N] = packed[s, ROWS + k:ROWS + k + 1, :]
    moves.wait()


def final_kernel(back_d, wave_in, phase_in, energy_in, wave, phase, energy, sems):
    r = lax.axis_index("row")
    last = 7 - 4 * r
    moves = Copies(sems)
    moves_out(moves, wave, (back_d, last))
    phase[...] = phase_in[...]
    energy[...] = energy_in[...]
    for k in range(ROWS):
        phase[pl.ds(last, 1), N * k:N * k + N] = back_d[N + k:N + k + 1, :]
        energy[pl.ds(last, 1), N * k:N * k + N] = back_d[N + ROWS + k:N + ROWS + k + 1, :]
    moves.wait()


def body(wavefront, particle_phase, particle_energy, row_offset, row_cell, col_cell):
    table = jnp.asarray(tables())
    r = lax.axis_index("row")
    nt = lax.axis_size("tm")
    both = BOTH
    swap = [(i, i ^ 1) for i in range(2 * nt)]
    chain = [(i, (i + 1) % (2 * nt)) for i in range(2 * nt)]
    far = [2 * t for t in range(nt) if (t + 1) % (nt // 2) == 0]
    ahead = [(i, i + 2 if i % 2 == 0 else i) for i in range(2 * nt) if i not in far]
    around = [(i, (i + 3) % (2 * nt)) for i in far]
    onward = [(j, j - 1) for i, j in around]
    back = [(j, i) for i, j in chain]
    wave = wavefront.reshape(8 * N, N)
    unit = 1 << 33

    full, field = (2, FIELDS, N), (2, N, N)
    pieces = [(PIECE, N), (PIECE, N)]
    raw = (wave, particle_phase, particle_energy, row_offset, row_cell, col_cell)
    stage = [pltpu.VMEM((3, 8, PART), F32), pltpu.VMEM((2, 8, PART), jnp.int32)]
    to_near, to_ahead, mine = call(
        early_pack_kernel, [(N + FIELDS, N), (2 * N + FIELDS, N), (FIELDS, N)], [VM] * 3, stage, 8, [HB] * 6, 1 << 20,
        vmem=61000 << 10,
    )(*raw)
    f_near = lax.ppermute(to_near, both, swap)
    f_around = lax.ppermute(to_ahead, both, around)
    parts, to_swap, to_chain = call(
        pack_kernel, [(8, FIELDS, N), (N + 3 * FIELDS, N), (2 * N + FIELDS, N)],
        [VM] * 3, stage, 8, [ANY] + [HB] * 6, 4 * unit, vmem=61000 << 10,
    )(to_near, *raw)
    f_swap = lax.ppermute(to_swap, both, swap)
    to_ahead, to_chain = lax.optimization_barrier((to_ahead, to_chain))
    f_ahead = lax.ppermute(to_ahead, both, ahead)

    d3, q2 = call(
        near_kernel, [field, full], [VM, VM], [FIELD, PARTS, TABLE] + WORK, 8, [ANY] * 4, unit, vmem=50000 << 10,
    )(wave, mine, f_near, table)
    q2, f_around, to_chain = lax.optimization_barrier((q2, f_around, to_chain))
    f_relay = lax.ppermute(f_around, both, onward)
    f_chain = lax.ppermute(to_chain, both, chain)
    q1, own_a, away_a = call(
        first_kernel, [full] + pieces, [VM] * 3, [FIELD, PARTS, PUSH, FIELD, TABLE] + WORK, 8,
        [VM] + [ANY] * 4, 2 * unit,
    )(q2, wave, parts, f_swap, table)
    back_a = lax.ppermute(away_a, both, swap)
    d0, q0, to_back, own_b, away_b = call(
        second_kernel, [field, full, (2, PUSHED, N)] + pieces, [VM] * 5,
        [FIELD, FIELD, PARTS, PARTS, PUSH, FIELD, TABLE] + WORK, 24, [VM] + [ANY] * 6, 3 * unit,
    )(q1, parts, f_swap, f_chain, f_ahead, f_relay, table)
    from_back = lax.ppermute(to_back, both, back)
    back_b = lax.ppermute(away_b, both, swap)
    own_c, away_c, wave = call(
        third_kernel, pieces + [(8 * N, N)], [VM, VM, ANY],
        [FIELD, PUSH, FIELD, TABLE] + WORK, 12, [ANY, VM] + [ANY] * 4, unit,
    )(d0, q0, own_a, own_b, back_a, table)
    back_c = lax.ppermute(away_c, both, swap)
    own_d, away_d, wave = call(
        fourth_kernel, pieces + [(8 * N, N)], [VM, VM, ANY],
        [PARTS, PUSH, FIELD, TABLE] + WORK, 12, [VM] + [ANY] * 6, 2 * unit, {6: 2},
    )(d3, parts, f_swap, from_back, own_c, table, wave)
    back_d = lax.ppermute(away_d, both, swap)
    particles = [(8, PART), (8, PART)]
    wave, phase, energy = call(
        late_kernel, [(8 * N, N)] + particles, [ANY, VM, VM], [pltpu.VMEM((8, PUSHED, N), F32)], 16,
        [ANY] * 8, 1 << 20, {7: 0},
    )(own_a, own_b, own_c, own_d, back_a, back_b, back_c, wave)
    wave, phase, energy = call(
        final_kernel, [(8 * N, N)] + particles, [HB, VM, VM], [], 4, [VM, HB, VM, VM], 1 << 20, {1: 0},
    )(back_d, wave, phase, energy)
    return wave.reshape(8, 2, HALF, N), phase, energy


def solution(mesh):
    P = jax.sharding.PartitionSpec
    wide, flat = P("tm", None, "row", None), P("tm", "row")
    return jax.shard_map(body, mesh=mesh, in_specs=(wide,) + (flat,) * 5,
                         out_specs=(wide, flat, flat), check_vma=False)
```

```python
import math

import jax
import jax.numpy as jnp
import ml_dtypes
import numpy as np
from jax import lax
from jax.experimental import pallas as pl
from jax.experimental.pallas import tpu as pltpu

BF = jnp.bfloat16
F32 = jnp.float32
F8 = jnp.float8_e5m2
UP = 1024.0
DOWN = 1.0 / UP
N = 256
HALF = 128
PART = 2048
ROWS = PART // N
WIN = 144
FIELDS = 5 * ROWS
PUSHED = 2 * ROWS
PIECE = 2 * HALF + PUSHED
BOTH = ("tm", "row")


def split_np(m):
    hi = m.astype(ml_dtypes.bfloat16)
    return hi, (m - hi.astype(np.float64)).astype(ml_dtypes.bfloat16)


def tables():
    k = np.arange(N)
    m = np.where(k < N // 2, k, k - N).astype(np.float64)
    h = np.exp(-1j * np.pi / N * m * m)
    dft = np.exp(-2j * np.pi / N * (k[:, None] * k[None, :] % N))
    a = (np.conj(dft) / N) @ (h[:, None] * dft)
    c0, c1 = a[:HALF, :HALF], a[:HALF, HALF:]
    both = [0.5 * (c0 + c1), 0.5 * (c0 - c1)]
    right = np.stack([np.block([[b.real, b.imag], [-b.imag, b.real]]) for b in both])
    left = np.stack([np.block([[b.real, -b.imag], [b.imag, b.real]]) for b in both])
    return np.stack(split_np(np.stack([right, left])))


def sincos(x):
    n = jnp.round(x * (1.0 / math.pi))
    r = x - n * 3.140625
    r = r - n * 9.670257568359375e-4
    r = r - n * 6.277114152908325e-07
    half = n * 0.5
    sign = 1.0 - 4.0 * (half - jnp.floor(half))
    y = r * r
    s = -2.3889859e-08
    for c in (2.7525562e-06, -1.98408740e-04, 8.33333310e-03, -1.66666667e-01):
        s = s * y + c
    s = r + r * y * s
    c = 2.08767570e-09 - 1.1470746e-11 * y
    for d in (-2.75573192e-07, 2.48015873e-05, -1.38888889e-03, 4.16666667e-02, -0.5, 1.0):
        c = c * y + d
    return s * sign, c * sign


def hilo(x):
    hi = x.astype(BF)
    return hi, (x - hi.astype(F32)).astype(BF)


def mm(a, b):
    return jnp.dot(a, b, preferred_element_type=F32)


def step(f_ref, p_ref, q_ref, tab, out_ref, c_ref, w_ref, s_ref, sr_ref, x_ref, samp_ref, c8_ref, sr8_ref, ready=None):
    iota_c = (lax.broadcasted_iota(jnp.int32, (16, 16, N), 0) * 16
              + lax.broadcasted_iota(jnp.int32, (16, 16, N), 1)).astype(F32).astype(BF)
    one = jnp.ones((16, N), BF)
    zero = jnp.zeros((16, N), BF)
    down = jnp.full((16, N), DOWN, BF)
    iota_r = lax.broadcasted_iota(jnp.int32, (WIN, N), 0).astype(F32)
    for h in range(2):
        off = p_ref[h, 2 * ROWS:3 * ROWS]
        lower = 0.5 - off
        upper = 0.5 + off
        w_ref[0] = 0.5 * lower * lower
        w_ref[1] = 0.75 - off * off
        w_ref[2] = 0.5 * upper * upper
        win0 = 0 if h == 0 else N - WIN
        field = f_ref[:, win0:win0 + WIN, :].reshape(2 * WIN, N)
        hi = field.astype(BF)
        lo = ((field - hi.astype(F32)) * UP).astype(F8)
        for k in range(ROWS):
            col = jnp.broadcast_to(p_ref[h, 4 * ROWS + k:4 * ROWS + k + 1, :], (16, N)).astype(BF)
            hot = jnp.where(iota_c == col[None], one[None], zero[None]).reshape(N, N)
            c_ref[h, :, N * k:N * k + N] = hot
            hot8 = jnp.where(iota_c == col[None], down[None], zero[None]).reshape(N, N).astype(F8)
            c8_ref[h, :, N * k:N * k + N] = hot8
            g = mm(hi, hot) + mm(lo, hot8)
            at = p_ref[h, 3 * ROWS + k:3 * ROWS + k + 1, :] - float(win0)
            w = jnp.where(iota_r == at, w_ref[1, k:k + 1, :],
                          jnp.where(iota_r == at - 1.0, w_ref[0, k:k + 1, :],
                                    jnp.where(iota_r == at + 1.0, w_ref[2, k:k + 1, :], 0.0)))
            samp_ref[0, k:k + 1, :] = jnp.sum(w * g[:WIN], 0, keepdims=True)
            samp_ref[1, k:k + 1, :] = jnp.sum(w * g[WIN:], 0, keepdims=True)
        phase = p_ref[h, :ROWS]
        sine, cosine = sincos(phase)
        energy = p_ref[h, ROWS:2 * ROWS] - 0.5 * (samp_ref[0] * cosine - samp_ref[1] * sine)
        phase = phase + energy
        q_ref[h, :ROWS] = phase
        q_ref[h, ROWS:2 * ROWS] = energy
        sine, cosine = sincos(phase)
        for z, v in ((0, cosine), (1, -sine)):
            vh = v.astype(BF).astype(F32)
            s_ref[2 * z] = vh
            s_ref[2 * z + 1] = v - vh
        for k in range(ROWS):
            at = jnp.broadcast_to(p_ref[h, 3 * ROWS + k:3 * ROWS + k + 1, :] - float(HALF * h), (16, N)).astype(BF)
            here = iota_c[:8] == at[None]
            for z in range(2):
                value = jnp.broadcast_to(s_ref[2 * z, k:k + 1, :], (16, N)).astype(BF)
                sr_ref[HALF * z:HALF * z + HALF, N * k:N * k + N] = jnp.where(here, value[None], zero[None]).reshape(HALF, N)
                value = jnp.broadcast_to(s_ref[2 * z + 1, k:k + 1, :] * UP, (16, N)).astype(BF)
                sr8_ref[HALF * z:HALF * z + HALF, N * k:N * k + N] = jnp.where(here, value[None], zero[None]).reshape(HALF, N).astype(F8)
        d = lax.dot_general(sr_ref[...], c_ref[h], (((1,), (1,)), ((), ())), preferred_element_type=F32)
        d = d + lax.dot_general(sr8_ref[...], c8_ref[h], (((1,), (1,)), ((), ())), preferred_element_type=F32)
        for z in range(2):
            x_ref[HALF * h:HALF * h + HALF, N * z:N * z + N] = (
                f_ref[z, HALF * h:HALF * h + HALF, :]
                + d[HALF * z:HALF * z + HALF])
    if ready is not None:
        ready.wait()
    quads = [[], []]
    for z in range(2):
        top = x_ref[:HALF, N * z:N * z + N]
        low = x_ref[HALF:, N * z:N * z + N]
        rows = jnp.concatenate([top + low, top - low], 0)
        quads[0].append(rows[:, :HALF] + rows[:, HALF:])
        quads[1].append(rows[:, :HALF] - rows[:, HALF:])
    turned = []
    for e in range(2):
        xh, xl = hilo(jnp.concatenate(quads[e], 1))
        t = mm(jnp.concatenate([xh, xl], 0), tab[0, 0, e])
        turned.append(t[:N] + t[N:] + mm(xh, tab[1, 0, e]))
    halves = []
    for e in range(2):
        rows = slice(HALF * e, HALF * e + HALF)
        y = jnp.concatenate([jnp.concatenate([turned[0][rows, :HALF], turned[1][rows, :HALF]], 1),
                             jnp.concatenate([turned[0][rows, HALF:], turned[1][rows, HALF:]], 1)], 0)
        yh, yl = hilo(y)
        t = mm(jnp.concatenate([tab[0, 1, e], tab[1, 1, e]], 0), yh)
        halves.append(t[:N] + t[N:] + mm(tab[0, 1, e], yl))
    for e, rows in enumerate((halves[0] + halves[1], halves[0] - halves[1])):
        left, right = rows[:, :HALF], rows[:, HALF:]
        out = jnp.concatenate([left + right, left - right], 1)
        out_ref[0, HALF * e:HALF * e + HALF] = out[:HALF]
        out_ref[1, HALF * e:HALF * e + HALF] = out[HALF:]


WORK = [pltpu.VMEM((2, N, PART), BF), pltpu.VMEM((3, ROWS, N), F32), pltpu.VMEM((4, ROWS, N), F32),
        pltpu.VMEM((N, PART), BF), pltpu.VMEM((N, 2 * N), F32), pltpu.VMEM((2, ROWS, N), F32),
        pltpu.VMEM((2, N, PART), F8), pltpu.VMEM((N, PART), F8)]
FIELD = pltpu.VMEM((2, N, N), F32)
PARTS = pltpu.VMEM((2, FIELDS, N), F32)
TABLE = pltpu.VMEM((2, 2, 2, N, N), BF)
PUSH = pltpu.VMEM((2, PUSHED, N), F32)
ANY = pl.BlockSpec(memory_space=pl.ANY)
VM = pl.BlockSpec(memory_space=pltpu.VMEM)
HB = pl.BlockSpec(memory_space=pltpu.HBM)


class Copies:
    def __init__(self, sems):
        self.sems = sems
        self.used = 0
        self.open = []

    def start(self, src, dst):
        copy = pltpu.make_async_copy(src, dst, self.sems.at[self.used])
        self.used += 1
        copy.start()
        self.open.append(copy)

    def wait(self):
        for copy in self.open:
            copy.wait()
        self.open = []


def call(kernel, outs, out_specs, scratch, copies, in_specs, flops, aliases={}, vmem=40 << 20):
    return pl.pallas_call(
        kernel, out_shape=[jax.ShapeDtypeStruct(s, F32) for s in outs], in_specs=in_specs, out_specs=out_specs,
        scratch_shapes=scratch + [pltpu.SemaphoreType.DMA((copies,))],
        input_output_aliases=aliases, cost_estimate=pl.CostEstimate(flops=flops, bytes_accessed=4 << 20, transcendentals=0),
        compiler_params=pltpu.CompilerParams(vmem_limit_bytes=vmem))


def load_all(copies, sources, floats, ints):
    for a, src in enumerate(sources):
        copies.start(src, floats.at[a] if a < 3 else ints.at[a - 3])


def pack_slice(floats, ints, index, dst, row):
    for a in range(5):
        src = floats.at[a] if a < 3 else ints.at[a - 3]
        for k in range(ROWS):
            at = row + a * ROWS + k
            dst[at:at + 1, :] = src[pl.ds(index, 1), N * k:N * k + N].astype(F32)


def early_pack_kernel(wave, *refs):
    sources, (near_ref, ahead_ref, next_ref, mine_ref), (floats, ints, sems) = refs[:5], refs[5:9], refs[9:]
    r = lax.axis_index("row")
    loads, copies = Copies(sems), Copies(sems)
    copies.used = 5
    load_all(loads, sources, floats, ints)
    copies.start(wave.at[pl.ds(N * (5 - 4 * r), N)], near_ref.at[pl.ds(0, N)])
    copies.start(wave.at[pl.ds(N * (6 - 4 * r), N)], ahead_ref.at[pl.ds(0, N)])
    copies.start(wave.at[pl.ds(N * (7 - 4 * r), N)], next_ref)
    loads.wait()
    pack_slice(floats, ints, 6 - 4 * r, near_ref, N)
    pack_slice(floats, ints, 2 + 4 * r, mine_ref, 0)
    pack_slice(floats, ints, 7 - 4 * r, ahead_ref, N)
    copies.wait()


def pack_kernel(near, wave, *refs):
    sources, (all_ref, swap_ref, chain_ref), (floats, ints, sems) = refs[:5], refs[5:8], refs[8:]
    r = lax.axis_index("row")
    loads, copies = Copies(sems), Copies(sems)
    copies.used = 5
    load_all(loads, sources, floats, ints)
    copies.start(wave.at[pl.ds(N * (4 - 4 * r), N)], swap_ref.at[pl.ds(0, N)])
    copies.start(wave.at[pl.ds(N * (2 + 4 * r), 2 * N)], chain_ref.at[pl.ds(0, 2 * N)])
    loads.wait()
    for s in range(8):
        pack_slice(floats, ints, s, all_ref.at[s], 0)
    for i, rel in enumerate((0, 1, 3)):
        swap_ref[N + FIELDS * i:N + FIELDS * i + FIELDS, :] = all_ref[4 - 4 * r + rel]
    chain_ref[2 * N:, :] = all_ref[3 + 4 * r]
    copies.wait()


def field_in(copies, r, f_ref, own, own_row, other, other_row):
    for z in range(2):
        copies.start(own.at[pl.ds(own_row + HALF * z, HALF)], f_ref.at[z, pl.ds(pl.multiple_of(HALF * r, HALF), HALF)])
        copies.start(other.at[pl.ds(other_row + HALF * z, HALF)],
                     f_ref.at[z, pl.ds(pl.multiple_of(HALF - HALF * r, HALF), HALF)])


def parts_in(copies, r, p_ref, parts, rel, other, row, first=0):
    count = FIELDS - first
    copies.start(parts.at[4 * r + rel, pl.ds(first, count)], p_ref.at[r, pl.ds(first, count)])
    copies.start(other.at[pl.ds(row + first, count)], p_ref.at[1 - r, pl.ds(first, count)])


def piece_out(r, z_ref, q_ref, own, away):
    for half, dst in ((r, own), (1 - r, away)):
        for z in range(2):
            dst[HALF * z:HALF * z + HALF, :] = z_ref[z, pl.ds(pl.multiple_of(HALF * half, HALF), HALF), :]
        dst[2 * HALF:, :] = q_ref[half, :PUSHED, :]


def moves_out(moves, wave, *items):
    for ref, slot in items:
        moves.start(ref.at[pl.ds(0, N)], wave.at[pl.ds(slot * N, N)])


def near_kernel(wave, mine, near, table, d_ref, q_ref, f3, p2, tab, *rest):
    work, sems = rest[:-1], rest[-1]
    r = lax.axis_index("row")
    copies, later = Copies(sems), Copies(sems)
    later.used = 7
    field_in(copies, r, f3, wave, N * (4 * r + 1), near, 0)
    copies.start(mine, p2.at[r])
    copies.start(near.at[pl.ds(N, FIELDS)], p2.at[1 - r])
    later.start(table, tab)
    copies.wait()
    step(f3, p2, p2, tab, d_ref, *work, ready=later)
    q_ref[...] = p2[...]


def first_kernel(q2, wave, parts, swap, table, q_ref, own, away, f2, p1, pushed, z, tab, *rest):
    work, sems = rest[:-1], rest[-1]
    r = lax.axis_index("row")
    copies, later = Copies(sems), Copies(sems)
    later.used = 7
    field_in(copies, r, f2, wave, N * 4 * r, swap, 0)
    parts_in(copies, r, p1, parts, 1, swap, N + FIELDS)
    later.start(table, tab)
    copies.wait()
    step(f2, p1, p1, tab, z, *work, ready=later)
    q_ref[...] = p1[...]
    step(z, q2, pushed, tab, f2, *work)
    piece_out(r, f2, pushed, own, away)


def second_kernel(q1, parts, swap, chain, ahead, following, relay, table, d_ref, q_ref, to_back, own, away,
                  f0, f1, p0, pm, pushed, z, tab, *rest):
    work, sems = rest[:-1], rest[-1]
    r = lax.axis_index("row")
    copies, later = Copies(sems), Copies(sems)
    later.used = 23
    field_in(copies, r, f0, ahead, 0, chain, 0)
    copies.start(ahead.at[pl.ds(N, FIELDS)], pm.at[r])
    copies.start(chain.at[pl.ds(2 * N, FIELDS)], pm.at[1 - r])
    later.start(table, tab)
    field_in(copies, r, f1, following, 0, chain, N)
    parts_in(copies, r, p0, parts, 0, swap, N)
    copies.wait()

    @pl.when((r == 0) & (lax.rem(lax.axis_index("tm"), lax.axis_size("tm") // 2) == 0))
    def _():
        again = Copies(sems)
        again.used = 15
        for z in range(2):
            again.start(relay.at[pl.ds(HALF * z, HALF)], f0.at[z, pl.ds(pl.multiple_of(HALF * r, HALF), HALF)])
        again.start(relay.at[pl.ds(N, FIELDS)], pm.at[r])
        again.wait()

    @pl.when((r == 0) & (lax.axis_index("tm") == 0))
    def _():
        f1[...] = jnp.zeros_like(f1)

    step(f0, pm, to_back, tab, d_ref, *work, ready=later)
    step(f1, p0, p0, tab, z, *work)
    q_ref[...] = p0[...]
    step(z, q1, pushed, tab, f1, *work)
    piece_out(r, f1, pushed, own, away)


def third_kernel(d_ref, q0, own_a, own_b, back_a, table, own, away, wave, f0, pushed, z, tab, *rest):
    work, sems = rest[:-1], rest[-1]
    r = lax.axis_index("row")
    copies, moves, later = Copies(sems), Copies(sems), Copies(sems)
    later.used = 11
    moves.used = 2
    copies.start(d_ref, f0)
    later.start(table, tab)
    moves_out(moves, wave, (own_a, 4 * r + 2), (own_b, 4 * r + 1), (back_a, 6 - 4 * r))
    copies.wait()

    @pl.when((r == 0) & (lax.axis_index("tm") == 0))
    def _():
        f0[...] = jnp.zeros_like(f0)

    step(f0, q0, pushed, tab, z, *work, ready=later)
    piece_out(r, z, pushed, own, away)
    moves.wait()


def fourth_kernel(d_ref, parts, swap, from_back, own_c, table, wave_in, own, away, wave,
                  p3, pushed, z, tab, *rest):
    work, sems = rest[:-1], rest[-1]
    r = lax.axis_index("row")
    copies, moves, later = Copies(sems), Copies(sems), Copies(sems)
    later.used = 11
    moves.used = 8
    parts_in(copies, r, p3, parts, 3, swap, N + 2 * FIELDS, PUSHED)
    copies.start(from_back, p3.at[:, pl.ds(0, PUSHED)])
    later.start(table, tab)
    moves_out(moves, wave, (own_c, 4 * r))
    copies.wait()
    step(d_ref, p3, pushed, tab, z, *work, ready=later)
    piece_out(r, z, pushed, own, away)
    moves.wait()


def late_kernel(own_a, own_b, own_c, own_d, back_a, back_b, back_c, wave_in, wave, phase, energy, packed, sems):
    r = lax.axis_index("row")
    own, other = 4 * r, 4 - 4 * r
    moves, copies = Copies(sems), Copies(sems)
    copies.used = 4
    for base, group in ((own, (own_a, own_b, own_c, own_d)), (other, (back_a, back_b, back_c, back_c))):
        for ref, slot in zip(group, (2, 1, 0, 3)):
            copies.start(ref.at[pl.ds(N, PUSHED)], packed.at[base + slot])
    moves_out(moves, wave, (back_b, other + 1), (back_c, other), (own_d, own + 3))
    copies.wait()
    for s in range(8):
        for k in range(ROWS):
            phase[s:s + 1, N * k:N * k + N] = packed[s, k:k + 1, :]
            energy[s:s + 1, N * k:N * k + N] = packed[s, ROWS + k:ROWS + k + 1, :]
    moves.wait()


def final_kernel(back_d, wave_in, phase_in, energy_in, wave, phase, energy, sems):
    r = lax.axis_index("row")
    last = 7 - 4 * r
    moves = Copies(sems)
    moves_out(moves, wave, (back_d, last))
    phase[...] = phase_in[...]
    energy[...] = energy_in[...]
    for k in range(ROWS):
        phase[pl.ds(last, 1), N * k:N * k + N] = back_d[N + k:N + k + 1, :]
        energy[pl.ds(last, 1), N * k:N * k + N] = back_d[N + ROWS + k:N + ROWS + k + 1, :]
    moves.wait()


def body(wavefront, particle_phase, particle_energy, row_offset, row_cell, col_cell):
    table = jnp.asarray(tables())
    r = lax.axis_index("row")
    nt = lax.axis_size("tm")
    both = BOTH
    swap = [(i, i ^ 1) for i in range(2 * nt)]
    chain = [(i, (i + 1) % (2 * nt)) for i in range(2 * nt)]
    far = [2 * t for t in range(nt) if (t + 1) % (nt // 2) == 0]
    ahead = [(i, i + 2 if i % 2 == 0 else i) for i in range(2 * nt) if i not in far]
    around = [(i, (i + 3) % (2 * nt)) for i in far]
    onward = [(j, j - 1) for i, j in around]
    direct = [(i, i + 2) for i in far if i + 2 < 2 * nt]
    back = [(j, i) for i, j in chain]
    wave = wavefront.reshape(8 * N, N)
    unit = 1 << 33

    full, field = (2, FIELDS, N), (2, N, N)
    pieces = [(PIECE, N), (PIECE, N)]
    raw = (wave, particle_phase, particle_energy, row_offset, row_cell, col_cell)
    stage = [pltpu.VMEM((3, 8, PART), F32), pltpu.VMEM((2, 8, PART), jnp.int32)]
    to_near, to_ahead, to_next, mine = call(
        early_pack_kernel, [(N + FIELDS, N), (N + FIELDS, N), (N, N), (FIELDS, N)], [VM] * 4, stage, 8, [HB] * 6, 1 << 20,
        vmem=61000 << 10,
    )(*raw)
    f_near = lax.ppermute(to_near, both, swap)
    f_around = lax.ppermute(to_ahead, both, around)
    f_next = lax.ppermute(to_next, both, ahead + direct)
    parts, to_swap, to_chain = call(
        pack_kernel, [(8, FIELDS, N), (N + 3 * FIELDS, N), (2 * N + FIELDS, N)],
        [VM] * 3, stage, 8, [ANY] + [HB] * 6, 4 * unit, vmem=61000 << 10,
    )(to_near, *raw)
    f_swap = lax.ppermute(to_swap, both, swap)
    to_ahead, to_chain = lax.optimization_barrier((to_ahead, to_chain))
    f_ahead = lax.ppermute(to_ahead, both, ahead)

    d3, q2 = call(
        near_kernel, [field, full], [VM, VM], [FIELD, PARTS, TABLE] + WORK, 8, [ANY] * 4, unit, vmem=50000 << 10,
    )(wave, mine, f_near, table)
    q2, f_around, to_chain = lax.optimization_barrier((q2, f_around, to_chain))
    f_relay = lax.ppermute(f_around, both, onward)
    f_chain = lax.ppermute(to_chain, both, chain)
    q1, own_a, away_a = call(
        first_kernel, [full] + pieces, [VM] * 3, [FIELD, PARTS, PUSH, FIELD, TABLE] + WORK, 8,
        [VM] + [ANY] * 4, 2 * unit,
    )(q2, wave, parts, f_swap, table)
    back_a = lax.ppermute(away_a, both, swap)
    d0, q0, to_back, own_b, away_b = call(
        second_kernel, [field, full, (2, PUSHED, N)] + pieces, [VM] * 5,
        [FIELD, FIELD, PARTS, PARTS, PUSH, FIELD, TABLE] + WORK, 24, [VM] + [ANY] * 7, 3 * unit,
    )(q1, parts, f_swap, f_chain, f_ahead, f_next, f_relay, table)
    from_back = lax.ppermute(to_back, both, back)
    back_b = lax.ppermute(away_b, both, swap)
    own_c, away_c, wave = call(
        third_kernel, pieces + [(8 * N, N)], [VM, VM, ANY],
        [FIELD, PUSH, FIELD, TABLE] + WORK, 12, [ANY, VM] + [ANY] * 4, unit,
    )(d0, q0, own_a, own_b, back_a, table)
    back_c = lax.ppermute(away_c, both, swap)
    own_d, away_d, wave = call(
        fourth_kernel, pieces + [(8 * N, N)], [VM, VM, ANY],
        [PARTS, PUSH, FIELD, TABLE] + WORK, 12, [VM] + [ANY] * 6, 2 * unit, {6: 2},
    )(d3, parts, f_swap, from_back, own_c, table, wave)
    back_d = lax.ppermute(away_d, both, swap)
    particles = [(8, PART), (8, PART)]
    wave, phase, energy = call(
        late_kernel, [(8 * N, N)] + particles, [ANY, VM, VM], [pltpu.VMEM((8, PUSHED, N), F32)], 16,
        [ANY] * 8, 1 << 20, {7: 0},
    )(own_a, own_b, own_c, own_d, back_a, back_b, back_c, wave)
    wave, phase, energy = call(
        final_kernel, [(8 * N, N)] + particles, [HB, VM, VM], [], 4, [VM, HB, VM, VM], 1 << 20, {1: 0},
    )(back_d, wave, phase, energy)
    return wave.reshape(8, 2, HALF, N), phase, energy


def solution(mesh):
    P = jax.sharding.PartitionSpec
    wide, flat = P("tm", None, "row", None), P("tm", "row")
    return jax.shard_map(body, mesh=mesh, in_specs=(wide,) + (flat,) * 5,
                         out_specs=(wide, flat, flat), check_vma=False)
```

```python
import math

import jax
import jax.numpy as jnp
import ml_dtypes
import numpy as np
from jax import lax
from jax.experimental import pallas as pl
from jax.experimental.pallas import tpu as pltpu

BF = jnp.bfloat16
F32 = jnp.float32
F8 = jnp.float8_e5m2
UP = 1024.0
DOWN = 1.0 / UP
N = 256
HALF = 128
PART = 2048
ROWS = PART // N
WIN = 144
FIELDS = 5 * ROWS
PUSHED = 2 * ROWS
PIECE = 2 * HALF + PUSHED
BOTH = ("tm", "row")


def split_np(m):
    hi = m.astype(ml_dtypes.bfloat16)
    return hi, (m - hi.astype(np.float64)).astype(ml_dtypes.bfloat16)


def tables():
    k = np.arange(N)
    m = np.where(k < N // 2, k, k - N).astype(np.float64)
    h = np.exp(-1j * np.pi / N * m * m)
    dft = np.exp(-2j * np.pi / N * (k[:, None] * k[None, :] % N))
    a = (np.conj(dft) / N) @ (h[:, None] * dft)
    c0, c1 = a[:HALF, :HALF], a[:HALF, HALF:]
    both = [0.5 * (c0 + c1), 0.5 * (c0 - c1)]
    right = np.stack([np.block([[b.real, b.imag], [-b.imag, b.real]]) for b in both])
    left = np.stack([np.block([[b.real, -b.imag], [b.imag, b.real]]) for b in both])
    return np.stack(split_np(np.stack([right, left])))


def sincos(x):
    n = jnp.round(x * (1.0 / math.pi))
    r = x - n * 3.140625
    r = r - n * 9.670257568359375e-4
    r = r - n * 6.277114152908325e-07
    half = n * 0.5
    sign = 1.0 - 4.0 * (half - jnp.floor(half))
    y = r * r
    s = -2.3889859e-08
    for c in (2.7525562e-06, -1.98408740e-04, 8.33333310e-03, -1.66666667e-01):
        s = s * y + c
    s = r + r * y * s
    c = 2.08767570e-09 - 1.1470746e-11 * y
    for d in (-2.75573192e-07, 2.48015873e-05, -1.38888889e-03, 4.16666667e-02, -0.5, 1.0):
        c = c * y + d
    return s * sign, c * sign


def hilo(x):
    hi = x.astype(BF)
    return hi, (x - hi.astype(F32)).astype(BF)


def mm(a, b):
    return jnp.dot(a, b, preferred_element_type=F32)


def step(f_ref, p_ref, q_ref, tab, out_ref, c_ref, w_ref, s_ref, sr_ref, x_ref, samp_ref, c8_ref, sr8_ref, ready=None):
    iota_c = (lax.broadcasted_iota(jnp.int32, (16, 16, N), 0) * 16
              + lax.broadcasted_iota(jnp.int32, (16, 16, N), 1)).astype(F32).astype(BF)
    one = jnp.ones((16, N), BF)
    zero = jnp.zeros((16, N), BF)
    down = jnp.full((16, N), DOWN, BF)
    iota_r = lax.broadcasted_iota(jnp.int32, (WIN, N), 0).astype(F32)
    for h in range(2):
        off = p_ref[h, 2 * ROWS:3 * ROWS]
        lower = 0.5 - off
        upper = 0.5 + off
        w_ref[0] = 0.5 * lower * lower
        w_ref[1] = 0.75 - off * off
        w_ref[2] = 0.5 * upper * upper
        win0 = 0 if h == 0 else N - WIN
        field = f_ref[:, win0:win0 + WIN, :].reshape(2 * WIN, N)
        hi = field.astype(BF)
        lo = ((field - hi.astype(F32)) * UP).astype(F8)
        for k in range(ROWS):
            col = jnp.broadcast_to(p_ref[h, 4 * ROWS + k:4 * ROWS + k + 1, :], (16, N)).astype(BF)
            hot = jnp.where(iota_c == col[None], one[None], zero[None]).reshape(N, N)
            c_ref[h, :, N * k:N * k + N] = hot
            hot8 = jnp.where(iota_c == col[None], down[None], zero[None]).reshape(N, N).astype(F8)
            c8_ref[h, :, N * k:N * k + N] = hot8
            g = mm(hi, hot) + mm(lo, hot8)
            at = p_ref[h, 3 * ROWS + k:3 * ROWS + k + 1, :] - float(win0)
            w = jnp.where(iota_r == at, w_ref[1, k:k + 1, :],
                          jnp.where(iota_r == at - 1.0, w_ref[0, k:k + 1, :],
                                    jnp.where(iota_r == at + 1.0, w_ref[2, k:k + 1, :], 0.0)))
            samp_ref[0, k:k + 1, :] = jnp.sum(w * g[:WIN], 0, keepdims=True)
            samp_ref[1, k:k + 1, :] = jnp.sum(w * g[WIN:], 0, keepdims=True)
        phase = p_ref[h, :ROWS]
        sine, cosine = sincos(phase)
        energy = p_ref[h, ROWS:2 * ROWS] - 0.5 * (samp_ref[0] * cosine - samp_ref[1] * sine)
        phase = phase + energy
        q_ref[h, :ROWS] = phase
        q_ref[h, ROWS:2 * ROWS] = energy
        sine, cosine = sincos(phase)
        for z, v in ((0, cosine), (1, -sine)):
            vh = v.astype(BF).astype(F32)
            s_ref[2 * z] = vh
            s_ref[2 * z + 1] = v - vh
        for k in range(ROWS):
            at = jnp.broadcast_to(p_ref[h, 3 * ROWS + k:3 * ROWS + k + 1, :] - float(HALF * h), (16, N)).astype(BF)
            here = iota_c[:8] == at[None]
            for z in range(2):
                value = jnp.broadcast_to(s_ref[2 * z, k:k + 1, :], (16, N)).astype(BF)
                sr_ref[HALF * z:HALF * z + HALF, N * k:N * k + N] = jnp.where(here, value[None], zero[None]).reshape(HALF, N)
                value = jnp.broadcast_to(s_ref[2 * z + 1, k:k + 1, :] * UP, (16, N)).astype(BF)
                sr8_ref[HALF * z:HALF * z + HALF, N * k:N * k + N] = jnp.where(here, value[None], zero[None]).reshape(HALF, N).astype(F8)
        d = lax.dot_general(sr_ref[...], c_ref[h], (((1,), (1,)), ((), ())), preferred_element_type=F32)
        d = d + lax.dot_general(sr8_ref[...], c8_ref[h], (((1,), (1,)), ((), ())), preferred_element_type=F32)
        for z in range(2):
            x_ref[HALF * h:HALF * h + HALF, N * z:N * z + N] = (
                f_ref[z, HALF * h:HALF * h + HALF, :]
                + d[HALF * z:HALF * z + HALF])
    if ready is not None:
        ready.wait()
    quads = [[], []]
    for z in range(2):
        top = x_ref[:HALF, N * z:N * z + N]
        low = x_ref[HALF:, N * z:N * z + N]
        rows = jnp.concatenate([top + low, top - low], 0)
        quads[0].append(rows[:, :HALF] + rows[:, HALF:])
        quads[1].append(rows[:, :HALF] - rows[:, HALF:])
    turned = []
    for e in range(2):
        xh, xl = hilo(jnp.concatenate(quads[e], 1))
        t = mm(jnp.concatenate([xh, xl], 0), tab[0, 0, e])
        turned.append(t[:N] + t[N:] + mm(xh, tab[1, 0, e]))
    halves = []
    for e in range(2):
        rows = slice(HALF * e, HALF * e + HALF)
        y = jnp.concatenate([jnp.concatenate([turned[0][rows, :HALF], turned[1][rows, :HALF]], 1),
                             jnp.concatenate([turned[0][rows, HALF:], turned[1][rows, HALF:]], 1)], 0)
        yh, yl = hilo(y)
        t = mm(jnp.concatenate([tab[0, 1, e], tab[1, 1, e]], 0), yh)
        halves.append(t[:N] + t[N:] + mm(tab[0, 1, e], yl))
    for e, rows in enumerate((halves[0] + halves[1], halves[0] - halves[1])):
        left, right = rows[:, :HALF], rows[:, HALF:]
        out = jnp.concatenate([left + right, left - right], 1)
        out_ref[0, HALF * e:HALF * e + HALF] = out[:HALF]
        out_ref[1, HALF * e:HALF * e + HALF] = out[HALF:]


WORK = [pltpu.VMEM((2, N, PART), BF), pltpu.VMEM((3, ROWS, N), F32), pltpu.VMEM((4, ROWS, N), F32),
        pltpu.VMEM((N, PART), BF), pltpu.VMEM((N, 2 * N), F32), pltpu.VMEM((2, ROWS, N), F32),
        pltpu.VMEM((2, N, PART), F8), pltpu.VMEM((N, PART), F8)]
FIELD = pltpu.VMEM((2, N, N), F32)
PARTS = pltpu.VMEM((2, FIELDS, N), F32)
TABLE = pltpu.VMEM((2, 2, 2, N, N), BF)
PUSH = pltpu.VMEM((2, PUSHED, N), F32)
ANY = pl.BlockSpec(memory_space=pl.ANY)
VM = pl.BlockSpec(memory_space=pltpu.VMEM)
HB = pl.BlockSpec(memory_space=pltpu.HBM)


class Copies:
    def __init__(self, sems):
        self.sems = sems
        self.used = 0
        self.open = []

    def start(self, src, dst):
        copy = pltpu.make_async_copy(src, dst, self.sems.at[self.used])
        self.used += 1
        copy.start()
        self.open.append(copy)

    def wait(self):
        for copy in self.open:
            copy.wait()
        self.open = []


def call(kernel, outs, out_specs, scratch, copies, in_specs, flops, aliases={}, vmem=40 << 20):
    return pl.pallas_call(
        kernel, out_shape=[jax.ShapeDtypeStruct(s, F32) for s in outs], in_specs=in_specs, out_specs=out_specs,
        scratch_shapes=scratch + [pltpu.SemaphoreType.DMA((copies,))],
        input_output_aliases=aliases, cost_estimate=pl.CostEstimate(flops=flops, bytes_accessed=4 << 20, transcendentals=0),
        compiler_params=pltpu.CompilerParams(vmem_limit_bytes=vmem))


def load_all(copies, sources, floats, ints):
    for a, src in enumerate(sources):
        copies.start(src, floats.at[a] if a < 3 else ints.at[a - 3])


def pack_slice(floats, ints, index, dst, row):
    for a in range(5):
        src = floats.at[a] if a < 3 else ints.at[a - 3]
        for k in range(ROWS):
            at = row + a * ROWS + k
            dst[at:at + 1, :] = src[pl.ds(index, 1), N * k:N * k + N].astype(F32)


def early_pack_kernel(wave, *refs):
    sources, (near_ref, ahead_ref, next_ref, mine_ref), (floats, ints, sems) = refs[:5], refs[5:9], refs[9:]
    r = lax.axis_index("row")
    loads, copies = Copies(sems), Copies(sems)
    copies.used = 5
    load_all(loads, sources, floats, ints)
    copies.start(wave.at[pl.ds(N * (5 - 4 * r), N)], near_ref.at[pl.ds(0, N)])
    copies.start(wave.at[pl.ds(N * (6 - 4 * r), N)], ahead_ref.at[pl.ds(0, N)])
    copies.start(wave.at[pl.ds(N * (7 - 4 * r), N)], next_ref)
    loads.wait()
    pack_slice(floats, ints, 6 - 4 * r, near_ref, N)
    pack_slice(floats, ints, 2 + 4 * r, mine_ref, 0)
    pack_slice(floats, ints, 7 - 4 * r, ahead_ref, N)
    copies.wait()


def pack_kernel(near, wave, *refs):
    sources, (all_ref, swap_ref, chain_ref, link_ref), (floats, ints, sems) = refs[:5], refs[5:9], refs[9:]
    r = lax.axis_index("row")
    loads, copies = Copies(sems), Copies(sems)
    copies.used = 5
    load_all(loads, sources, floats, ints)
    copies.start(wave.at[pl.ds(N * (4 - 4 * r), N)], swap_ref.at[pl.ds(0, N)])
    copies.start(wave.at[pl.ds(N * (2 + 4 * r), N)], chain_ref.at[pl.ds(0, N)])
    copies.start(wave.at[pl.ds(N * (3 + 4 * r), N)], link_ref)
    loads.wait()
    for s in range(8):
        pack_slice(floats, ints, s, all_ref.at[s], 0)
    for i, rel in enumerate((0, 1, 3)):
        swap_ref[N + FIELDS * i:N + FIELDS * i + FIELDS, :] = all_ref[4 - 4 * r + rel]
    chain_ref[N:, :] = all_ref[3 + 4 * r]
    copies.wait()


def field_in(copies, r, f_ref, own, own_row, other, other_row):
    for z in range(2):
        copies.start(own.at[pl.ds(own_row + HALF * z, HALF)], f_ref.at[z, pl.ds(pl.multiple_of(HALF * r, HALF), HALF)])
        copies.start(other.at[pl.ds(other_row + HALF * z, HALF)],
                     f_ref.at[z, pl.ds(pl.multiple_of(HALF - HALF * r, HALF), HALF)])


def parts_in(copies, r, p_ref, parts, rel, other, row, first=0):
    count = FIELDS - first
    copies.start(parts.at[4 * r + rel, pl.ds(first, count)], p_ref.at[r, pl.ds(first, count)])
    copies.start(other.at[pl.ds(row + first, count)], p_ref.at[1 - r, pl.ds(first, count)])


def piece_out(r, z_ref, q_ref, own, away):
    for half, dst in ((r, own), (1 - r, away)):
        for z in range(2):
            dst[HALF * z:HALF * z + HALF, :] = z_ref[z, pl.ds(pl.multiple_of(HALF * half, HALF), HALF), :]
        dst[2 * HALF:, :] = q_ref[half, :PUSHED, :]


def moves_out(moves, wave, *items):
    for ref, slot in items:
        moves.start(ref.at[pl.ds(0, N)], wave.at[pl.ds(slot * N, N)])


def near_kernel(wave, mine, near, table, d_ref, q_ref, f3, p2, tab, *rest):
    work, sems = rest[:-1], rest[-1]
    r = lax.axis_index("row")
    copies, later = Copies(sems), Copies(sems)
    later.used = 7
    field_in(copies, r, f3, wave, N * (4 * r + 1), near, 0)
    copies.start(mine, p2.at[r])
    copies.start(near.at[pl.ds(N, FIELDS)], p2.at[1 - r])
    later.start(table, tab)
    copies.wait()
    step(f3, p2, p2, tab, d_ref, *work, ready=later)
    q_ref[...] = p2[...]


def first_kernel(q2, wave, parts, swap, table, q_ref, own, away, f2, p1, pushed, z, tab, *rest):
    work, sems = rest[:-1], rest[-1]
    r = lax.axis_index("row")
    copies, later = Copies(sems), Copies(sems)
    later.used = 7
    field_in(copies, r, f2, wave, N * 4 * r, swap, 0)
    parts_in(copies, r, p1, parts, 1, swap, N + FIELDS)
    later.start(table, tab)
    copies.wait()
    step(f2, p1, p1, tab, z, *work, ready=later)
    q_ref[...] = p1[...]
    step(z, q2, pushed, tab, f2, *work)
    piece_out(r, f2, pushed, own, away)


def second_kernel(q1, parts, swap, link, following, table, q_ref, own, away, f1, p0, pushed, z, tab, *rest):
    work, sems = rest[:-1], rest[-1]
    r = lax.axis_index("row")
    copies, later = Copies(sems), Copies(sems)
    later.used = 7
    field_in(copies, r, f1, following, 0, link, 0)
    parts_in(copies, r, p0, parts, 0, swap, N)
    later.start(table, tab)
    copies.wait()

    @pl.when((r == 0) & (lax.axis_index("tm") == 0))
    def _():
        f1[...] = jnp.zeros_like(f1)

    step(f1, p0, p0, tab, z, *work, ready=later)
    q_ref[...] = p0[...]
    step(z, q1, pushed, tab, f1, *work)
    piece_out(r, f1, pushed, own, away)


def edge_kernel(after, chain, ahead, relay, table, d_ref, to_back, f0, pm, tab, *rest):
    work, sems = rest[:-1], rest[-1]
    r = lax.axis_index("row")
    copies, later = Copies(sems), Copies(sems)
    later.used = 15
    field_in(copies, r, f0, ahead, 0, chain, 0)
    copies.start(ahead.at[pl.ds(N, FIELDS)], pm.at[r])
    copies.start(chain.at[pl.ds(N, FIELDS)], pm.at[1 - r])
    later.start(table, tab)
    copies.wait()

    @pl.when((r == 0) & (lax.rem(lax.axis_index("tm"), lax.axis_size("tm") // 2) == 0))
    def _():
        again = Copies(sems)
        again.used = 8
        for z in range(2):
            again.start(relay.at[pl.ds(HALF * z, HALF)], f0.at[z, pl.ds(pl.multiple_of(HALF * r, HALF), HALF)])
        again.start(relay.at[pl.ds(N, FIELDS)], pm.at[r])
        again.wait()

    step(f0, pm, to_back, tab, d_ref, *work, ready=later)


def third_kernel(d_ref, q0, own_a, own_b, back_a, table, own, away, wave, f0, pushed, z, tab, *rest):
    work, sems = rest[:-1], rest[-1]
    r = lax.axis_index("row")
    copies, moves, later = Copies(sems), Copies(sems), Copies(sems)
    later.used = 11
    moves.used = 2
    copies.start(d_ref, f0)
    later.start(table, tab)
    moves_out(moves, wave, (own_a, 4 * r + 2), (own_b, 4 * r + 1), (back_a, 6 - 4 * r))
    copies.wait()

    @pl.when((r == 0) & (lax.axis_index("tm") == 0))
    def _():
        f0[...] = jnp.zeros_like(f0)

    step(f0, q0, pushed, tab, z, *work, ready=later)
    piece_out(r, z, pushed, own, away)
    moves.wait()


def fourth_kernel(d_ref, parts, swap, from_back, own_c, table, wave_in, own, away, wave,
                  p3, pushed, z, tab, *rest):
    work, sems = rest[:-1], rest[-1]
    r = lax.axis_index("row")
    copies, moves, later = Copies(sems), Copies(sems), Copies(sems)
    later.used = 11
    moves.used = 8
    parts_in(copies, r, p3, parts, 3, swap, N + 2 * FIELDS, PUSHED)
    copies.start(from_back, p3.at[:, pl.ds(0, PUSHED)])
    later.start(table, tab)
    moves_out(moves, wave, (own_c, 4 * r))
    copies.wait()
    step(d_ref, p3, pushed, tab, z, *work, ready=later)
    piece_out(r, z, pushed, own, away)
    moves.wait()


def late_kernel(own_a, own_b, own_c, own_d, back_a, back_b, back_c, wave_in, wave, phase, energy, packed, sems):
    r = lax.axis_index("row")
    own, other = 4 * r, 4 - 4 * r
    moves, copies = Copies(sems), Copies(sems)
    copies.used = 4
    for base, group in ((own, (own_a, own_b, own_c, own_d)), (other, (back_a, back_b, back_c, back_c))):
        for ref, slot in zip(group, (2, 1, 0, 3)):
            copies.start(ref.at[pl.ds(N, PUSHED)], packed.at[base + slot])
    moves_out(moves, wave, (back_b, other + 1), (back_c, other), (own_d, own + 3))
    copies.wait()
    for s in range(8):
        for k in range(ROWS):
            phase[s:s + 1, N * k:N * k + N] = packed[s, k:k + 1, :]
            energy[s:s + 1, N * k:N * k + N] = packed[s, ROWS + k:ROWS + k + 1, :]
    moves.wait()


def final_kernel(back_d, wave_in, phase_in, energy_in, wave, phase, energy, sems):
    r = lax.axis_index("row")
    last = 7 - 4 * r
    moves = Copies(sems)
    moves_out(moves, wave, (back_d, last))
    phase[...] = phase_in[...]
    energy[...] = energy_in[...]
    for k in range(ROWS):
        phase[pl.ds(last, 1), N * k:N * k + N] = back_d[N + k:N + k + 1, :]
        energy[pl.ds(last, 1), N * k:N * k + N] = back_d[N + ROWS + k:N + ROWS + k + 1, :]
    moves.wait()


def body(wavefront, particle_phase, particle_energy, row_offset, row_cell, col_cell):
    table = jnp.asarray(tables())
    r = lax.axis_index("row")
    nt = lax.axis_size("tm")
    both = BOTH
    swap = [(i, i ^ 1) for i in range(2 * nt)]
    chain = [(i, (i + 1) % (2 * nt)) for i in range(2 * nt)]
    far = [2 * t for t in range(nt) if (t + 1) % (nt // 2) == 0]
    ahead = [(i, i + 2 if i % 2 == 0 else i) for i in range(2 * nt) if i not in far]
    around = [(i, (i + 3) % (2 * nt)) for i in far]
    onward = [(j, j - 1) for i, j in around]
    direct = [(i, i + 2) for i in far if i + 2 < 2 * nt]
    back = [(j, i) for i, j in chain]
    wave = wavefront.reshape(8 * N, N)
    unit = 1 << 33

    full, field = (2, FIELDS, N), (2, N, N)
    pieces = [(PIECE, N), (PIECE, N)]
    raw = (wave, particle_phase, particle_energy, row_offset, row_cell, col_cell)
    stage = [pltpu.VMEM((3, 8, PART), F32), pltpu.VMEM((2, 8, PART), jnp.int32)]
    to_near, to_ahead, to_next, mine = call(
        early_pack_kernel, [(N + FIELDS, N), (N + FIELDS, N), (N, N), (FIELDS, N)], [VM] * 4, stage, 8, [HB] * 6, 1 << 20,
        vmem=61000 << 10,
    )(*raw)
    f_near = lax.ppermute(to_near, both, swap)
    f_around = lax.ppermute(to_ahead, both, around)
    f_next = lax.ppermute(to_next, both, ahead + direct)
    parts, to_swap, to_chain, to_link = call(
        pack_kernel, [(8, FIELDS, N), (N + 3 * FIELDS, N), (N + FIELDS, N), (N, N)],
        [VM] * 4, stage, 8, [ANY] + [HB] * 6, 4 * unit, vmem=61000 << 10,
    )(to_near, *raw)
    f_swap = lax.ppermute(to_swap, both, swap)
    to_ahead, to_chain = lax.optimization_barrier((to_ahead, to_chain))
    f_ahead = lax.ppermute(to_ahead, both, ahead)

    d3, q2 = call(
        near_kernel, [field, full], [VM, VM], [FIELD, PARTS, TABLE] + WORK, 8, [ANY] * 4, unit, vmem=50000 << 10,
    )(wave, mine, f_near, table)
    q2, to_chain, to_link = lax.optimization_barrier((q2, to_chain, to_link))
    f_link = lax.ppermute(to_link, both, chain)
    f_chain = lax.ppermute(to_chain, both, chain)
    q1, own_a, away_a = call(
        first_kernel, [full] + pieces, [VM] * 3, [FIELD, PARTS, PUSH, FIELD, TABLE] + WORK, 8,
        [VM] + [ANY] * 4, 2 * unit,
    )(q2, wave, parts, f_swap, table)
    q1, f_around = lax.optimization_barrier((q1, f_around))
    f_relay = lax.ppermute(f_around, both, onward)
    back_a = lax.ppermute(away_a, both, swap)
    q0, own_b, away_b = call(
        second_kernel, [full] + pieces, [VM] * 3, [FIELD, PARTS, PUSH, FIELD, TABLE] + WORK, 8,
        [VM] + [ANY] * 5, 2 * unit,
    )(q1, parts, f_swap, f_link, f_next, table)
    back_b = lax.ppermute(away_b, both, swap)
    d0, to_back = call(
        edge_kernel, [field, (2, PUSHED, N)], [VM, VM], [FIELD, PARTS, TABLE] + WORK, 16, [ANY] * 5, unit,
    )(q0, f_chain, f_ahead, f_relay, table)
    from_back = lax.ppermute(to_back, both, back)
    own_c, away_c, wave = call(
        third_kernel, pieces + [(8 * N, N)], [VM, VM, ANY],
        [FIELD, PUSH, FIELD, TABLE] + WORK, 12, [ANY, VM] + [ANY] * 4, unit,
    )(d0, q0, own_a, own_b, back_a, table)
    back_c = lax.ppermute(away_c, both, swap)
    own_d, away_d, wave = call(
        fourth_kernel, pieces + [(8 * N, N)], [VM, VM, ANY],
        [PARTS, PUSH, FIELD, TABLE] + WORK, 12, [VM] + [ANY] * 6, 2 * unit, {6: 2},
    )(d3, parts, f_swap, from_back, own_c, table, wave)
    back_d = lax.ppermute(away_d, both, swap)
    particles = [(8, PART), (8, PART)]
    wave, phase, energy = call(
        late_kernel, [(8 * N, N)] + particles, [ANY, VM, VM], [pltpu.VMEM((8, PUSHED, N), F32)], 16,
        [ANY] * 8, 1 << 20, {7: 0},
    )(own_a, own_b, own_c, own_d, back_a, back_b, back_c, wave)
    wave, phase, energy = call(
        final_kernel, [(8 * N, N)] + particles, [HB, VM, VM], [], 4, [VM, HB, VM, VM], 1 << 20, {1: 0},
    )(back_d, wave, phase, energy)
    return wave.reshape(8, 2, HALF, N), phase, energy


def solution(mesh):
    P = jax.sharding.PartitionSpec
    wide, flat = P("tm", None, "row", None), P("tm", "row")
    return jax.shard_map(body, mesh=mesh, in_specs=(wide,) + (flat,) * 5,
                         out_specs=(wide, flat, flat), check_vma=False)
```

```python
import math

import jax
import jax.numpy as jnp
import ml_dtypes
import numpy as np
from jax import lax
from jax.experimental import pallas as pl
from jax.experimental.pallas import tpu as pltpu

BF = jnp.bfloat16
F32 = jnp.float32
F8 = jnp.float8_e5m2
UP = 1024.0
DOWN = 1.0 / UP
N = 256
HALF = 128
PART = 2048
ROWS = PART // N
WIN = 144
NEAR = 136
FIELDS = 5 * ROWS
PUSHED = 2 * ROWS
PIECE = 2 * HALF + PUSHED
BOTH = ("tm", "row")


def split_np(m):
    hi = m.astype(ml_dtypes.bfloat16)
    return hi, (m - hi.astype(np.float64)).astype(ml_dtypes.bfloat16)


def tables():
    k = np.arange(N)
    m = np.where(k < N // 2, k, k - N).astype(np.float64)
    h = np.exp(-1j * np.pi / N * m * m)
    dft = np.exp(-2j * np.pi / N * (k[:, None] * k[None, :] % N))
    a = (np.conj(dft) / N) @ (h[:, None] * dft)
    c0, c1 = a[:HALF, :HALF], a[:HALF, HALF:]
    both = [0.5 * (c0 + c1), 0.5 * (c0 - c1)]
    right = np.stack([np.block([[b.real, b.imag], [-b.imag, b.real]]) for b in both])
    left = np.stack([np.block([[b.real, -b.imag], [b.imag, b.real]]) for b in both])
    return np.stack(split_np(np.stack([right, left])))


def sincos(x):
    n = jnp.round(x * (1.0 / math.pi))
    r = x - n * 3.140625
    r = r - n * 9.670257568359375e-4
    r = r - n * 6.277114152908325e-07
    half = n * 0.5
    sign = 1.0 - 4.0 * (half - jnp.floor(half))
    y = r * r
    s = -2.3889859e-08
    for c in (2.7525562e-06, -1.98408740e-04, 8.33333310e-03, -1.66666667e-01):
        s = s * y + c
    s = r + r * y * s
    c = 2.08767570e-09 - 1.1470746e-11 * y
    for d in (-2.75573192e-07, 2.48015873e-05, -1.38888889e-03, 4.16666667e-02, -0.5, 1.0):
        c = c * y + d
    return s * sign, c * sign


def hilo(x):
    hi = x.astype(BF)
    return hi, (x - hi.astype(F32)).astype(BF)


def mm(a, b):
    return jnp.dot(a, b, preferred_element_type=F32)


def step(f_ref, p_ref, q_ref, tab, out_ref, c_ref, w_ref, s_ref, sr_ref, x_ref, samp_ref, c8_ref, sr8_ref, ready=None):
    iota_c = (lax.broadcasted_iota(jnp.int32, (16, 16, N), 0) * 16
              + lax.broadcasted_iota(jnp.int32, (16, 16, N), 1)).astype(F32).astype(BF)
    one = jnp.ones((16, N), BF)
    zero = jnp.zeros((16, N), BF)
    down = jnp.full((16, N), DOWN, BF)
    iota_r = lax.broadcasted_iota(jnp.int32, (NEAR, N), 0).astype(F32)
    phase = jnp.concatenate([p_ref[0, :ROWS], p_ref[1, :ROWS]], 0)
    sine, cosine = sincos(phase)
    for h in range(2):
        off = p_ref[h, 2 * ROWS:3 * ROWS]
        lower = 0.5 - off
        upper = 0.5 + off
        w_ref[h, 0] = 0.5 * lower * lower
        w_ref[h, 1] = 0.75 - off * off
        w_ref[h, 2] = 0.5 * upper * upper
        win0 = 0 if h == 0 else N - WIN
        skip = h * (WIN - NEAR)
        field = f_ref[:, win0:win0 + WIN, :].reshape(2 * WIN, N)
        both = jnp.concatenate(hilo(field), 0)
        for k in range(ROWS):
            col = jnp.broadcast_to(p_ref[h, 4 * ROWS + k:4 * ROWS + k + 1, :], (16, N)).astype(BF)
            hot = jnp.where(iota_c == col[None], one[None], zero[None]).reshape(N, N)
            c_ref[h, :, N * k:N * k + N] = hot
            hot8 = jnp.where(iota_c == col[None], down[None], zero[None]).reshape(N, N).astype(F8)
            c8_ref[h, :, N * k:N * k + N] = hot8
            g = mm(both, hot)
            g = g[:2 * WIN] + g[2 * WIN:]
            at = p_ref[h, 3 * ROWS + k:3 * ROWS + k + 1, :] - float(win0 + skip)
            w = jnp.where(iota_r == at, w_ref[h, 1, k:k + 1, :],
                          jnp.where(iota_r == at - 1.0, w_ref[h, 0, k:k + 1, :],
                                    jnp.where(iota_r == at + 1.0, w_ref[h, 2, k:k + 1, :], 0.0)))
            samp_ref[0, h * ROWS + k:h * ROWS + k + 1, :] = jnp.sum(w * g[skip:skip + NEAR], 0, keepdims=True)
            samp_ref[1, h * ROWS + k:h * ROWS + k + 1, :] = jnp.sum(
                w * g[WIN + skip:WIN + skip + NEAR], 0, keepdims=True)
    energy = jnp.concatenate([p_ref[0, ROWS:2 * ROWS], p_ref[1, ROWS:2 * ROWS]], 0)
    energy = energy - 0.5 * (samp_ref[0] * cosine - samp_ref[1] * sine)
    phase = phase + energy
    for h in range(2):
        q_ref[h, :ROWS] = phase[h * ROWS:h * ROWS + ROWS]
        q_ref[h, ROWS:2 * ROWS] = energy[h * ROWS:h * ROWS + ROWS]
    sine, cosine = sincos(phase)
    for z, v in ((0, cosine), (1, -sine)):
        vh = v.astype(BF).astype(F32)
        s_ref[2 * z] = vh
        s_ref[2 * z + 1] = (v - vh) * UP
    for h in range(2):
        for k in range(ROWS):
            at = jnp.broadcast_to(p_ref[h, 3 * ROWS + k:3 * ROWS + k + 1, :] - float(HALF * h), (16, N)).astype(BF)
            here = iota_c[:8] == at[None]
            row = h * ROWS + k
            for z in range(2):
                value = jnp.broadcast_to(s_ref[2 * z, row:row + 1, :], (16, N)).astype(BF)
                sr_ref[h, HALF * z:HALF * z + HALF, N * k:N * k + N] = jnp.where(here, value[None], zero[None]).reshape(HALF, N)
                value = jnp.broadcast_to(s_ref[2 * z + 1, row:row + 1, :], (16, N)).astype(BF)
                sr8_ref[h, HALF * z:HALF * z + HALF, N * k:N * k + N] = jnp.where(
                    here, value[None], zero[None]).reshape(HALF, N).astype(F8)
        d = lax.dot_general(sr8_ref[h], c8_ref[h], (((1,), (1,)), ((), ())), preferred_element_type=F32)
        d = d + lax.dot_general(sr_ref[h], c_ref[h], (((1,), (1,)), ((), ())), preferred_element_type=F32)
        for z in range(2):
            x_ref[HALF * h:HALF * h + HALF, N * z:N * z + N] = (
                f_ref[z, HALF * h:HALF * h + HALF, :] + d[HALF * z:HALF * z + HALF])
    if ready is not None:
        ready.wait()
    quads = [[], []]
    for z in range(2):
        top = x_ref[:HALF, N * z:N * z + N]
        low = x_ref[HALF:, N * z:N * z + N]
        rows = jnp.concatenate([top + low, top - low], 0)
        quads[0].append(rows[:, :HALF] + rows[:, HALF:])
        quads[1].append(rows[:, :HALF] - rows[:, HALF:])
    turned = []
    for e in range(2):
        xh, xl = hilo(jnp.concatenate(quads[e], 1))
        t = mm(jnp.concatenate([xh, xl], 0), tab[0, 0, e])
        turned.append(t[:N] + t[N:] + mm(xh, tab[1, 0, e]))
    halves = []
    for e in range(2):
        rows = slice(HALF * e, HALF * e + HALF)
        y = jnp.concatenate([jnp.concatenate([turned[0][rows, :HALF], turned[1][rows, :HALF]], 1),
                             jnp.concatenate([turned[0][rows, HALF:], turned[1][rows, HALF:]], 1)], 0)
        yh, yl = hilo(y)
        t = mm(jnp.concatenate([tab[0, 1, e], tab[1, 1, e]], 0), yh)
        halves.append(t[:N] + t[N:] + mm(tab[0, 1, e], yl))
    for e, rows in enumerate((halves[0] + halves[1], halves[0] - halves[1])):
        left, right = rows[:, :HALF], rows[:, HALF:]
        out = jnp.concatenate([left + right, left - right], 1)
        out_ref[0, HALF * e:HALF * e + HALF] = out[:HALF]
        out_ref[1, HALF * e:HALF * e + HALF] = out[HALF:]


WORK = [pltpu.VMEM((2, N, PART), BF), pltpu.VMEM((2, 3, ROWS, N), F32), pltpu.VMEM((4, 2 * ROWS, N), F32),
        pltpu.VMEM((2, N, PART), BF), pltpu.VMEM((N, 2 * N), F32), pltpu.VMEM((2, 2 * ROWS, N), F32),
        pltpu.VMEM((2, N, PART), F8), pltpu.VMEM((2, N, PART), F8)]
FIELD = pltpu.VMEM((2, N, N), F32)
PARTS = pltpu.VMEM((2, FIELDS, N), F32)
TABLE = pltpu.VMEM((2, 2, 2, N, N), BF)
PUSH = pltpu.VMEM((2, PUSHED, N), F32)
ANY = pl.BlockSpec(memory_space=pl.ANY)
VM = pl.BlockSpec(memory_space=pltpu.VMEM)
HB = pl.BlockSpec(memory_space=pltpu.HBM)


class Copies:
    def __init__(self, sems):
        self.sems = sems
        self.used = 0
        self.open = []

    def start(self, src, dst):
        copy = pltpu.make_async_copy(src, dst, self.sems.at[self.used])
        self.used += 1
        copy.start()
        self.open.append(copy)

    def wait(self):
        for copy in self.open:
            copy.wait()
        self.open = []


def call(kernel, outs, out_specs, scratch, copies, in_specs, flops, aliases={}, vmem=40 << 20):
    return pl.pallas_call(
        kernel, out_shape=[jax.ShapeDtypeStruct(s, F32) for s in outs], in_specs=in_specs, out_specs=out_specs,
        scratch_shapes=scratch + [pltpu.SemaphoreType.DMA((copies,))],
        input_output_aliases=aliases, cost_estimate=pl.CostEstimate(flops=flops, bytes_accessed=4 << 20, transcendentals=0),
        compiler_params=pltpu.CompilerParams(vmem_limit_bytes=vmem))


def load_all(copies, sources, floats, ints):
    for a, src in enumerate(sources):
        copies.start(src, floats.at[a] if a < 3 else ints.at[a - 3])


def pack_slice(floats, ints, index, dst, row):
    for a in range(5):
        src = floats.at[a] if a < 3 else ints.at[a - 3]
        for k in range(ROWS):
            at = row + a * ROWS + k
            dst[at:at + 1, :] = src[pl.ds(index, 1), N * k:N * k + N].astype(F32)


def early_pack_kernel(wave, *refs):
    sources, (near_ref, ahead_ref, mine_ref), (floats, ints, sems) = refs[:5], refs[5:8], refs[8:]
    r = lax.axis_index("row")
    loads, copies = Copies(sems), Copies(sems)
    copies.used = 5
    load_all(loads, sources, floats, ints)
    copies.start(wave.at[pl.ds(N * (5 - 4 * r), N)], near_ref.at[pl.ds(0, N)])
    copies.start(wave.at[pl.ds(N * (6 - 4 * r), N)], ahead_ref.at[pl.ds(0, N)])
    loads.wait()
    pack_slice(floats, ints, 6 - 4 * r, near_ref, N)
    pack_slice(floats, ints, 2 + 4 * r, mine_ref, 0)
    pack_slice(floats, ints, 7 - 4 * r, ahead_ref, N)
    copies.wait()


def pack_kernel(near, wave, *refs):
    sources, (all_ref, swap_ref, chain_ref, link_ref, next_ref), (floats, ints, sems) = refs[:5], refs[5:10], refs[10:]
    r = lax.axis_index("row")
    loads, copies = Copies(sems), Copies(sems)
    copies.used = 5
    load_all(loads, sources, floats, ints)
    copies.start(wave.at[pl.ds(N * (4 - 4 * r), N)], swap_ref.at[pl.ds(0, N)])
    copies.start(wave.at[pl.ds(N * (2 + 4 * r), N)], chain_ref.at[pl.ds(0, N)])
    copies.start(wave.at[pl.ds(N * (3 + 4 * r), N)], link_ref)
    copies.start(wave.at[pl.ds(N * (7 - 4 * r), N)], next_ref)
    loads.wait()
    for s in range(8):
        pack_slice(floats, ints, s, all_ref.at[s], 0)
    for i, rel in enumerate((0, 1, 3)):
        swap_ref[N + FIELDS * i:N + FIELDS * i + FIELDS, :] = all_ref[4 - 4 * r + rel]
    chain_ref[N:, :] = all_ref[3 + 4 * r]
    copies.wait()


def field_in(copies, r, f_ref, own, own_row, other, other_row):
    for z in range(2):
        copies.start(own.at[pl.ds(own_row + HALF * z, HALF)], f_ref.at[z, pl.ds(pl.multiple_of(HALF * r, HALF), HALF)])
        copies.start(other.at[pl.ds(other_row + HALF * z, HALF)],
                     f_ref.at[z, pl.ds(pl.multiple_of(HALF - HALF * r, HALF), HALF)])


def parts_in(copies, r, p_ref, parts, rel, other, row, first=0):
    count = FIELDS - first
    copies.start(parts.at[4 * r + rel, pl.ds(first, count)], p_ref.at[r, pl.ds(first, count)])
    copies.start(other.at[pl.ds(row + first, count)], p_ref.at[1 - r, pl.ds(first, count)])


def piece_out(r, z_ref, q_ref, own, away):
    for half, dst in ((r, own), (1 - r, away)):
        for z in range(2):
            dst[HALF * z:HALF * z + HALF, :] = z_ref[z, pl.ds(pl.multiple_of(HALF * half, HALF), HALF), :]
        dst[2 * HALF:, :] = q_ref[half, :PUSHED, :]


def moves_out(moves, wave, *items):
    for ref, slot in items:
        moves.start(ref.at[pl.ds(0, N)], wave.at[pl.ds(slot * N, N)])


def near_kernel(wave, mine, near, table, d_ref, q_ref, f3, p2, tab, *rest):
    work, sems = rest[:-1], rest[-1]
    r = lax.axis_index("row")
    copies, later = Copies(sems), Copies(sems)
    later.used = 7
    field_in(copies, r, f3, wave, N * (4 * r + 1), near, 0)
    copies.start(mine, p2.at[r])
    copies.start(near.at[pl.ds(N, FIELDS)], p2.at[1 - r])
    later.start(table, tab)
    copies.wait()
    step(f3, p2, p2, tab, d_ref, *work, ready=later)
    q_ref[...] = p2[...]


def first_kernel(q2, wave, parts, swap, table, q_ref, own, away, f2, p1, pushed, z, tab, *rest):
    work, sems = rest[:-1], rest[-1]
    r = lax.axis_index("row")
    copies, later = Copies(sems), Copies(sems)
    later.used = 7
    field_in(copies, r, f2, wave, N * 4 * r, swap, 0)
    parts_in(copies, r, p1, parts, 1, swap, N + FIELDS)
    later.start(table, tab)
    copies.wait()
    step(f2, p1, p1, tab, z, *work, ready=later)
    q_ref[...] = p1[...]
    step(z, q2, pushed, tab, f2, *work)
    piece_out(r, f2, pushed, own, away)


def second_kernel(q1, parts, swap, link, following, table, q_ref, own, away, f1, p0, pushed, z, tab, *rest):
    work, sems = rest[:-1], rest[-1]
    r = lax.axis_index("row")
    copies, later = Copies(sems), Copies(sems)
    later.used = 7
    field_in(copies, r, f1, following, 0, link, 0)
    parts_in(copies, r, p0, parts, 0, swap, N)
    later.start(table, tab)
    copies.wait()

    @pl.when((r == 0) & (lax.axis_index("tm") == 0))
    def _():
        f1[...] = jnp.zeros_like(f1)

    step(f1, p0, p0, tab, z, *work, ready=later)
    q_ref[...] = p0[...]
    step(z, q1, pushed, tab, f1, *work)
    piece_out(r, f1, pushed, own, away)


def edge_kernel(after, chain, ahead, relay, table, d_ref, to_back, f0, pm, tab, *rest):
    work, sems = rest[:-1], rest[-1]
    r = lax.axis_index("row")
    copies, later = Copies(sems), Copies(sems)
    later.used = 15
    field_in(copies, r, f0, ahead, 0, chain, 0)
    copies.start(ahead.at[pl.ds(N, FIELDS)], pm.at[r])
    copies.start(chain.at[pl.ds(N, FIELDS)], pm.at[1 - r])
    later.start(table, tab)
    copies.wait()

    @pl.when((r == 0) & (lax.rem(lax.axis_index("tm"), lax.axis_size("tm") // 2) == 0))
    def _():
        again = Copies(sems)
        again.used = 8
        for z in range(2):
            again.start(relay.at[pl.ds(HALF * z, HALF)], f0.at[z, pl.ds(pl.multiple_of(HALF * r, HALF), HALF)])
        again.start(relay.at[pl.ds(N, FIELDS)], pm.at[r])
        again.wait()

    step(f0, pm, to_back, tab, d_ref, *work, ready=later)


def third_kernel(d_ref, q0, own_a, own_b, back_a, table, own, away, wave, f0, pushed, z, tab, *rest):
    work, sems = rest[:-1], rest[-1]
    r = lax.axis_index("row")
    copies, moves, later = Copies(sems), Copies(sems), Copies(sems)
    later.used = 11
    moves.used = 2
    copies.start(d_ref, f0)
    later.start(table, tab)
    moves_out(moves, wave, (own_a, 4 * r + 2), (own_b, 4 * r + 1), (back_a, 6 - 4 * r))
    copies.wait()

    @pl.when((r == 0) & (lax.axis_index("tm") == 0))
    def _():
        f0[...] = jnp.zeros_like(f0)

    step(f0, q0, pushed, tab, z, *work, ready=later)
    piece_out(r, z, pushed, own, away)
    moves.wait()


def fourth_kernel(d_ref, parts, swap, from_back, own_c, table, wave_in, own, away, wave,
                  p3, pushed, z, tab, *rest):
    work, sems = rest[:-1], rest[-1]
    r = lax.axis_index("row")
    copies, moves, later = Copies(sems), Copies(sems), Copies(sems)
    later.used = 11
    moves.used = 8
    parts_in(copies, r, p3, parts, 3, swap, N + 2 * FIELDS, PUSHED)
    copies.start(from_back, p3.at[:, pl.ds(0, PUSHED)])
    later.start(table, tab)
    moves_out(moves, wave, (own_c, 4 * r))
    copies.wait()
    step(d_ref, p3, pushed, tab, z, *work, ready=later)
    piece_out(r, z, pushed, own, away)
    moves.wait()


def late_kernel(own_a, own_b, own_c, own_d, back_a, back_b, back_c, wave_in, wave, phase, energy, packed, sems):
    r = lax.axis_index("row")
    own, other = 4 * r, 4 - 4 * r
    moves, copies = Copies(sems), Copies(sems)
    copies.used = 4
    for base, group in ((own, (own_a, own_b, own_c, own_d)), (other, (back_a, back_b, back_c, back_c))):
        for ref, slot in zip(group, (2, 1, 0, 3)):
            copies.start(ref.at[pl.ds(N, PUSHED)], packed.at[base + slot])
    moves_out(moves, wave, (back_b, other + 1), (back_c, other), (own_d, own + 3))
    copies.wait()
    for s in range(8):
        for k in range(ROWS):
            phase[s:s + 1, N * k:N * k + N] = packed[s, k:k + 1, :]
            energy[s:s + 1, N * k:N * k + N] = packed[s, ROWS + k:ROWS + k + 1, :]
    moves.wait()


def final_kernel(back_d, wave_in, phase_in, energy_in, wave, phase, energy, sems):
    r = lax.axis_index("row")
    last = 7 - 4 * r
    moves = Copies(sems)
    moves_out(moves, wave, (back_d, last))
    phase[...] = phase_in[...]
    energy[...] = energy_in[...]
    for k in range(ROWS):
        phase[pl.ds(last, 1), N * k:N * k + N] = back_d[N + k:N + k + 1, :]
        energy[pl.ds(last, 1), N * k:N * k + N] = back_d[N + ROWS + k:N + ROWS + k + 1, :]
    moves.wait()


def body(wavefront, particle_phase, particle_energy, row_offset, row_cell, col_cell):
    table = jnp.asarray(tables())
    r = lax.axis_index("row")
    nt = lax.axis_size("tm")
    both = BOTH
    swap = [(i, i ^ 1) for i in range(2 * nt)]
    chain = [(i, (i + 1) % (2 * nt)) for i in range(2 * nt)]
    far = [2 * t for t in range(nt) if (t + 1) % (nt // 2) == 0]
    ahead = [(i, i + 2 if i % 2 == 0 else i) for i in range(2 * nt) if i not in far]
    around = [(i, (i + 3) % (2 * nt)) for i in far]
    onward = [(j, j - 1) for i, j in around]
    direct = [(i, i + 2) for i in far if i + 2 < 2 * nt]
    back = [(j, i) for i, j in chain]
    wave = wavefront.reshape(8 * N, N)
    unit = 1 << 33

    full, field = (2, FIELDS, N), (2, N, N)
    pieces = [(PIECE, N), (PIECE, N)]
    raw = (wave, particle_phase, particle_energy, row_offset, row_cell, col_cell)
    stage = [pltpu.VMEM((3, 8, PART), F32), pltpu.VMEM((2, 8, PART), jnp.int32)]
    to_near, to_ahead, mine = call(
        early_pack_kernel, [(N + FIELDS, N), (N + FIELDS, N), (FIELDS, N)], [VM] * 3, stage, 8, [HB] * 6, 1 << 20,
        vmem=61000 << 10,
    )(*raw)
    f_near = lax.ppermute(to_near, both, swap)
    f_around = lax.ppermute(to_ahead, both, around)
    parts, to_swap, to_chain, to_link, to_next = call(
        pack_kernel, [(8, FIELDS, N), (N + 3 * FIELDS, N), (N + FIELDS, N), (N, N), (N, N)],
        [VM] * 5, stage, 12, [ANY] + [HB] * 6, 4 * unit, vmem=61000 << 10,
    )(to_near, *raw)
    f_swap = lax.ppermute(to_swap, both, swap)
    f_next = lax.ppermute(to_next, both, ahead + direct)

    d3, q2 = call(
        near_kernel, [field, full], [VM, VM], [FIELD, PARTS, TABLE] + WORK, 8, [ANY] * 4, unit, vmem=50000 << 10,
    )(wave, mine, f_near, table)
    q2, to_chain, to_link, to_ahead = lax.optimization_barrier((q2, to_chain, to_link, to_ahead))
    f_link = lax.ppermute(to_link, both, chain)
    f_chain = lax.ppermute(to_chain, both, chain)
    f_ahead = lax.ppermute(to_ahead, both, ahead)
    q1, own_a, away_a = call(
        first_kernel, [full] + pieces, [VM] * 3, [FIELD, PARTS, PUSH, FIELD, TABLE] + WORK, 8,
        [VM] + [ANY] * 4, 2 * unit,
    )(q2, wave, parts, f_swap, table)
    q1, f_around = lax.optimization_barrier((q1, f_around))
    f_relay = lax.ppermute(f_around, both, onward)
    back_a = lax.ppermute(away_a, both, swap)
    q0, own_b, away_b = call(
        second_kernel, [full] + pieces, [VM] * 3, [FIELD, PARTS, PUSH, FIELD, TABLE] + WORK, 8,
        [VM] + [ANY] * 5, 2 * unit,
    )(q1, parts, f_swap, f_link, f_next, table)
    back_b = lax.ppermute(away_b, both, swap)
    d0, to_back = call(
        edge_kernel, [field, (2, PUSHED, N)], [VM, VM], [FIELD, PARTS, TABLE] + WORK, 16, [ANY] * 5, unit,
    )(q0, f_chain, f_ahead, f_relay, table)
    from_back = lax.ppermute(to_back, both, back)
    own_c, away_c, wave = call(
        third_kernel, pieces + [(8 * N, N)], [VM, VM, ANY],
        [FIELD, PUSH, FIELD, TABLE] + WORK, 12, [ANY, VM] + [ANY] * 4, unit,
    )(d0, q0, own_a, own_b, back_a, table)
    back_c = lax.ppermute(away_c, both, swap)
    own_d, away_d, wave = call(
        fourth_kernel, pieces + [(8 * N, N)], [VM, VM, ANY],
        [PARTS, PUSH, FIELD, TABLE] + WORK, 12, [VM] + [ANY] * 6, 2 * unit, {6: 2},
    )(d3, parts, f_swap, from_back, own_c, table, wave)
    back_d = lax.ppermute(away_d, both, swap)
    particles = [(8, PART), (8, PART)]
    wave, phase, energy = call(
        late_kernel, [(8 * N, N)] + particles, [ANY, VM, VM], [pltpu.VMEM((8, PUSHED, N), F32)], 16,
        [ANY] * 8, 1 << 20, {7: 0},
    )(own_a, own_b, own_c, own_d, back_a, back_b, back_c, wave)
    wave, phase, energy = call(
        final_kernel, [(8 * N, N)] + particles, [HB, VM, VM], [], 4, [VM, HB, VM, VM], 1 << 20, {1: 0},
    )(back_d, wave, phase, energy)
    return wave.reshape(8, 2, HALF, N), phase, energy


def solution(mesh):
    P = jax.sharding.PartitionSpec
    wide, flat = P("tm", None, "row", None), P("tm", "row")
    return jax.shard_map(body, mesh=mesh, in_specs=(wide,) + (flat,) * 5,
                         out_specs=(wide, flat, flat), check_vma=False)
```

```python
import math

import jax
import jax.numpy as jnp
import ml_dtypes
import numpy as np
from jax import lax
from jax.experimental import pallas as pl
from jax.experimental.pallas import tpu as pltpu

BF = jnp.bfloat16
F32 = jnp.float32
F8 = jnp.float8_e5m2
UP = 1024.0
DOWN = 1.0 / UP
N = 256
HALF = 128
PART = 2048
ROWS = PART // N
WIN = 144
NEAR = 136
FIELDS = 5 * ROWS
PUSHED = 2 * ROWS
PIECE = 2 * HALF + PUSHED
BOTH = ("tm", "row")


def split_np(m):
    hi = m.astype(ml_dtypes.bfloat16)
    return hi, (m - hi.astype(np.float64)).astype(ml_dtypes.bfloat16)


def tables():
    k = np.arange(N)
    m = np.where(k < N // 2, k, k - N).astype(np.float64)
    h = np.exp(-1j * np.pi / N * m * m)
    dft = np.exp(-2j * np.pi / N * (k[:, None] * k[None, :] % N))
    a = (np.conj(dft) / N) @ (h[:, None] * dft)
    c0, c1 = a[:HALF, :HALF], a[:HALF, HALF:]
    both = [0.5 * (c0 + c1), 0.5 * (c0 - c1)]
    right = np.stack([np.block([[b.real, b.imag], [-b.imag, b.real]]) for b in both])
    left = np.stack([np.block([[b.real, -b.imag], [b.imag, b.real]]) for b in both])
    return np.stack(split_np(np.stack([right, left])))


def sincos(x):
    n = jnp.round(x * (1.0 / math.pi))
    r = x - n * 3.140625
    r = r - n * 9.670257568359375e-4
    r = r - n * 6.277114152908325e-07
    half = n * 0.5
    sign = 1.0 - 4.0 * (half - jnp.floor(half))
    y = r * r
    s = -2.3889859e-08
    for c in (2.7525562e-06, -1.98408740e-04, 8.33333310e-03, -1.66666667e-01):
        s = s * y + c
    s = r + r * y * s
    c = 2.08767570e-09 - 1.1470746e-11 * y
    for d in (-2.75573192e-07, 2.48015873e-05, -1.38888889e-03, 4.16666667e-02, -0.5, 1.0):
        c = c * y + d
    return s * sign, c * sign


def hilo(x):
    hi = x.astype(BF)
    return hi, (x - hi.astype(F32)).astype(BF)


def mm(a, b):
    return jnp.dot(a, b, preferred_element_type=F32)


def step(f_ref, p_ref, q_ref, tab, out_ref, c_ref, w_ref, s_ref, sr_ref, x_ref, samp_ref, c8_ref, sr8_ref, ready=None):
    iota_c = (lax.broadcasted_iota(jnp.int32, (16, 16, N), 0) * 16
              + lax.broadcasted_iota(jnp.int32, (16, 16, N), 1)).astype(F32).astype(BF)
    one = jnp.ones((16, N), BF)
    zero = jnp.zeros((16, N), BF)
    down = jnp.full((16, N), DOWN, BF)
    iota_r = lax.broadcasted_iota(jnp.int32, (NEAR, N), 0).astype(F32)
    phase = jnp.concatenate([p_ref[0, :ROWS], p_ref[1, :ROWS]], 0)
    sine, cosine = sincos(phase)
    for h in range(2):
        off = p_ref[h, 2 * ROWS:3 * ROWS]
        lower = 0.5 - off
        upper = 0.5 + off
        w_ref[h, 0] = 0.5 * lower * lower
        w_ref[h, 1] = 0.75 - off * off
        w_ref[h, 2] = 0.5 * upper * upper
        win0 = 0 if h == 0 else N - WIN
        skip = h * (WIN - NEAR)
        field = f_ref[:, win0:win0 + WIN, :].reshape(2 * WIN, N)
        both = jnp.concatenate(hilo(field), 0)
        for k in range(ROWS):
            col = jnp.broadcast_to(p_ref[h, 4 * ROWS + k:4 * ROWS + k + 1, :], (16, N)).astype(BF)
            hot = jnp.where(iota_c == col[None], one[None], zero[None]).reshape(N, N)
            c_ref[h, :, N * k:N * k + N] = hot
            hot8 = jnp.where(iota_c == col[None], down[None], zero[None]).reshape(N, N).astype(F8)
            c8_ref[h, :, N * k:N * k + N] = hot8
            g = mm(both, hot)
            g = g[:2 * WIN] + g[2 * WIN:]
            at = p_ref[h, 3 * ROWS + k:3 * ROWS + k + 1, :] - float(win0 + skip)
            w = jnp.where(iota_r == at, w_ref[h, 1, k:k + 1, :],
                          jnp.where(iota_r == at - 1.0, w_ref[h, 0, k:k + 1, :],
                                    jnp.where(iota_r == at + 1.0, w_ref[h, 2, k:k + 1, :], 0.0)))
            samp_ref[0, h * ROWS + k:h * ROWS + k + 1, :] = jnp.sum(w * g[skip:skip + NEAR], 0, keepdims=True)
            samp_ref[1, h * ROWS + k:h * ROWS + k + 1, :] = jnp.sum(
                w * g[WIN + skip:WIN + skip + NEAR], 0, keepdims=True)
    energy = jnp.concatenate([p_ref[0, ROWS:2 * ROWS], p_ref[1, ROWS:2 * ROWS]], 0)
    energy = energy - 0.5 * (samp_ref[0] * cosine - samp_ref[1] * sine)
    phase = phase + energy
    for h in range(2):
        q_ref[h, :ROWS] = phase[h * ROWS:h * ROWS + ROWS]
        q_ref[h, ROWS:2 * ROWS] = energy[h * ROWS:h * ROWS + ROWS]
    sine, cosine = sincos(phase)
    for z, v in ((0, cosine), (1, -sine)):
        vh = v.astype(BF).astype(F32)
        s_ref[2 * z] = vh
        s_ref[2 * z + 1] = (v - vh) * UP
    for h in range(2):
        for k in range(ROWS):
            at = jnp.broadcast_to(p_ref[h, 3 * ROWS + k:3 * ROWS + k + 1, :] - float(HALF * h), (16, N)).astype(BF)
            here = iota_c[:8] == at[None]
            row = h * ROWS + k
            for z in range(2):
                value = jnp.broadcast_to(s_ref[2 * z, row:row + 1, :], (16, N)).astype(BF)
                sr_ref[h, HALF * z:HALF * z + HALF, N * k:N * k + N] = jnp.where(here, value[None], zero[None]).reshape(HALF, N)
                value = jnp.broadcast_to(s_ref[2 * z + 1, row:row + 1, :], (16, N)).astype(BF)
                sr8_ref[h, HALF * z:HALF * z + HALF, N * k:N * k + N] = jnp.where(
                    here, value[None], zero[None]).reshape(HALF, N).astype(F8)
        d = lax.dot_general(sr8_ref[h], c8_ref[h], (((1,), (1,)), ((), ())), preferred_element_type=F32)
        d = d + lax.dot_general(sr_ref[h], c_ref[h], (((1,), (1,)), ((), ())), preferred_element_type=F32)
        for z in range(2):
            x_ref[HALF * h:HALF * h + HALF, N * z:N * z + N] = (
                f_ref[z, HALF * h:HALF * h + HALF, :] + d[HALF * z:HALF * z + HALF])
    if ready is not None:
        ready.wait()
    quads = [[], []]
    for z in range(2):
        top = x_ref[:HALF, N * z:N * z + N]
        low = x_ref[HALF:, N * z:N * z + N]
        rows = jnp.concatenate([top + low, top - low], 0)
        quads[0].append(rows[:, :HALF] + rows[:, HALF:])
        quads[1].append(rows[:, :HALF] - rows[:, HALF:])
    turned = []
    for e in range(2):
        xh, xl = hilo(jnp.concatenate(quads[e], 1))
        t = mm(jnp.concatenate([xh, xl], 0), tab[0, 0, e])
        turned.append(t[:N] + t[N:] + mm(xh, tab[1, 0, e]))
    halves = []
    for e in range(2):
        rows = slice(HALF * e, HALF * e + HALF)
        y = jnp.concatenate([jnp.concatenate([turned[0][rows, :HALF], turned[1][rows, :HALF]], 1),
                             jnp.concatenate([turned[0][rows, HALF:], turned[1][rows, HALF:]], 1)], 0)
        yh, yl = hilo(y)
        t = mm(jnp.concatenate([tab[0, 1, e], tab[1, 1, e]], 0), yh)
        halves.append(t[:N] + t[N:] + mm(tab[0, 1, e], yl))
    for e, rows in enumerate((halves[0] + halves[1], halves[0] - halves[1])):
        left, right = rows[:, :HALF], rows[:, HALF:]
        out = jnp.concatenate([left + right, left - right], 1)
        out_ref[0, HALF * e:HALF * e + HALF] = out[:HALF]
        out_ref[1, HALF * e:HALF * e + HALF] = out[HALF:]


WORK = [pltpu.VMEM((2, N, PART), BF), pltpu.VMEM((2, 3, ROWS, N), F32), pltpu.VMEM((4, 2 * ROWS, N), F32),
        pltpu.VMEM((2, N, PART), BF), pltpu.VMEM((N, 2 * N), F32), pltpu.VMEM((2, 2 * ROWS, N), F32),
        pltpu.VMEM((2, N, PART), F8), pltpu.VMEM((2, N, PART), F8)]
FIELD = pltpu.VMEM((2, N, N), F32)
PARTS = pltpu.VMEM((2, FIELDS, N), F32)
TABLE = pltpu.VMEM((2, 2, 2, N, N), BF)
PUSH = pltpu.VMEM((2, PUSHED, N), F32)
ANY = pl.BlockSpec(memory_space=pl.ANY)
VM = pl.BlockSpec(memory_space=pltpu.VMEM)
HB = pl.BlockSpec(memory_space=pltpu.HBM)


class Copies:
    def __init__(self, sems):
        self.sems = sems
        self.used = 0
        self.open = []

    def start(self, src, dst):
        copy = pltpu.make_async_copy(src, dst, self.sems.at[self.used])
        self.used += 1
        copy.start()
        self.open.append(copy)

    def wait(self):
        for copy in self.open:
            copy.wait()
        self.open = []


def call(kernel, outs, out_specs, scratch, copies, in_specs, flops, aliases={}, vmem=40 << 20):
    return pl.pallas_call(
        kernel, out_shape=[jax.ShapeDtypeStruct(s, F32) for s in outs], in_specs=in_specs, out_specs=out_specs,
        scratch_shapes=scratch + [pltpu.SemaphoreType.DMA((copies,))],
        input_output_aliases=aliases, cost_estimate=pl.CostEstimate(flops=flops, bytes_accessed=4 << 20, transcendentals=0),
        compiler_params=pltpu.CompilerParams(vmem_limit_bytes=vmem))


def load_all(copies, sources, floats, ints):
    for a, src in enumerate(sources):
        copies.start(src, floats.at[a] if a < 3 else ints.at[a - 3])


def pack_slice(floats, ints, index, dst, row):
    for a in range(5):
        src = floats.at[a] if a < 3 else ints.at[a - 3]
        for k in range(ROWS):
            at = row + a * ROWS + k
            dst[at:at + 1, :] = src[pl.ds(index, 1), N * k:N * k + N].astype(F32)


def early_pack_kernel(wave, *refs):
    sources, (near_ref, ahead_ref, mine_ref), (floats, ints, sems) = refs[:5], refs[5:8], refs[8:]
    r = lax.axis_index("row")
    loads, copies = Copies(sems), Copies(sems)
    copies.used = 5
    load_all(loads, sources, floats, ints)
    copies.start(wave.at[pl.ds(N * (5 - 4 * r), N)], near_ref.at[pl.ds(0, N)])
    copies.start(wave.at[pl.ds(N * (6 - 4 * r), N)], ahead_ref.at[pl.ds(0, N)])
    loads.wait()
    pack_slice(floats, ints, 6 - 4 * r, near_ref, N)
    pack_slice(floats, ints, 2 + 4 * r, mine_ref, 0)
    pack_slice(floats, ints, 7 - 4 * r, ahead_ref, N)
    copies.wait()


def pack_kernel(near, wave, *refs):
    sources, (all_ref, swap_ref, chain_ref, link_ref, next_ref), (floats, ints, sems) = refs[:5], refs[5:10], refs[10:]
    r = lax.axis_index("row")
    loads, copies = Copies(sems), Copies(sems)
    copies.used = 5
    load_all(loads, sources, floats, ints)
    copies.start(wave.at[pl.ds(N * (4 - 4 * r), N)], swap_ref.at[pl.ds(0, N)])
    copies.start(wave.at[pl.ds(N * (2 + 4 * r), N)], chain_ref.at[pl.ds(0, N)])
    copies.start(wave.at[pl.ds(N * (3 + 4 * r), N)], link_ref)
    copies.start(wave.at[pl.ds(N * (7 - 4 * r), N)], next_ref)
    loads.wait()
    for s in range(8):
        pack_slice(floats, ints, s, all_ref.at[s], 0)
    for i, rel in enumerate((0, 1, 3)):
        swap_ref[N + FIELDS * i:N + FIELDS * i + FIELDS, :] = all_ref[4 - 4 * r + rel]
    chain_ref[N:, :] = all_ref[3 + 4 * r]
    copies.wait()


def field_in(copies, r, f_ref, own, own_row, other, other_row):
    for z in range(2):
        copies.start(own.at[pl.ds(own_row + HALF * z, HALF)], f_ref.at[z, pl.ds(pl.multiple_of(HALF * r, HALF), HALF)])
        copies.start(other.at[pl.ds(other_row + HALF * z, HALF)],
                     f_ref.at[z, pl.ds(pl.multiple_of(HALF - HALF * r, HALF), HALF)])


def parts_in(copies, r, p_ref, parts, rel, other, row, first=0):
    count = FIELDS - first
    copies.start(parts.at[4 * r + rel, pl.ds(first, count)], p_ref.at[r, pl.ds(first, count)])
    copies.start(other.at[pl.ds(row + first, count)], p_ref.at[1 - r, pl.ds(first, count)])


def piece_out(r, z_ref, q_ref, own, away):
    for half, dst in ((r, own), (1 - r, away)):
        for z in range(2):
            dst[HALF * z:HALF * z + HALF, :] = z_ref[z, pl.ds(pl.multiple_of(HALF * half, HALF), HALF), :]
        dst[2 * HALF:, :] = q_ref[half, :PUSHED, :]


def moves_out(moves, wave, *items):
    for ref, slot in items:
        moves.start(ref.at[pl.ds(0, N)], wave.at[pl.ds(slot * N, N)])


def near_kernel(wave, mine, near, table, d_ref, q_ref, f3, p2, tab, *rest):
    work, sems = rest[:-1], rest[-1]
    r = lax.axis_index("row")
    copies, later = Copies(sems), Copies(sems)
    later.used = 7
    field_in(copies, r, f3, wave, N * (4 * r + 1), near, 0)
    copies.start(mine, p2.at[r])
    copies.start(near.at[pl.ds(N, FIELDS)], p2.at[1 - r])
    later.start(table, tab)
    copies.wait()
    step(f3, p2, p2, tab, d_ref, *work, ready=later)
    q_ref[...] = p2[...]


def first_kernel(q2, wave, parts, swap, table, q_ref, own, away, f2, p1, pushed, z, tab, *rest):
    work, sems = rest[:-1], rest[-1]
    r = lax.axis_index("row")
    copies, later = Copies(sems), Copies(sems)
    later.used = 7
    field_in(copies, r, f2, wave, N * 4 * r, swap, 0)
    parts_in(copies, r, p1, parts, 1, swap, N + FIELDS)
    later.start(table, tab)
    copies.wait()
    step(f2, p1, p1, tab, z, *work, ready=later)
    q_ref[...] = p1[...]
    step(z, q2, pushed, tab, f2, *work)
    piece_out(r, f2, pushed, own, away)


def second_kernel(q1, parts, swap, link, following, table, q_ref, own, away, f1, p0, pushed, z, tab, *rest):
    work, sems = rest[:-1], rest[-1]
    r = lax.axis_index("row")
    copies, later = Copies(sems), Copies(sems)
    later.used = 7
    field_in(copies, r, f1, following, 0, link, 0)
    parts_in(copies, r, p0, parts, 0, swap, N)
    later.start(table, tab)
    copies.wait()

    @pl.when((r == 0) & (lax.axis_index("tm") == 0))
    def _():
        f1[...] = jnp.zeros_like(f1)

    step(f1, p0, p0, tab, z, *work, ready=later)
    q_ref[...] = p0[...]
    step(z, q1, pushed, tab, f1, *work)
    piece_out(r, f1, pushed, own, away)


def edge_kernel(after, chain, ahead, relay, table, d_ref, to_back, f0, pm, tab, *rest):
    work, sems = rest[:-1], rest[-1]
    r = lax.axis_index("row")
    copies, later = Copies(sems), Copies(sems)
    later.used = 15
    field_in(copies, r, f0, ahead, 0, chain, 0)
    copies.start(ahead.at[pl.ds(N, FIELDS)], pm.at[r])
    copies.start(chain.at[pl.ds(N, FIELDS)], pm.at[1 - r])
    later.start(table, tab)
    copies.wait()

    @pl.when((r == 0) & (lax.rem(lax.axis_index("tm"), lax.axis_size("tm") // 2) == 0))
    def _():
        again = Copies(sems)
        again.used = 8
        for z in range(2):
            again.start(relay.at[pl.ds(HALF * z, HALF)], f0.at[z, pl.ds(pl.multiple_of(HALF * r, HALF), HALF)])
        again.start(relay.at[pl.ds(N, FIELDS)], pm.at[r])
        again.wait()

    step(f0, pm, to_back, tab, d_ref, *work, ready=later)


def third_kernel(d_ref, q0, own_a, own_b, back_a, table, own, away, wave, f0, pushed, z, tab, *rest):
    work, sems = rest[:-1], rest[-1]
    r = lax.axis_index("row")
    copies, moves, later = Copies(sems), Copies(sems), Copies(sems)
    later.used = 11
    moves.used = 2
    copies.start(d_ref, f0)
    later.start(table, tab)
    moves_out(moves, wave, (own_a, 4 * r + 2), (own_b, 4 * r + 1), (back_a, 6 - 4 * r))
    copies.wait()

    @pl.when((r == 0) & (lax.axis_index("tm") == 0))
    def _():
        f0[...] = jnp.zeros_like(f0)

    step(f0, q0, pushed, tab, z, *work, ready=later)
    piece_out(r, z, pushed, own, away)
    moves.wait()


def fourth_kernel(d_ref, parts, swap, from_back, own_c, table, wave_in, own, away, wave,
                  p3, pushed, z, tab, *rest):
    work, sems = rest[:-1], rest[-1]
    r = lax.axis_index("row")
    copies, moves, later = Copies(sems), Copies(sems), Copies(sems)
    later.used = 11
    moves.used = 8
    parts_in(copies, r, p3, parts, 3, swap, N + 2 * FIELDS, PUSHED)
    copies.start(from_back, p3.at[:, pl.ds(0, PUSHED)])
    later.start(table, tab)
    moves_out(moves, wave, (own_c, 4 * r))
    copies.wait()
    step(d_ref, p3, pushed, tab, z, *work, ready=later)
    piece_out(r, z, pushed, own, away)
    moves.wait()


def late_kernel(own_a, own_b, own_c, own_d, back_a, back_b, back_c, wave_in, wave, phase, energy, packed, sems):
    r = lax.axis_index("row")
    own, other = 4 * r, 4 - 4 * r
    moves, copies = Copies(sems), Copies(sems)
    copies.used = 4
    for base, group in ((own, (own_a, own_b, own_c, own_d)), (other, (back_a, back_b, back_c, back_c))):
        for ref, slot in zip(group, (2, 1, 0, 3)):
            copies.start(ref.at[pl.ds(N, PUSHED)], packed.at[base + slot])
    moves_out(moves, wave, (back_b, other + 1), (back_c, other), (own_d, own + 3))
    copies.wait()
    for s in range(8):
        for k in range(ROWS):
            phase[s:s + 1, N * k:N * k + N] = packed[s, k:k + 1, :]
            energy[s:s + 1, N * k:N * k + N] = packed[s, ROWS + k:ROWS + k + 1, :]
    moves.wait()


def final_kernel(back_d, wave_in, phase_in, energy_in, wave, phase, energy, sems):
    r = lax.axis_index("row")
    last = 7 - 4 * r
    moves = Copies(sems)
    moves_out(moves, wave, (back_d, last))
    phase[...] = phase_in[...]
    energy[...] = energy_in[...]
    for k in range(ROWS):
        phase[pl.ds(last, 1), N * k:N * k + N] = back_d[N + k:N + k + 1, :]
        energy[pl.ds(last, 1), N * k:N * k + N] = back_d[N + ROWS + k:N + ROWS + k + 1, :]
    moves.wait()


def body(wavefront, particle_phase, particle_energy, row_offset, row_cell, col_cell):
    table = jnp.asarray(tables())
    r = lax.axis_index("row")
    nt = lax.axis_size("tm")
    both = BOTH
    swap = [(i, i ^ 1) for i in range(2 * nt)]
    chain = [(i, (i + 1) % (2 * nt)) for i in range(2 * nt)]
    far = [2 * t for t in range(nt) if (t + 1) % (nt // 2) == 0]
    ahead = [(i, i + 2 if i % 2 == 0 else i) for i in range(2 * nt) if i not in far]
    around = [(i, (i + 3) % (2 * nt)) for i in far]
    onward = [(j, j - 1) for i, j in around]
    direct = [(i, i + 2) for i in far if i + 2 < 2 * nt]
    back = [(j, i) for i, j in chain]
    wave = wavefront.reshape(8 * N, N)
    unit = 1 << 33

    full, field = (2, FIELDS, N), (2, N, N)
    pieces = [(PIECE, N), (PIECE, N)]
    raw = (wave, particle_phase, particle_energy, row_offset, row_cell, col_cell)
    stage = [pltpu.VMEM((3, 8, PART), F32), pltpu.VMEM((2, 8, PART), jnp.int32)]
    to_near, to_ahead, mine = call(
        early_pack_kernel, [(N + FIELDS, N), (N + FIELDS, N), (FIELDS, N)], [VM] * 3, stage, 8, [HB] * 6, 1 << 20,
        vmem=61000 << 10,
    )(*raw)
    f_near = lax.ppermute(to_near, both, swap)
    f_around = lax.ppermute(to_ahead, both, around)
    parts, to_swap, to_chain, to_link, to_next = call(
        pack_kernel, [(8, FIELDS, N), (N + 3 * FIELDS, N), (N + FIELDS, N), (N, N), (N, N)],
        [VM] * 5, stage, 12, [ANY] + [HB] * 6, 4 * unit, vmem=61000 << 10,
    )(to_near, *raw)
    f_swap = lax.ppermute(to_swap, both, swap)

    d3, q2 = call(
        near_kernel, [field, full], [VM, VM], [FIELD, PARTS, TABLE] + WORK, 8, [ANY] * 4, unit, vmem=50000 << 10,
    )(wave, mine, f_near, table)
    q2, to_chain, to_link, to_next = lax.optimization_barrier((q2, to_chain, to_link, to_next))
    f_next = lax.ppermute(to_next, both, ahead + direct)
    f_link = lax.ppermute(to_link, both, chain)
    f_chain = lax.ppermute(to_chain, both, chain)
    q1, own_a, away_a = call(
        first_kernel, [full] + pieces, [VM] * 3, [FIELD, PARTS, PUSH, FIELD, TABLE] + WORK, 8,
        [VM] + [ANY] * 4, 2 * unit,
    )(q2, wave, parts, f_swap, table)
    q1, f_around, to_ahead = lax.optimization_barrier((q1, f_around, to_ahead))
    f_ahead = lax.ppermute(to_ahead, both, ahead)
    f_relay = lax.ppermute(f_around, both, onward)
    back_a = lax.ppermute(away_a, both, swap)
    q0, own_b, away_b = call(
        second_kernel, [full] + pieces, [VM] * 3, [FIELD, PARTS, PUSH, FIELD, TABLE] + WORK, 8,
        [VM] + [ANY] * 5, 2 * unit,
    )(q1, parts, f_swap, f_link, f_next, table)
    back_b = lax.ppermute(away_b, both, swap)
    d0, to_back = call(
        edge_kernel, [field, (2, PUSHED, N)], [VM, VM], [FIELD, PARTS, TABLE] + WORK, 16, [ANY] * 5, unit,
    )(q0, f_chain, f_ahead, f_relay, table)
    from_back = lax.ppermute(to_back, both, back)
    own_c, away_c, wave = call(
        third_kernel, pieces + [(8 * N, N)], [VM, VM, ANY],
        [FIELD, PUSH, FIELD, TABLE] + WORK, 12, [ANY, VM] + [ANY] * 4, unit,
    )(d0, q0, own_a, own_b, back_a, table)
    back_c = lax.ppermute(away_c, both, swap)
    own_d, away_d, wave = call(
        fourth_kernel, pieces + [(8 * N, N)], [VM, VM, ANY],
        [PARTS, PUSH, FIELD, TABLE] + WORK, 12, [VM] + [ANY] * 6, 2 * unit, {6: 2},
    )(d3, parts, f_swap, from_back, own_c, table, wave)
    back_d = lax.ppermute(away_d, both, swap)
    particles = [(8, PART), (8, PART)]
    wave, phase, energy = call(
        late_kernel, [(8 * N, N)] + particles, [ANY, VM, VM], [pltpu.VMEM((8, PUSHED, N), F32)], 16,
        [ANY] * 8, 1 << 20, {7: 0},
    )(own_a, own_b, own_c, own_d, back_a, back_b, back_c, wave)
    wave, phase, energy = call(
        final_kernel, [(8 * N, N)] + particles, [HB, VM, VM], [], 4, [VM, HB, VM, VM], 1 << 20, {1: 0},
    )(back_d, wave, phase, energy)
    return wave.reshape(8, 2, HALF, N), phase, energy


def solution(mesh):
    P = jax.sharding.PartitionSpec
    wide, flat = P("tm", None, "row", None), P("tm", "row")
    return jax.shard_map(body, mesh=mesh, in_specs=(wide,) + (flat,) * 5,
                         out_specs=(wide, flat, flat), check_vma=False)
```

```python
import math

import jax
import jax.numpy as jnp
import ml_dtypes
import numpy as np
from jax import lax
from jax.experimental import pallas as pl
from jax.experimental.pallas import tpu as pltpu

BF = jnp.bfloat16
F32 = jnp.float32
F8 = jnp.float8_e5m2
UP = 1024.0
DOWN = 1.0 / UP
N = 256
HALF = 128
PART = 2048
ROWS = PART // N
WIN = 144
NEAR = 136
FIELDS = 5 * ROWS
PUSHED = 2 * ROWS
PIECE = 2 * HALF + PUSHED
BOTH = ("tm", "row")


def split_np(m):
    hi = m.astype(ml_dtypes.bfloat16)
    return hi, (m - hi.astype(np.float64)).astype(ml_dtypes.bfloat16)


def tables():
    k = np.arange(N)
    m = np.where(k < N // 2, k, k - N).astype(np.float64)
    h = np.exp(-1j * np.pi / N * m * m)
    dft = np.exp(-2j * np.pi / N * (k[:, None] * k[None, :] % N))
    a = (np.conj(dft) / N) @ (h[:, None] * dft)
    c0, c1 = a[:HALF, :HALF], a[:HALF, HALF:]
    both = [0.5 * (c0 + c1), 0.5 * (c0 - c1)]
    right = np.stack([np.block([[b.real, b.imag], [-b.imag, b.real]]) for b in both])
    left = np.stack([np.block([[b.real, -b.imag], [b.imag, b.real]]) for b in both])
    return np.stack(split_np(np.stack([right, left])))


def sincos(x):
    n = jnp.round(x * (1.0 / math.pi))
    r = x - n * 3.140625
    r = r - n * 9.670257568359375e-4
    r = r - n * 6.277114152908325e-07
    half = n * 0.5
    sign = 1.0 - 4.0 * (half - jnp.floor(half))
    y = r * r
    s = -2.3889859e-08
    for c in (2.7525562e-06, -1.98408740e-04, 8.33333310e-03, -1.66666667e-01):
        s = s * y + c
    s = r + r * y * s
    c = 2.08767570e-09 - 1.1470746e-11 * y
    for d in (-2.75573192e-07, 2.48015873e-05, -1.38888889e-03, 4.16666667e-02, -0.5, 1.0):
        c = c * y + d
    return s * sign, c * sign


def hilo(x):
    hi = x.astype(BF)
    return hi, (x - hi.astype(F32)).astype(BF)


def mm(a, b):
    return jnp.dot(a, b, preferred_element_type=F32)


def step(f_ref, p_ref, q_ref, tab, out_ref, c_ref, w_ref, s_ref, sr_ref, x_ref, samp_ref, c8_ref, sr8_ref, ready=None):
    iota_c = (lax.broadcasted_iota(jnp.int32, (16, 16, N), 0) * 16
              + lax.broadcasted_iota(jnp.int32, (16, 16, N), 1)).astype(F32).astype(BF)
    one = jnp.ones((16, N), BF)
    zero = jnp.zeros((16, N), BF)
    down = jnp.full((16, N), DOWN, BF)
    iota_r = lax.broadcasted_iota(jnp.int32, (NEAR, N), 0).astype(F32)
    phase = jnp.concatenate([p_ref[0, :ROWS], p_ref[1, :ROWS]], 0)
    sine, cosine = sincos(phase)
    for h in range(2):
        off = p_ref[h, 2 * ROWS:3 * ROWS]
        lower = 0.5 - off
        upper = 0.5 + off
        w_ref[h, 0] = 0.5 * lower * lower
        w_ref[h, 1] = 0.75 - off * off
        w_ref[h, 2] = 0.5 * upper * upper
        win0 = 0 if h == 0 else N - WIN
        skip = h * (WIN - NEAR)
        field = f_ref[:, win0:win0 + WIN, :].reshape(2 * WIN, N)
        both = jnp.concatenate(hilo(field), 0)
        for k in range(ROWS):
            col = jnp.broadcast_to(p_ref[h, 4 * ROWS + k:4 * ROWS + k + 1, :], (16, N)).astype(BF)
            hot = jnp.where(iota_c == col[None], one[None], zero[None]).reshape(N, N)
            c_ref[h, :, N * k:N * k + N] = hot
            hot8 = jnp.where(iota_c == col[None], down[None], zero[None]).reshape(N, N).astype(F8)
            c8_ref[h, :, N * k:N * k + N] = hot8
            g = mm(both, hot)
            g = g[:2 * WIN] + g[2 * WIN:]
            at = p_ref[h, 3 * ROWS + k:3 * ROWS + k + 1, :] - float(win0 + skip)
            w = jnp.where(iota_r == at, w_ref[h, 1, k:k + 1, :],
                          jnp.where(iota_r == at - 1.0, w_ref[h, 0, k:k + 1, :],
                                    jnp.where(iota_r == at + 1.0, w_ref[h, 2, k:k + 1, :], 0.0)))
            samp_ref[0, h * ROWS + k:h * ROWS + k + 1, :] = jnp.sum(w * g[skip:skip + NEAR], 0, keepdims=True)
            samp_ref[1, h * ROWS + k:h * ROWS + k + 1, :] = jnp.sum(
                w * g[WIN + skip:WIN + skip + NEAR], 0, keepdims=True)
    energy = jnp.concatenate([p_ref[0, ROWS:2 * ROWS], p_ref[1, ROWS:2 * ROWS]], 0)
    energy = energy - 0.5 * (samp_ref[0] * cosine - samp_ref[1] * sine)
    phase = phase + energy
    for h in range(2):
        q_ref[h, :ROWS] = phase[h * ROWS:h * ROWS + ROWS]
        q_ref[h, ROWS:2 * ROWS] = energy[h * ROWS:h * ROWS + ROWS]
    sine, cosine = sincos(phase)
    for z, v in ((0, cosine), (1, -sine)):
        vh = v.astype(BF).astype(F32)
        s_ref[2 * z] = vh
        s_ref[2 * z + 1] = (v - vh) * UP
    for h in range(2):
        for k in range(ROWS):
            at = jnp.broadcast_to(p_ref[h, 3 * ROWS + k:3 * ROWS + k + 1, :] - float(HALF * h), (16, N)).astype(BF)
            here = iota_c[:8] == at[None]
            row = h * ROWS + k
            for z in range(2):
                value = jnp.broadcast_to(s_ref[2 * z, row:row + 1, :], (16, N)).astype(BF)
                sr_ref[h, HALF * z:HALF * z + HALF, N * k:N * k + N] = jnp.where(here, value[None], zero[None]).reshape(HALF, N)
                value = jnp.broadcast_to(s_ref[2 * z + 1, row:row + 1, :], (16, N)).astype(BF)
                sr8_ref[h, HALF * z:HALF * z + HALF, N * k:N * k + N] = jnp.where(
                    here, value[None], zero[None]).reshape(HALF, N).astype(F8)
        d = lax.dot_general(sr8_ref[h], c8_ref[h], (((1,), (1,)), ((), ())), preferred_element_type=F32)
        d = d + lax.dot_general(sr_ref[h], c_ref[h], (((1,), (1,)), ((), ())), preferred_element_type=F32)
        for z in range(2):
            x_ref[HALF * h:HALF * h + HALF, N * z:N * z + N] = (
                f_ref[z, HALF * h:HALF * h + HALF, :] + d[HALF * z:HALF * z + HALF])
    if ready is not None:
        ready.wait()
    quads = [[], []]
    for z in range(2):
        top = x_ref[:HALF, N * z:N * z + N]
        low = x_ref[HALF:, N * z:N * z + N]
        rows = jnp.concatenate([top + low, top - low], 0)
        quads[0].append(rows[:, :HALF] + rows[:, HALF:])
        quads[1].append(rows[:, :HALF] - rows[:, HALF:])
    turned = []
    for e in range(2):
        xh, xl = hilo(jnp.concatenate(quads[e], 1))
        t = mm(jnp.concatenate([xh, xl], 0), tab[0, 0, e])
        turned.append(t[:N] + t[N:] + mm(xh, tab[1, 0, e]))
    halves = []
    for e in range(2):
        rows = slice(HALF * e, HALF * e + HALF)
        y = jnp.concatenate([jnp.concatenate([turned[0][rows, :HALF], turned[1][rows, :HALF]], 1),
                             jnp.concatenate([turned[0][rows, HALF:], turned[1][rows, HALF:]], 1)], 0)
        yh, yl = hilo(y)
        t = mm(jnp.concatenate([tab[0, 1, e], tab[1, 1, e]], 0), yh)
        halves.append(t[:N] + t[N:] + mm(tab[0, 1, e], yl))
    for e, rows in enumerate((halves[0] + halves[1], halves[0] - halves[1])):
        left, right = rows[:, :HALF], rows[:, HALF:]
        out = jnp.concatenate([left + right, left - right], 1)
        out_ref[0, HALF * e:HALF * e + HALF] = out[:HALF]
        out_ref[1, HALF * e:HALF * e + HALF] = out[HALF:]


WORK = [pltpu.VMEM((2, N, PART), BF), pltpu.VMEM((2, 3, ROWS, N), F32), pltpu.VMEM((4, 2 * ROWS, N), F32),
        pltpu.VMEM((2, N, PART), BF), pltpu.VMEM((N, 2 * N), F32), pltpu.VMEM((2, 2 * ROWS, N), F32),
        pltpu.VMEM((2, N, PART), F8), pltpu.VMEM((2, N, PART), F8)]
FIELD = pltpu.VMEM((2, N, N), F32)
PARTS = pltpu.VMEM((2, FIELDS, N), F32)
TABLE = pltpu.VMEM((2, 2, 2, N, N), BF)
PUSH = pltpu.VMEM((2, PUSHED, N), F32)
ANY = pl.BlockSpec(memory_space=pl.ANY)
VM = pl.BlockSpec(memory_space=pltpu.VMEM)
HB = pl.BlockSpec(memory_space=pltpu.HBM)


class Copies:
    def __init__(self, sems):
        self.sems = sems
        self.used = 0
        self.open = []

    def start(self, src, dst):
        copy = pltpu.make_async_copy(src, dst, self.sems.at[self.used])
        self.used += 1
        copy.start()
        self.open.append(copy)

    def wait(self):
        for copy in self.open:
            copy.wait()
        self.open = []


def call(kernel, outs, out_specs, scratch, copies, in_specs, flops, aliases={}, vmem=40 << 20):
    return pl.pallas_call(
        kernel, out_shape=[jax.ShapeDtypeStruct(s, F32) for s in outs], in_specs=in_specs, out_specs=out_specs,
        scratch_shapes=scratch + [pltpu.SemaphoreType.DMA((copies,))],
        input_output_aliases=aliases, cost_estimate=pl.CostEstimate(flops=flops, bytes_accessed=4 << 20, transcendentals=0),
        compiler_params=pltpu.CompilerParams(vmem_limit_bytes=vmem))


def load_all(copies, sources, floats, ints):
    for a, src in enumerate(sources):
        copies.start(src, floats.at[a] if a < 3 else ints.at[a - 3])


def pack_slice(floats, ints, index, dst, row):
    for a in range(5):
        src = floats.at[a] if a < 3 else ints.at[a - 3]
        for k in range(ROWS):
            at = row + a * ROWS + k
            dst[at:at + 1, :] = src[pl.ds(index, 1), N * k:N * k + N].astype(F32)


def early_pack_kernel(wave, *refs):
    sources, (near_ref, ahead_ref, mine_ref), (floats, ints, sems) = refs[:5], refs[5:8], refs[8:]
    r = lax.axis_index("row")
    loads, copies = Copies(sems), Copies(sems)
    copies.used = 5
    load_all(loads, sources, floats, ints)
    copies.start(wave.at[pl.ds(N * (5 - 4 * r), N)], near_ref.at[pl.ds(0, N)])
    copies.start(wave.at[pl.ds(N * (6 - 4 * r), N)], ahead_ref.at[pl.ds(0, N)])
    loads.wait()
    pack_slice(floats, ints, 6 - 4 * r, near_ref, N)
    pack_slice(floats, ints, 2 + 4 * r, mine_ref, 0)
    pack_slice(floats, ints, 7 - 4 * r, ahead_ref, N)
    copies.wait()


def pack_kernel(near, wave, *refs):
    sources, (all_ref, swap_ref, chain_ref, link_ref, next_ref), (floats, ints, sems) = refs[:5], refs[5:10], refs[10:]
    r = lax.axis_index("row")
    loads, copies = Copies(sems), Copies(sems)
    copies.used = 5
    load_all(loads, sources, floats, ints)
    copies.start(wave.at[pl.ds(N * (4 - 4 * r), N)], swap_ref.at[pl.ds(0, N)])
    copies.start(wave.at[pl.ds(N * (2 + 4 * r), N)], chain_ref.at[pl.ds(0, N)])
    copies.start(wave.at[pl.ds(N * (3 + 4 * r), N)], link_ref)
    copies.start(wave.at[pl.ds(N * (7 - 4 * r), N)], next_ref)
    loads.wait()
    for s in range(8):
        pack_slice(floats, ints, s, all_ref.at[s], 0)
    for i, rel in enumerate((0, 1, 3)):
        swap_ref[N + FIELDS * i:N + FIELDS * i + FIELDS, :] = all_ref[4 - 4 * r + rel]
    chain_ref[N:, :] = all_ref[3 + 4 * r]
    copies.wait()


def field_in(copies, r, f_ref, own, own_row, other, other_row):
    for z in range(2):
        copies.start(own.at[pl.ds(own_row + HALF * z, HALF)], f_ref.at[z, pl.ds(pl.multiple_of(HALF * r, HALF), HALF)])
        copies.start(other.at[pl.ds(other_row + HALF * z, HALF)],
                     f_ref.at[z, pl.ds(pl.multiple_of(HALF - HALF * r, HALF), HALF)])


def parts_in(copies, r, p_ref, parts, rel, other, row, first=0):
    count = FIELDS - first
    copies.start(parts.at[4 * r + rel, pl.ds(first, count)], p_ref.at[r, pl.ds(first, count)])
    copies.start(other.at[pl.ds(row + first, count)], p_ref.at[1 - r, pl.ds(first, count)])


def piece_out(r, z_ref, q_ref, own, away):
    for half, dst in ((r, own), (1 - r, away)):
        for z in range(2):
            dst[HALF * z:HALF * z + HALF, :] = z_ref[z, pl.ds(pl.multiple_of(HALF * half, HALF), HALF), :]
        dst[2 * HALF:, :] = q_ref[half, :PUSHED, :]


def moves_out(moves, wave, *items):
    for ref, slot in items:
        moves.start(ref.at[pl.ds(0, N)], wave.at[pl.ds(slot * N, N)])


def near_kernel(wave, mine, near, table, d_ref, q_ref, f3, p2, tab, *rest):
    work, sems = rest[:-1], rest[-1]
    r = lax.axis_index("row")
    copies, later = Copies(sems), Copies(sems)
    later.used = 7
    field_in(copies, r, f3, wave, N * (4 * r + 1), near, 0)
    copies.start(mine, p2.at[r])
    copies.start(near.at[pl.ds(N, FIELDS)], p2.at[1 - r])
    later.start(table, tab)
    copies.wait()
    step(f3, p2, p2, tab, d_ref, *work, ready=later)
    q_ref[...] = p2[...]


def first_kernel(q2, wave, parts, swap, table, q_ref, own, away, f2, p1, pushed, z, tab, *rest):
    work, sems = rest[:-1], rest[-1]
    r = lax.axis_index("row")
    copies, later = Copies(sems), Copies(sems)
    later.used = 7
    field_in(copies, r, f2, wave, N * 4 * r, swap, 0)
    parts_in(copies, r, p1, parts, 1, swap, N + FIELDS)
    later.start(table, tab)
    copies.wait()
    step(f2, p1, p1, tab, z, *work, ready=later)
    q_ref[...] = p1[...]
    step(z, q2, pushed, tab, f2, *work)
    piece_out(r, f2, pushed, own, away)


def second_kernel(q1, parts, swap, link, following, straight, table, q_ref, own, away, f1, p0, pushed, z, tab, *rest):
    work, sems = rest[:-1], rest[-1]
    r = lax.axis_index("row")
    copies, later = Copies(sems), Copies(sems)
    later.used = 7
    field_in(copies, r, f1, following, 0, link, 0)
    parts_in(copies, r, p0, parts, 0, swap, N)
    later.start(table, tab)
    copies.wait()

    @pl.when((r == 0) & (lax.axis_index("tm") == lax.axis_size("tm") // 2))
    def _():
        again = Copies(sems)
        again.used = 8
        for zz in range(2):
            again.start(straight.at[pl.ds(HALF * zz, HALF)], f1.at[zz, pl.ds(pl.multiple_of(HALF * r, HALF), HALF)])
        again.wait()

    @pl.when((r == 0) & (lax.axis_index("tm") == 0))
    def _():
        f1[...] = jnp.zeros_like(f1)

    step(f1, p0, p0, tab, z, *work, ready=later)
    q_ref[...] = p0[...]
    step(z, q1, pushed, tab, f1, *work)
    piece_out(r, f1, pushed, own, away)


def edge_kernel(after, chain, ahead, relay, table, d_ref, to_back, f0, pm, tab, *rest):
    work, sems = rest[:-1], rest[-1]
    r = lax.axis_index("row")
    copies, later = Copies(sems), Copies(sems)
    later.used = 15
    field_in(copies, r, f0, ahead, 0, chain, 0)
    copies.start(ahead.at[pl.ds(N, FIELDS)], pm.at[r])
    copies.start(chain.at[pl.ds(N, FIELDS)], pm.at[1 - r])
    later.start(table, tab)
    copies.wait()

    @pl.when((r == 0) & (lax.rem(lax.axis_index("tm"), lax.axis_size("tm") // 2) == 0))
    def _():
        again = Copies(sems)
        again.used = 8
        for z in range(2):
            again.start(relay.at[pl.ds(HALF * z, HALF)], f0.at[z, pl.ds(pl.multiple_of(HALF * r, HALF), HALF)])
        again.start(relay.at[pl.ds(N, FIELDS)], pm.at[r])
        again.wait()

    step(f0, pm, to_back, tab, d_ref, *work, ready=later)


def third_kernel(d_ref, q0, own_a, own_b, back_a, table, own, away, wave, f0, pushed, z, tab, *rest):
    work, sems = rest[:-1], rest[-1]
    r = lax.axis_index("row")
    copies, moves, later = Copies(sems), Copies(sems), Copies(sems)
    later.used = 11
    moves.used = 2
    copies.start(d_ref, f0)
    later.start(table, tab)
    moves_out(moves, wave, (own_a, 4 * r + 2), (own_b, 4 * r + 1), (back_a, 6 - 4 * r))
    copies.wait()

    @pl.when((r == 0) & (lax.axis_index("tm") == 0))
    def _():
        f0[...] = jnp.zeros_like(f0)

    step(f0, q0, pushed, tab, z, *work, ready=later)
    piece_out(r, z, pushed, own, away)
    moves.wait()


def fourth_kernel(d_ref, parts, swap, from_back, own_c, table, wave_in, own, away, wave,
                  p3, pushed, z, tab, *rest):
    work, sems = rest[:-1], rest[-1]
    r = lax.axis_index("row")
    copies, moves, later = Copies(sems), Copies(sems), Copies(sems)
    later.used = 11
    moves.used = 8
    parts_in(copies, r, p3, parts, 3, swap, N + 2 * FIELDS, PUSHED)
    copies.start(from_back, p3.at[:, pl.ds(0, PUSHED)])
    later.start(table, tab)
    moves_out(moves, wave, (own_c, 4 * r))
    copies.wait()
    step(d_ref, p3, pushed, tab, z, *work, ready=later)
    piece_out(r, z, pushed, own, away)
    moves.wait()


def late_kernel(own_a, own_b, own_c, own_d, back_a, back_b, back_c, wave_in, wave, phase, energy, packed, sems):
    r = lax.axis_index("row")
    own, other = 4 * r, 4 - 4 * r
    moves, copies = Copies(sems), Copies(sems)
    copies.used = 4
    for base, group in ((own, (own_a, own_b, own_c, own_d)), (other, (back_a, back_b, back_c, back_c))):
        for ref, slot in zip(group, (2, 1, 0, 3)):
            copies.start(ref.at[pl.ds(N, PUSHED)], packed.at[base + slot])
    moves_out(moves, wave, (back_b, other + 1), (back_c, other), (own_d, own + 3))
    copies.wait()
    for s in range(8):
        for k in range(ROWS):
            phase[s:s + 1, N * k:N * k + N] = packed[s, k:k + 1, :]
            energy[s:s + 1, N * k:N * k + N] = packed[s, ROWS + k:ROWS + k + 1, :]
    moves.wait()


def final_kernel(back_d, wave_in, phase_in, energy_in, wave, phase, energy, sems):
    r = lax.axis_index("row")
    last = 7 - 4 * r
    moves = Copies(sems)
    moves_out(moves, wave, (back_d, last))
    phase[...] = phase_in[...]
    energy[...] = energy_in[...]
    for k in range(ROWS):
        phase[pl.ds(last, 1), N * k:N * k + N] = back_d[N + k:N + k + 1, :]
        energy[pl.ds(last, 1), N * k:N * k + N] = back_d[N + ROWS + k:N + ROWS + k + 1, :]
    moves.wait()


def body(wavefront, particle_phase, particle_energy, row_offset, row_cell, col_cell):
    table = jnp.asarray(tables())
    r = lax.axis_index("row")
    nt = lax.axis_size("tm")
    both = BOTH
    swap = [(i, i ^ 1) for i in range(2 * nt)]
    chain = [(i, (i + 1) % (2 * nt)) for i in range(2 * nt)]
    far = [2 * t for t in range(nt) if (t + 1) % (nt // 2) == 0]
    ahead = [(i, i + 2 if i % 2 == 0 else i) for i in range(2 * nt) if i not in far]
    around = [(i, (i + 3) % (2 * nt)) for i in far]
    onward = [(j, j - 1) for i, j in around]
    direct = [(i, i + 2) for i in far if i + 2 < 2 * nt]
    back = [(j, i) for i, j in chain]
    wave = wavefront.reshape(8 * N, N)
    unit = 1 << 33

    full, field = (2, FIELDS, N), (2, N, N)
    pieces = [(PIECE, N), (PIECE, N)]
    raw = (wave, particle_phase, particle_energy, row_offset, row_cell, col_cell)
    stage = [pltpu.VMEM((3, 8, PART), F32), pltpu.VMEM((2, 8, PART), jnp.int32)]
    to_near, to_ahead, mine = call(
        early_pack_kernel, [(N + FIELDS, N), (N + FIELDS, N), (FIELDS, N)], [VM] * 3, stage, 8, [HB] * 6, 1 << 20,
        vmem=61000 << 10,
    )(*raw)
    f_near = lax.ppermute(to_near, both, swap)
    f_around = lax.ppermute(to_ahead, both, around)
    parts, to_swap, to_chain, to_link, to_next = call(
        pack_kernel, [(8, FIELDS, N), (N + 3 * FIELDS, N), (N + FIELDS, N), (N, N), (N, N)],
        [VM] * 5, stage, 12, [ANY] + [HB] * 6, 4 * unit, vmem=61000 << 10,
    )(to_near, *raw)
    f_swap = lax.ppermute(to_swap, both, swap)
    f_next = lax.ppermute(to_next, both, ahead)

    d3, q2 = call(
        near_kernel, [field, full], [VM, VM], [FIELD, PARTS, TABLE] + WORK, 8, [ANY] * 4, unit, vmem=50000 << 10,
    )(wave, mine, f_near, table)
    q2, to_chain, to_link, to_ahead, to_next = lax.optimization_barrier((q2, to_chain, to_link, to_ahead, to_next))
    f_direct = lax.ppermute(to_next, both, direct)
    f_link = lax.ppermute(to_link, both, chain)
    f_chain = lax.ppermute(to_chain, both, chain)
    f_ahead = lax.ppermute(to_ahead, both, ahead)
    q1, own_a, away_a = call(
        first_kernel, [full] + pieces, [VM] * 3, [FIELD, PARTS, PUSH, FIELD, TABLE] + WORK, 8,
        [VM] + [ANY] * 4, 2 * unit,
    )(q2, wave, parts, f_swap, table)
    q1, f_around = lax.optimization_barrier((q1, f_around))
    f_relay = lax.ppermute(f_around, both, onward)
    back_a = lax.ppermute(away_a, both, swap)
    q0, own_b, away_b = call(
        second_kernel, [full] + pieces, [VM] * 3, [FIELD, PARTS, PUSH, FIELD, TABLE] + WORK, 12,
        [VM] + [ANY] * 6, 2 * unit,
    )(q1, parts, f_swap, f_link, f_next, f_direct, table)
    back_b = lax.ppermute(away_b, both, swap)
    d0, to_back = call(
        edge_kernel, [field, (2, PUSHED, N)], [VM, VM], [FIELD, PARTS, TABLE] + WORK, 16, [ANY] * 5, unit,
    )(q0, f_chain, f_ahead, f_relay, table)
    from_back = lax.ppermute(to_back, both, back)
    own_c, away_c, wave = call(
        third_kernel, pieces + [(8 * N, N)], [VM, VM, ANY],
        [FIELD, PUSH, FIELD, TABLE] + WORK, 12, [ANY, VM] + [ANY] * 4, unit,
    )(d0, q0, own_a, own_b, back_a, table)
    back_c = lax.ppermute(away_c, both, swap)
    own_d, away_d, wave = call(
        fourth_kernel, pieces + [(8 * N, N)], [VM, VM, ANY],
        [PARTS, PUSH, FIELD, TABLE] + WORK, 12, [VM] + [ANY] * 6, 2 * unit, {6: 2},
    )(d3, parts, f_swap, from_back, own_c, table, wave)
    back_d = lax.ppermute(away_d, both, swap)
    particles = [(8, PART), (8, PART)]
    wave, phase, energy = call(
        late_kernel, [(8 * N, N)] + particles, [ANY, VM, VM], [pltpu.VMEM((8, PUSHED, N), F32)], 16,
        [ANY] * 8, 1 << 20, {7: 0},
    )(own_a, own_b, own_c, own_d, back_a, back_b, back_c, wave)
    wave, phase, energy = call(
        final_kernel, [(8 * N, N)] + particles, [HB, VM, VM], [], 4, [VM, HB, VM, VM], 1 << 20, {1: 0},
    )(back_d, wave, phase, energy)
    return wave.reshape(8, 2, HALF, N), phase, energy


def solution(mesh):
    P = jax.sharding.PartitionSpec
    wide, flat = P("tm", None, "row", None), P("tm", "row")
    return jax.shard_map(body, mesh=mesh, in_specs=(wide,) + (flat,) * 5,
                         out_specs=(wide, flat, flat), check_vma=False)
```
